32 devices in a mesh: dp: 8 (over z, y), mp: 4 (over x, core).
Axes of the slice: x: 2, y: 2, z: 4, core: 2. Of those that a mesh axis runs over, the one named last changes fastest.
Arguments:
- hidden_in: bfloat16 [8192, 2048], P('dp', 'mp'), may hold values from -13 to 13
- cotangent: bfloat16 [8192, 2048], P('dp', 'mp'), may hold values from -6 to 6
- span_starts: int32 [32], P('dp'), may hold values from 0 to 1, as said below
- span_fill: int32 [32], P('dp'), may hold values from 128 to 256, as said below
- norm_gain: float32 [2048], replicated, may hold values from 0.5 to 1.5
- w_gate: bfloat16 [2048, 4096], P(None, 'mp'), may hold values from -0.125 to 0.125
- w_value: bfloat16 [2048, 4096], P(None, 'mp'), may hold values from -0.125 to 0.125
- w_select: bfloat16 [2048, 256], replicated, may hold values from -0.125 to 0.125
- w_step: bfloat16 [2048, 64], P(None, 'mp'), may hold values from -0.125 to 0.125
- conv_value: float32 [4, 4096], P(None, 'mp'), may hold values from -3 to 3
- conv_value_bias: float32 [4096], P('mp'), may hold values from -3 to 3
- conv_select: float32 [4, 256], replicated, may hold values from -3 to 3
- conv_select_bias: float32 [256], replicated, may hold values from -3 to 3
- step_bias: float32 [64], P('mp'), may hold values from -6 to -3
- decay_log: float32 [64], P('mp'), may hold values from 0 to 2.7
- skip_gain: float32 [64], P('mp'), may hold values from 0.5 to 1.5
- gate_gain: float32 [4096], P('mp'), may hold values from 0.5 to 1.5
- w_out: bfloat16 [4096, 2048], P('mp'), may hold values from -0.09375 to 0.09375
Outputs:
- output: bfloat16 [8192, 2048], P('dp', 'mp')
- grad_hidden_in: float32 [8192, 2048], P('dp', 'mp')
- grad_norm_gain: float32 [2048], P('mp')
- grad_w_gate: float32 [2048, 4096], P('dp', 'mp')
- grad_w_value: float32 [2048, 4096], P('dp', 'mp')
- grad_w_select: float32 [2048, 256], P('dp')
- grad_w_step: float32 [2048, 64], P('dp', 'mp')
- grad_conv_value: float32 [4, 4096], P(None, 'mp')
- grad_conv_value_bias: float32 [4096], P('mp')
- grad_conv_select: float32 [4, 256], replicated
- grad_conv_select_bias: float32 [256], replicated
- grad_step_bias: float32 [64], P('mp')
- grad_decay_log: float32 [64], P('mp')
- grad_skip_gain: float32 [64], P('mp')
- grad_gate_gain: float32 [4096], P('mp')
- grad_w_out: float32 [4096, 2048], P('mp', 'dp')
The draws below stay inside these ranges and needn't reach their ends.
Inputs may be any that keep to these rules, and one draw needn't show every extreme that they name: `span_starts`: the first of every device's 1024 / 256 spans has 1; a sequence runs from a span with 1 to the span before the next one or to its device's last span; on some device a single sequence fills every span. `span_fill`: 256 in every span but the last one of a sequence; the real tokens come first in a span.
All inputs are finite; a program needn't handle non-finite values.
Results may differ from the reference program's by a relative error of at most 0.00205.
The reference program's roundings to bfloat16 on the way count: a program that leaves them out, or rounds other values in their place, can miss the bound.
Values may be sent and summed in bfloat16 or wider, within the bound.
No kernel may reach another device: no remote copies, remote signals or barrier semaphores. Data moves between devices by JAX's collectives and lax.ppermute only.
A program may use at most 192 MiB of HBM per device.

```python
import jax
import jax.numpy as jnp
from jax import lax

D = 2048
HEADS = 64
HEAD_DIM = 64
STATE = 128
CONV = 4
SPAN = 256
TOK_DEV = 1024
INNER = 4096
TOKENS = 8192
N_DP = 8


def sequence_layout(key):
    devices = TOKENS // TOK_DEV
    per_device = TOK_DEV // SPAN
    key_starts, key_full, key_fill = jax.random.split(key, 3)
    dice_rolls = jax.random.randint(key_starts, (devices, per_device), 0, 100)
    starts = (dice_rolls < 35).astype(jnp.int32)
    full_device = jax.random.randint(key_full, (), 0, devices)
    device_ids = jnp.arange(devices)[:, None]
    span_ids = jnp.arange(per_device)[None, :]
    starts = jnp.where(device_ids == full_device, 0, starts)
    starts = jnp.where(span_ids == 0, 1, starts)
    following = jnp.concatenate([starts[:, 1:], jnp.ones((devices, 1), jnp.int32)], axis=1)
    fills = jax.random.randint(key_fill, (devices, per_device), SPAN // 2, SPAN + 1)
    fills = jnp.where(following == 1, fills, SPAN)
    fills = jnp.where(device_ids == full_device, SPAN, fills)
    return (starts.reshape(-1).astype(jnp.int32), fills.reshape(-1).astype(jnp.int32))


def draw_span_starts(key, part):
    return sequence_layout(jax.random.fold_in(key, 11))[0]


def draw_span_fill(key, part):
    return sequence_layout(jax.random.fold_in(key, 11))[1]


def draw_hidden_in(key, part):
    place = jnp.arange(D, dtype=jnp.float32) / (D - 1)
    noise_key = jax.random.fold_in(key, 23)
    base = jnp.clip(jax.random.normal(noise_key, (TOKENS, D), jnp.float32), -4.0, 4.0)
    column_scale = jnp.exp((place - 0.5) * 2.302585)
    return (base * column_scale[None, :]).astype(jnp.bfloat16)


def raised(entries, rng, source, target, blocks, factor):
    owner, partner = [(jnp.arange(entries.shape[position]) // (entries.shape[position] // blocks)).reshape([-1 if axis == position else 1 for axis in range(entries.ndim)]) for position in (source, target)]
    chosen = jax.random.permutation(rng, blocks)[partner]
    strong = (owner == chosen) | (owner == (partner + blocks // 2) % blocks)
    return jnp.where(strong, factor * entries, entries)


def block_levels(own_key, dims, cuts, smallest, largest):
    def one(axis_at, parts):
        steps = jax.random.uniform(jax.random.fold_in(jax.random.fold_in(own_key, 6), axis_at), (parts,), jnp.float32, smallest / len(cuts), largest / len(cuts))
        return jnp.repeat(jnp.exp(steps), dims[axis_at] // parts).reshape((-1,) + (1,) * (len(dims) - axis_at - 1))

    level = one(*cuts[0])
    for cut in cuts[1:]:
        level = level * one(*cut)
    return level


def gaussian(key, dims, spread, bound, pieces=(), held_as=jnp.bfloat16):
    values = spread * jax.random.normal(key, dims, jnp.float32)
    if pieces:
        values = values * block_levels(key, dims, pieces, -0.22, 0.18)
    return jnp.clip(values, -bound, bound).astype(held_as)


def heavy_noise(own_key, extent, spread, reach, cuts, heavy, held_as=jnp.bfloat16):
    values = spread * jax.random.normal(own_key, extent, jnp.float32)
    if cuts:
        values = values * block_levels(own_key, extent, cuts, -0.22, 0.18)
    return jnp.clip(raised(values, jax.random.fold_in(own_key, 3), *heavy), -reach, reach).astype(held_as)


def setup_inputs(seed: int = 0) -> dict:
    key_list = jax.random.split(jax.random.key(seed), 19)
    return {
        "hidden_in": draw_hidden_in(jax.random.fold_in(key_list[18], 71), 0),
        "cotangent": heavy_noise(key_list[1], (TOKENS, D), 1.0, 6.0, ((0, 8), (1, 4)), (0, 1, 8, 2.0)),
        "span_starts": draw_span_starts(jax.random.fold_in(key_list[18], 71), 0),
        "span_fill": draw_span_fill(jax.random.fold_in(key_list[18], 71), 0),
        "norm_gain": jnp.clip(1.0 + 0.1 * jax.random.normal(key_list[4], (D,), jnp.float32), 0.5, 1.5),
        "w_gate": gaussian(key_list[5], (D, INNER), D ** -0.5, 0.125, ((1, 4),)),
        "w_value": gaussian(key_list[6], (D, INNER), D ** -0.5, 0.125, ((1, 4),)),
        "w_select": gaussian(key_list[7], (D, 2 * STATE), D ** -0.5, 0.125),
        "w_step": gaussian(key_list[8], (D, HEADS), D ** -0.5, 0.125, ((1, 4),)),
        "conv_value": gaussian(key_list[9], (CONV, INNER), CONV ** -0.5, 3.0, ((1, 4),), jnp.float32),
        "conv_value_bias": gaussian(key_list[10], (INNER,), 0.5, 3.0, ((0, 4),), jnp.float32),
        "conv_select": gaussian(key_list[11], (CONV, 2 * STATE), CONV ** -0.5, 3.0, (), jnp.float32),
        "conv_select_bias": gaussian(key_list[12], (2 * STATE,), 0.5, 3.0, (), jnp.float32),
        "step_bias": jnp.clip(-6.0 + 3.0 * jax.random.uniform(key_list[13], (HEADS,), jnp.float32) ** block_levels(key_list[13], (HEADS,), ((0, 4),), -0.2, 0.2), -6.0, -3.0),
        "decay_log": jnp.clip(2.7 * jax.random.uniform(key_list[14], (HEADS,), jnp.float32) ** block_levels(key_list[14], (HEADS,), ((0, 4),), -0.2, 0.2), 0.0, 2.7),
        "skip_gain": jnp.clip(0.5 + 1.0 * jax.random.uniform(key_list[15], (HEADS,), jnp.float32) ** block_levels(key_list[15], (HEADS,), ((0, 4),), -0.2, 0.2), 0.5, 1.5),
        "gate_gain": jnp.clip(1.0 + 0.1 * jax.random.normal(key_list[16], (INNER,), jnp.float32), 0.5, 1.5),
        "w_out": gaussian(key_list[17], (INNER, D), INNER ** -0.5, 0.09375, ((0, 4),)),
    }


@jax.custom_vjp
def low(v):
    return lax.optimization_barrier(v.astype(jnp.bfloat16)).astype(jnp.float32)

@jax.custom_vjp
def low_back(v):
    return v

def low_keep(v):
    return (low(v), None)

def low_pass(kept, grad):
    return (grad,)

def back_keep(v):
    return (v, None)

def back_low(kept, grad):
    return (low(grad),)
low.defvjp(low_keep, low_pass)
low_back.defvjp(back_keep, back_low)
exact_mode = lax.Precision.HIGHEST
epsilon = 1e-05

def layout(start_flags, fill_counts, token_rows):
    places = jnp.arange(token_rows) % SPAN
    fill_tokens = jnp.repeat(fill_counts.astype(jnp.int32), SPAN, total_repeat_length=token_rows)
    live_mask = (places < fill_tokens).astype(jnp.float32)
    seq_numbers = jnp.repeat(jnp.cumsum(start_flags).astype(jnp.int32), SPAN, total_repeat_length=token_rows)
    same_links = []
    for back_steps in range(1, CONV):
        earlier = jnp.concatenate([jnp.full((back_steps,), -1, jnp.int32), seq_numbers[:-back_steps]])
        same_links.append((earlier == seq_numbers).astype(jnp.float32))
    keep_flags = (1 - start_flags).astype(jnp.float32)
    return (live_mask, same_links, keep_flags)

def conv_silu(pre_act, kernel, bias_vec, same_links):
    running_sum = bias_vec[None, :] + kernel[CONV - 1][None, :] * pre_act
    for back_steps in range(1, CONV):
        shifted = jnp.concatenate([jnp.zeros((back_steps, pre_act.shape[1]), jnp.float32), pre_act[:-back_steps]], axis=0)
        running_sum = running_sum + kernel[CONV - 1 - back_steps][None, :] * shifted * same_links[back_steps - 1][:, None]
    return jax.nn.silu(running_sum)

def scan_span(state, span_values, inflow, readout, step_sizes, decay_rates, skip_factor):
    length = span_values.shape[0]
    lower_mask = (jnp.arange(length)[:, None] >= jnp.arange(length)[None, :]).astype(jnp.float32)
    log_steps = (step_sizes * decay_rates[None, :]).T
    cumulative = jnp.dot(log_steps, lower_mask.T, precision=exact_mode)
    log_gaps = cumulative[:, :, None] - cumulative[:, None, :]
    weights = jnp.exp(jnp.where(lower_mask[None, :, :] > 0, log_gaps, 0.0)) * lower_mask[None, :, :]
    scores = jnp.dot(readout, inflow.T, precision=exact_mode)
    inputs = span_values * step_sizes[:, :, None]
    inner_part = jnp.einsum('hts,shp->thp', scores[None, :, :] * weights, inputs, precision=exact_mode)
    carried = jnp.einsum('tn,hpn->thp', readout, state, precision=exact_mode) * jnp.exp(cumulative).T[:, :, None]
    outputs = inner_part + carried + skip_factor[None, :, None] * span_values
    tail_decay = jnp.exp(cumulative[:, -1:] - cumulative)
    fresh_state = jnp.einsum('hs,shp,sn->hpn', tail_decay, inputs, inflow, precision=exact_mode)
    new_state = jnp.exp(cumulative[:, -1])[:, None, None] * state + fresh_state
    return (outputs, new_state)

def forward(params, block, live_mask, same_links, keep_flags):
    norm_gain, w_gate, w_value, w_select, w_step, conv_value, conv_value_bias, conv_select, conv_select_bias, step_bias, decay_log, skip_gain, gate_gain, w_out = params
    token_rows = block.shape[0]
    span_count = token_rows // SPAN
    input_scale = lax.rsqrt(lax.optimization_barrier(jnp.mean(block * block, axis=1, keepdims=True)) + epsilon)
    normed = low(block * input_scale * norm_gain[None, :])
    gate_pre = low_back(jnp.dot(normed, w_gate, precision=exact_mode))
    value_pre = low_back(jnp.dot(normed, w_value, precision=exact_mode))
    step_pre = low_back(jnp.dot(normed, w_step, precision=exact_mode))
    select_pre = low_back(jnp.dot(normed, w_select, precision=exact_mode))
    values = low(conv_silu(value_pre, conv_value, conv_value_bias, same_links))
    selects = low(conv_silu(select_pre, conv_select, conv_select_bias, same_links))
    step_sizes = jax.nn.softplus(step_pre + step_bias[None, :]) * live_mask[:, None]
    decay_rates = -jnp.exp(decay_log)
    value_blocks = values.reshape(span_count, SPAN, HEADS, HEAD_DIM)
    inflow = selects[:, :STATE].reshape(span_count, SPAN, STATE)
    readout = selects[:, STATE:].reshape(span_count, SPAN, STATE)
    step_blocks = step_sizes.reshape(span_count, SPAN, HEADS)
    stepper = jax.checkpoint(scan_span)

    def advance(state_carry, span_items):
        keep_flag, span_values, span_inflow, span_readout, span_steps = span_items
        entering = state_carry * keep_flag
        outputs, leaving = stepper(entering, span_values, span_inflow, span_readout, span_steps, decay_rates, skip_gain)
        return (leaving, outputs)
    start_state = jnp.zeros((HEADS, HEAD_DIM, STATE), jnp.float32)
    _, scanned = lax.scan(advance, start_state, (keep_flags, value_blocks, inflow, readout, step_blocks))
    scan_flat = scanned.reshape(token_rows, INNER)
    gated_rows = live_mask[:, None] * scan_flat * jax.nn.silu(gate_pre)
    gate_scale = lax.rsqrt(lax.optimization_barrier(jnp.mean(gated_rows * gated_rows, axis=1, keepdims=True)) + epsilon)
    scaled = low(gated_rows * gate_scale * gate_gain[None, :])
    mixed_rows = jnp.dot(scaled, w_out, precision=exact_mode)
    return block + mixed_rows

def reference(hidden_in, cotangent, span_starts, span_fill, norm_gain, w_gate, w_value, w_select, w_step, conv_value, conv_value_bias, conv_select, conv_select_bias, step_bias, decay_log, skip_gain, gate_gain, w_out):
    params = tuple((item.astype(jnp.float32) for item in (norm_gain, w_gate, w_value, w_select, w_step, conv_value, conv_value_bias, conv_select, conv_select_bias, step_bias, decay_log, skip_gain, gate_gain, w_out)))
    blocks = hidden_in.astype(jnp.float32).reshape(N_DP, TOK_DEV, D)
    upstream = cotangent.astype(jnp.float32).reshape(N_DP, TOK_DEV, D)
    start_rows = span_starts.reshape(N_DP, TOK_DEV // SPAN)
    fill_rows = span_fill.reshape(N_DP, TOK_DEV // SPAN)

    def one_block(totals, block_items):
        block, block_upstream, start_flags, fill_counts = block_items
        live_mask, same_links, keep_flags = layout(start_flags, fill_counts, TOK_DEV)

        def run_block(weights, inputs):
            return forward(weights, inputs, live_mask, same_links, keep_flags)
        result, pull_back = jax.vjp(run_block, params, block)
        grad_params, grad_block = pull_back(block_upstream)
        totals = jax.tree.map(lambda summed, addend: summed + addend, totals, grad_params)
        return (totals, (result.astype(jnp.bfloat16), grad_block))
    initial = jax.tree.map(jnp.zeros_like, params)
    totals, (outputs, grad_blocks) = lax.scan(one_block, initial, (blocks, upstream, start_rows, fill_rows))
    grad_norm_gain, grad_w_gate, grad_w_value, grad_w_select, grad_w_step, grad_conv_value, grad_conv_value_bias, grad_conv_select, grad_conv_select_bias, grad_step_bias, grad_decay_log, grad_skip_gain, grad_gate_gain, grad_w_out = totals
    return (outputs.reshape(TOKENS, D), grad_blocks.reshape(TOKENS, D), grad_norm_gain, grad_w_gate, grad_w_value, grad_w_select, grad_w_step, grad_conv_value, grad_conv_value_bias, grad_conv_select, grad_conv_select_bias, grad_step_bias, grad_decay_log, grad_skip_gain, grad_gate_gain, grad_w_out)
```

```python
import functools

import jax
import jax.numpy as jnp
from jax import lax
from jax.experimental import pallas as pl
from jax.experimental.pallas import tpu as pltpu
from jax.sharding import PartitionSpec as P

CONV = 4
SPAN = 256
LANES = 128
EXTRA = 8
TOP = 15.0
FAR = -1e30
epsilon = 1e-05
exact_mode = lax.Precision.HIGHEST


def settings(mebibytes, axes=1):
    return pltpu.CompilerParams(
        dimension_semantics=("arbitrary",) * axes, vmem_limit_bytes=mebibytes << 20
    )


def scalars():
    return pl.BlockSpec(memory_space=pltpu.SMEM)


def fixed(shape):
    return pl.BlockSpec(shape, lambda *_: (0,) * len(shape))


def split_bits(value):
    high = value.astype(jnp.bfloat16)
    low = (value - high.astype(jnp.float32)).astype(jnp.bfloat16)
    return high, low


def dot(left, right):
    return lax.dot_general(left, right, (((1,), (0,)), ((), ())), preferred_element_type=jnp.float32)


def dot_lanes(left, right):
    return lax.dot_general(left, right, (((1,), (1,)), ((), ())), preferred_element_type=jnp.float32)


def dot_rows(left, right):
    return lax.dot_general(left, right, (((0,), (0,)), ((), ())), preferred_element_type=jnp.float32)


def exact(left, right):
    return jnp.dot(left, right, precision=exact_mode, preferred_element_type=jnp.float32)


def beside(*pieces):
    return jnp.concatenate(pieces, axis=1)


def above(*pieces):
    return jnp.concatenate(pieces, axis=0)


def sigmoid(value):
    return 1.0 / (1.0 + jnp.exp(-value))


def iota(shape, axis):
    return lax.broadcasted_iota(jnp.int32, shape, axis)


def two_heads(columns, pair, in_first):
    first = columns[:, 2 * pair : 2 * pair + 1]
    second = columns[:, 2 * pair + 1 : 2 * pair + 2]
    return jnp.where(in_first, first, second)


def row_of(columns):
    return jnp.sum(jnp.transpose(columns), axis=0, keepdims=True)


def live_rows(fill, width):
    return (iota((SPAN, width), 0) < fill).astype(jnp.float32)


def norm_kernel(side, hidden, gain, normed_out, split_out, scale_out, *, piece):
    block = hidden[...].astype(jnp.float32)
    scale = lax.rsqrt(jnp.mean(block * block, axis=1, keepdims=True) + epsilon)
    normed = (block * scale * gain[...]).astype(jnp.bfloat16)
    normed_out[...] = normed
    scale_out[...] = jnp.broadcast_to(scale, scale_out.shape)
    store_split(side, normed, split_out, piece)


def store_split(side, block, split_out, piece):
    for index in range(block.shape[1] // piece):
        slot = jnp.where(side[0] == index % 2, 1, 0)
        start = index // 2 * piece
        split_out[pl.ds(slot, 1), :, start : start + piece] = block[
            None, :, index * piece : (index + 1) * piece
        ]


def split_kernel(side, block, split_out, *, piece):
    store_split(side, block[...], split_out, piece)


def normalize(hidden, gain, side, piece):
    rows, width = hidden.shape
    return pl.pallas_call(
        functools.partial(norm_kernel, piece=piece),
        grid=(rows // SPAN,),
        in_specs=[
            scalars(),
            pl.BlockSpec((SPAN, width), lambda i: (i, 0)),
            fixed((1, width)),
        ],
        out_specs=[
            pl.BlockSpec((SPAN, width), lambda i: (i, 0)),
            pl.BlockSpec((2, SPAN, width // 2), lambda i: (0, i, 0)),
            pl.BlockSpec((SPAN, LANES), lambda i: (i, 0)),
        ],
        out_shape=[
            jax.ShapeDtypeStruct((rows, width), jnp.bfloat16),
            jax.ShapeDtypeStruct((2, rows, width // 2), jnp.bfloat16),
            jax.ShapeDtypeStruct((rows, LANES), jnp.float32),
        ],
        compiler_params=settings(32),
        name="norm",
    )(side, hidden, gain)


def split_columns(array, side, piece):
    rows, width = array.shape
    return pl.pallas_call(
        functools.partial(split_kernel, piece=piece),
        grid=(rows // SPAN,),
        in_specs=[scalars(), pl.BlockSpec((SPAN, width), lambda i: (i, 0))],
        out_specs=pl.BlockSpec((2, SPAN, width // 2), lambda i: (0, i, 0)),
        out_shape=jax.ShapeDtypeStruct((2, rows, width // 2), array.dtype),
        compiler_params=settings(32),
        name="split",
    )(side, array)


def conv_of(extended, kernel, bias, lanes):
    total = bias[:, lanes]
    for back in range(CONV):
        tap = kernel[CONV - 1 - back : CONV - back, lanes]
        total = total + tap * extended[EXTRA - back : EXTRA - back + SPAN, lanes]
    return total


def forward_kernel(
    starts,
    fills,
    value_pre,
    gate_pre,
    grad_scaled,
    select_pre,
    step_pre,
    conv_value,
    conv_value_bias,
    conv_select,
    conv_select_bias,
    step_bias,
    decay_log,
    skip,
    gain,
    values_out,
    selects_out,
    scan_out,
    delta_out,
    sum_out,
    state_out,
    rows_out,
    extended,
    extended_select,
    state,
):
    step = pl.program_id(0)
    fresh = starts[step] == 1
    width = value_pre.shape[1]
    state_dim = select_pre.shape[1] // 2

    @pl.when(fresh)
    def _():
        extended[:EXTRA, :] = jnp.zeros((EXTRA, width), jnp.float32)
        extended_select[:EXTRA, :] = jnp.zeros((EXTRA, 2 * state_dim), jnp.float32)
        state[...] = jnp.zeros(state.shape, jnp.float32)

    @pl.when(jnp.logical_not(fresh))
    def _():
        extended[:EXTRA, :] = extended[SPAN:, :]
        extended_select[:EXTRA, :] = extended_select[SPAN:, :]

    extended[EXTRA:, :] = value_pre[...]
    extended_select[EXTRA:, :] = select_pre[...]
    state_out[0] = state[...]

    live = live_rows(fills[step], LANES)
    pre_step = step_pre[...] + step_bias[...]
    delta = live * (jnp.maximum(pre_step, 0.0) + jnp.log1p(jnp.exp(-jnp.abs(pre_step))))
    rate = -jnp.exp(decay_log[...])
    lower = (iota((SPAN, SPAN), 0) >= iota((SPAN, SPAN), 1)).astype(jnp.float32)
    cumulative = exact(lower, delta * rate)
    delta_out[...] = delta
    sum_out[...] = cumulative
    sums_across = jnp.transpose(cumulative)
    delta_across = jnp.transpose(delta)
    grown = jnp.exp(cumulative)
    tail = delta * jnp.exp(cumulative[SPAN - 1 : SPAN, :] - cumulative)

    halves = []
    for half in range(2):
        lanes = slice(half * state_dim, (half + 1) * state_dim)
        mixed = conv_of(extended_select, conv_select, conv_select_bias, lanes)
        chosen = (mixed * sigmoid(mixed)).astype(jnp.bfloat16)
        selects_out[:, lanes] = chosen
        halves.append(chosen)
    inflow, readout = halves
    inflow_across = jnp.transpose(inflow.astype(jnp.float32)).astype(jnp.bfloat16)
    scores = dot_lanes(readout, inflow)
    past = iota((SPAN, SPAN), 0) >= iota((SPAN, SPAN), 1)
    in_first = iota((SPAN, LANES), 1) < LANES // 2
    row_first = iota((1, LANES), 1) < LANES // 2
    readout_twice = beside(readout, readout)
    squares = jnp.zeros((SPAN, LANES), jnp.float32)
    products = jnp.zeros((SPAN, LANES), jnp.float32)
    for pair in range(width // LANES):
        lanes = slice(pair * LANES, (pair + 1) * LANES)
        mixed = conv_of(extended, conv_value, conv_value_bias, lanes)
        value_low = (mixed * sigmoid(mixed)).astype(jnp.bfloat16)
        values_out[:, lanes] = value_low
        value = value_low.astype(jnp.float32)
        entering = state[:, lanes]
        scan = dot(readout_twice, above(*split_bits(entering))) * two_heads(grown, pair, in_first)
        scan = scan + skip[:, lanes] * value
        for which in range(2):
            head = 2 * pair + which
            gaps = cumulative[:, head : head + 1] - sums_across[head : head + 1, :]
            weights = jnp.exp(jnp.where(past, gaps, FAR))
            mixing = scores * weights * delta_across[head : head + 1, :]
            own = jnp.where(in_first == (which == 0), value_low, jnp.zeros_like(value_low))
            high, low = split_bits(mixing)
            scan = scan + dot(high, own) + dot(low, own)
        scan_out[:, lanes] = scan
        gate = gate_pre[:, lanes]
        gated = live * scan * gate * sigmoid(gate)
        squares = squares + gated * gated
        products = products + grad_scaled[:, lanes] * gain[:, lanes] * gated
        weighted = value * two_heads(tail, pair, in_first)
        high, low = split_bits(weighted)
        last = two_heads(grown[SPAN - 1 : SPAN, :], pair, row_first)
        state[:, lanes] = entering * last + dot(inflow_across, high) + dot(inflow_across, low)
    rows_out[...] = above(row_of(squares), row_of(products), jnp.zeros((6, SPAN), jnp.float32))


def run_forward(starts, fills, tiles, vectors):
    value_pre, gate_pre, grad_scaled, select_pre, step_pre = tiles
    rows, width = value_pre.shape
    spans = rows // SPAN
    select_width = select_pre.shape[1]

    def tile(columns):
        return pl.BlockSpec((SPAN, columns), lambda i: (i, 0))

    def like(columns, dtype):
        return jax.ShapeDtypeStruct((rows, columns), dtype)

    return pl.pallas_call(
        forward_kernel,
        grid=(spans,),
        in_specs=[scalars(), scalars()]
        + [tile(array.shape[1]) for array in tiles]
        + [fixed(array.shape) for array in vectors],
        out_specs=[
            tile(width),
            tile(select_width),
            tile(width),
            tile(LANES),
            tile(LANES),
            pl.BlockSpec((1, select_width // 2, width), lambda i: (i, 0, 0)),
            pl.BlockSpec((8, SPAN), lambda i: (0, i)),
        ],
        out_shape=[
            like(width, jnp.bfloat16),
            like(select_width, jnp.bfloat16),
            like(width, jnp.float32),
            like(LANES, jnp.float32),
            like(LANES, jnp.float32),
            jax.ShapeDtypeStruct((spans, select_width // 2, width), jnp.float32),
            jax.ShapeDtypeStruct((8, rows), jnp.float32),
        ],
        scratch_shapes=[
            pltpu.VMEM((SPAN + EXTRA, width), jnp.float32),
            pltpu.VMEM((SPAN + EXTRA, select_width), jnp.float32),
            pltpu.VMEM((select_width // 2, width), jnp.float32),
        ],
        compiler_params=settings(48),
        name="forward",
    )(starts, fills, *tiles, *vectors)


def gate_kernel(
    fills,
    gate_pre,
    scan_in,
    grad_scaled,
    sums,
    gain,
    scaled_out,
    gate_out,
    scan_out,
    rows_out,
    stat_out,
    *,
    total_width,
):
    step = pl.program_id(0)
    width = gate_pre.shape[1]
    live = live_rows(fills[step], LANES)
    turned = jnp.transpose(above(sums[...], jnp.zeros((LANES - 8, SPAN), jnp.float32)))
    scale = lax.rsqrt(turned[:, 0:1] / total_width + epsilon)
    pull = scale * scale * scale * turned[:, 1:2] / total_width
    scale = jnp.broadcast_to(scale, (SPAN, LANES))
    pull = jnp.broadcast_to(pull, (SPAN, LANES))

    @pl.when(step == 0)
    def _():
        stat_out[...] = jnp.zeros(stat_out.shape, jnp.float32)

    dots = jnp.zeros((SPAN, LANES), jnp.float32)
    for pair in range(width // LANES):
        lanes = slice(pair * LANES, (pair + 1) * LANES)
        gate = gate_pre[:, lanes]
        scan = scan_in[:, lanes]
        upstream = grad_scaled[:, lanes]
        sig = sigmoid(gate)
        opened = live * gate * sig
        gated = scan * opened
        own_gain = gain[:, lanes]
        shrunk = gated * scale
        scaled_out[:, lanes] = (shrunk * own_gain).astype(jnp.bfloat16)
        grad_gated = upstream * own_gain * scale - gated * pull
        scan_out[:, lanes] = grad_gated * opened
        grad_gate = (grad_gated * live * scan * sig * (1.0 + gate * (1.0 - sig))).astype(jnp.bfloat16)
        gate_out[:, lanes] = grad_gate
        wide = grad_gate.astype(jnp.float32)
        dots = dots + wide * gate
        stat_out[0:1, lanes] += jnp.sum(upstream * shrunk, axis=0, keepdims=True)
        stat_out[1:2, lanes] = jnp.maximum(
            stat_out[1:2, lanes], jnp.max(jnp.abs(wide), axis=0, keepdims=True)
        )
    rows_out[...] = above(row_of(dots), jnp.zeros((7, SPAN), jnp.float32))


def run_gate(fills, gate_pre, scan, grad_scaled, sums, gain, total_width):
    rows, width = gate_pre.shape
    tile = pl.BlockSpec((SPAN, width), lambda i: (i, 0))
    strip = pl.BlockSpec((8, SPAN), lambda i: (0, i))
    return pl.pallas_call(
        functools.partial(gate_kernel, total_width=total_width),
        grid=(rows // SPAN,),
        in_specs=[scalars(), tile, tile, tile, strip, fixed((1, width))],
        out_specs=[tile, tile, tile, strip, fixed((8, width))],
        out_shape=[
            jax.ShapeDtypeStruct((rows, width), jnp.bfloat16),
            jax.ShapeDtypeStruct((rows, width), jnp.bfloat16),
            jax.ShapeDtypeStruct((rows, width), jnp.float32),
            jax.ShapeDtypeStruct((8, rows), jnp.float32),
            jax.ShapeDtypeStruct((8, width), jnp.float32),
        ],
        compiler_params=settings(40),
        name="gate",
    )(fills, gate_pre, scan, grad_scaled, sums, gain)


def backward_kernel(
    starts,
    fills,
    grad_scan,
    scan_in,
    values_in,
    value_pre,
    value_before,
    selects_in,
    delta_in,
    sum_in,
    step_pre,
    state_in,
    conv_value,
    conv_value_bias,
    step_bias,
    decay_log,
    skip,
    value_out,
    select_out,
    step_out,
    rows_out,
    stat_out,
    small_out,
    extended,
    shifted,
    state,
    carried,
    *,
    spans,
):
    step = pl.program_id(0)
    span = spans - 1 - step
    width = values_in.shape[1]
    state_dim = selects_in.shape[1] // 2
    following = jnp.minimum(span + 1, spans - 1)
    joined = jnp.logical_and(step > 0, starts[following] == 0)

    @pl.when(jnp.logical_not(joined))
    def _():
        shifted[SPAN:, :] = jnp.zeros((EXTRA, width), jnp.float32)
        state[...] = jnp.zeros(state.shape, jnp.float32)
        carried[...] = jnp.zeros(carried.shape, jnp.float32)

    @pl.when(joined)
    def _():
        shifted[SPAN:, :] = shifted[:EXTRA, :]

    @pl.when(step == 0)
    def _():
        stat_out[...] = jnp.zeros(stat_out.shape, jnp.float32)
        small_out[...] = jnp.zeros(small_out.shape, jnp.float32)

    fresh = starts[span] == 1

    @pl.when(fresh)
    def _():
        extended[:EXTRA, :] = jnp.zeros((EXTRA, width), jnp.float32)

    @pl.when(jnp.logical_not(fresh))
    def _():
        extended[:EXTRA, :] = value_before[...]

    extended[EXTRA:, :] = value_pre[...]

    delta = delta_in[...]
    cumulative = sum_in[...]
    sums_across = jnp.transpose(cumulative)
    grown = jnp.exp(cumulative)
    tail = jnp.exp(cumulative[SPAN - 1 : SPAN, :] - cumulative)
    delta_tail = delta * tail
    inflow = selects_in[:, :state_dim]
    readout = selects_in[:, state_dim:]
    readout_across = jnp.transpose(readout.astype(jnp.float32)).astype(jnp.bfloat16)
    scores = dot_lanes(inflow, readout)
    ahead = iota((SPAN, SPAN), 1) >= iota((SPAN, SPAN), 0)
    in_first = iota((SPAN, LANES), 1) < LANES // 2
    row_first = iota((1, LANES), 1) < LANES // 2
    inflow_twice = beside(inflow, inflow)
    grad_scores = jnp.zeros((SPAN, SPAN), jnp.float32)
    grad_inflow = jnp.zeros((SPAN, state_dim), jnp.float32)
    grad_readout = jnp.zeros((SPAN, state_dim), jnp.float32)
    change = jnp.zeros((SPAN, LANES), jnp.float32)
    direct = jnp.zeros((SPAN, LANES), jnp.float32)
    jump = jnp.zeros((8, LANES), jnp.float32)
    dots = jnp.zeros((SPAN, LANES), jnp.float32)
    for pair in range(width // LANES):
        lanes = slice(pair * LANES, (pair + 1) * LANES)
        upstream = grad_scan[:, lanes]
        up_high, up_low = split_bits(upstream)
        value_low = values_in[:, lanes]
        value = value_low.astype(jnp.float32)
        own_skip = skip[:, lanes]
        arriving = state[:, lanes]
        arriving_high, arriving_low = split_bits(arriving)
        entering = state_in[0, :, lanes]
        entering_high, entering_low = split_bits(entering)
        pulled = dot(inflow_twice, above(arriving_high, arriving_low)) * two_heads(tail, pair, in_first)
        up_both = beside(up_high, up_low)
        for which in range(2):
            head = 2 * pair + which
            mine = in_first == (which == 0)
            nothing = jnp.zeros_like(value_low)
            gaps = sums_across[head : head + 1, :] - cumulative[:, head : head + 1]
            weights = jnp.exp(jnp.where(ahead, gaps, FAR))
            high, low = split_bits(scores * weights)
            own_high = jnp.where(mine, up_high, nothing)
            own_low = jnp.where(mine, up_low, nothing)
            pulled = pulled + dot(high, own_high) + dot(high, own_low) + dot(low, own_high)
            own_value = jnp.where(mine, value_low, nothing)
            outer = dot_lanes(beside(own_value, own_value), up_both)
            grad_scores = grad_scores + outer * weights * delta[:, head : head + 1]
        delta_both = two_heads(delta, pair, in_first)
        grad_value = own_skip * upstream + delta_both * pulled
        pull_value = value * pulled
        spread = (
            iota((LANES, LANES), 1) == 2 * pair + iota((LANES, LANES), 0) // (LANES // 2)
        ).astype(jnp.bfloat16)
        spread_twice = above(spread, spread)
        moved = upstream * (scan_in[:, lanes] - own_skip * value) - delta_both * pull_value
        change = change + dot(beside(*split_bits(moved)), spread_twice)
        direct = direct + dot(beside(*split_bits(pull_value)), spread_twice)
        grown_up = upstream * two_heads(grown, pair, in_first)
        high, low = split_bits(grown_up)
        grad_readout = grad_readout + dot_lanes(
            beside(high, low, high), beside(entering_high, entering_high, entering_low)
        )
        last = two_heads(grown[SPAN - 1 : SPAN, :], pair, row_first)
        leaving = arriving * last + dot(readout_across, high) + dot(readout_across, low)
        tail_value = value * two_heads(delta_tail, pair, in_first)
        high, low = split_bits(tail_value)
        grad_inflow = grad_inflow + dot_lanes(
            beside(high, low, high), beside(arriving_high, arriving_high, arriving_low)
        )
        jump = jump + exact(carried[:, lanes], spread.astype(jnp.float32))
        state[:, lanes] = leaving
        carried[:, lanes] = jnp.broadcast_to(
            jnp.sum(leaving * entering, axis=0, keepdims=True), (8, LANES)
        )
        mixed = conv_of(extended, conv_value, conv_value_bias, lanes)
        sig = sigmoid(mixed)
        inner = grad_value * sig * (1.0 + mixed * (1.0 - sig))
        shifted[:SPAN, lanes] = inner
        grad_pre = jnp.zeros((SPAN, LANES), jnp.float32)
        for back in range(CONV):
            tap = conv_value[CONV - 1 - back : CONV - back, lanes]
            grad_pre = grad_pre + tap * shifted[back : back + SPAN, lanes]
            stat_out[CONV - 1 - back : CONV - back, lanes] += jnp.sum(
                inner * extended[EXTRA - back : EXTRA - back + SPAN, lanes], axis=0, keepdims=True
            )
        stat_out[CONV : CONV + 1, lanes] += jnp.sum(inner, axis=0, keepdims=True)
        stat_out[CONV + 1 : CONV + 2, lanes] += jnp.sum(value * upstream, axis=0, keepdims=True)
        grad_low = grad_pre.astype(jnp.bfloat16)
        value_out[:, lanes] = grad_low
        wide = grad_low.astype(jnp.float32)
        dots = dots + wide * extended[EXTRA:, lanes]
        stat_out[CONV + 2 : CONV + 3, lanes] = jnp.maximum(
            stat_out[CONV + 2 : CONV + 3, lanes], jnp.max(jnp.abs(wide), axis=0, keepdims=True)
        )
    high, low = split_bits(grad_scores)
    grad_inflow = grad_inflow + dot(high, readout) + dot(low, readout)
    high, low = split_bits(jnp.transpose(grad_scores))
    grad_readout = grad_readout + dot(high, inflow) + dot(low, inflow)
    part = select_out.shape[2]
    both = (grad_inflow, grad_readout)
    for index in range(select_out.shape[0]):
        start = index * part
        source = both[start // state_dim]
        select_out[index] = source[:, start % state_dim : start % state_dim + part]
    upper = (iota((SPAN, SPAN), 1) >= iota((SPAN, SPAN), 0)).astype(jnp.float32)
    flow = exact(upper, change) + jump[0:1, :]
    rate = -jnp.exp(decay_log[...])
    grad_delta = direct + rate * flow
    live = live_rows(fills[span], LANES)
    pre_step = step_pre[...]
    grad_step = grad_delta * live * sigmoid(pre_step + step_bias[...])
    grad_step = jnp.where(iota((SPAN, LANES), 1) < width // (LANES // 2), grad_step, 0.0)
    step_low = grad_step.astype(jnp.bfloat16)
    step_out[...] = step_low
    wide = step_low.astype(jnp.float32)
    dots = dots + wide * pre_step
    small_out[0:1, :] += jnp.sum(grad_step, axis=0, keepdims=True)
    small_out[1:2, :] += rate * jnp.sum(delta * flow, axis=0, keepdims=True)
    small_out[2:3, :] = jnp.maximum(small_out[2:3, :], jnp.max(jnp.abs(wide), axis=0, keepdims=True))
    rows_out[...] = above(row_of(dots), jnp.zeros((7, SPAN), jnp.float32))


def run_backward(starts, fills, tiles, states, vectors, parts):
    grad_scan, scan, values, value_pre, selects, delta, sums, step_pre = tiles
    rows, width = value_pre.shape
    spans = rows // SPAN
    select_width = selects.shape[1]

    def tile(columns):
        return pl.BlockSpec((SPAN, columns), lambda i: (spans - 1 - i, 0))

    before = pl.BlockSpec(
        (EXTRA, width), lambda i: (jnp.maximum((spans - 1 - i) * (SPAN // EXTRA) - 1, 0), 0)
    )
    return pl.pallas_call(
        functools.partial(backward_kernel, spans=spans),
        grid=(spans,),
        in_specs=[
            scalars(),
            scalars(),
            tile(width),
            tile(width),
            tile(width),
            tile(width),
            before,
            tile(select_width),
            tile(LANES),
            tile(LANES),
            tile(LANES),
            pl.BlockSpec((1, select_width // 2, width), lambda i: (spans - 1 - i, 0, 0)),
        ]
        + [fixed(array.shape) for array in vectors],
        out_specs=[
            tile(width),
            pl.BlockSpec((parts, SPAN, select_width // parts), lambda i: (0, spans - 1 - i, 0)),
            tile(LANES),
            pl.BlockSpec((8, SPAN), lambda i: (0, spans - 1 - i)),
            fixed((8, width)),
            fixed((8, LANES)),
        ],
        out_shape=[
            jax.ShapeDtypeStruct((rows, width), jnp.bfloat16),
            jax.ShapeDtypeStruct((parts, rows, select_width // parts), jnp.float32),
            jax.ShapeDtypeStruct((rows, LANES), jnp.bfloat16),
            jax.ShapeDtypeStruct((8, rows), jnp.float32),
            jax.ShapeDtypeStruct((8, width), jnp.float32),
            jax.ShapeDtypeStruct((8, LANES), jnp.float32),
        ],
        scratch_shapes=[
            pltpu.VMEM((SPAN + EXTRA, width), jnp.float32),
            pltpu.VMEM((SPAN + EXTRA, width), jnp.float32),
            pltpu.VMEM((select_width // 2, width), jnp.float32),
            pltpu.VMEM((8, width), jnp.float32),
        ],
        compiler_params=settings(52),
        name="backward",
    )(
        starts,
        fills,
        grad_scan,
        scan,
        values,
        value_pre,
        value_pre,
        selects,
        delta,
        sums,
        step_pre,
        states,
        *vectors,
    )


def exponent_of(bound):
    return jnp.ceil(jnp.log2(jnp.maximum(bound, 1e-30)) + 0.01)


def narrow(values, exponent):
    low = (values * jnp.exp2(TOP - exponent)).astype(jnp.float16)
    mark = jnp.broadcast_to(exponent.astype(jnp.float16), (EXTRA, low.shape[1]))
    return jnp.concatenate([low, mark], axis=0)


def mark_of(packet):
    return packet[-1, 0].astype(jnp.float32)


def pair_of(size):
    return [(spot, spot ^ 1) for spot in range(size)]


def shift_of(size, hops):
    groups = size // 2
    return [(spot, ((spot // 2 + hops) % groups) * 2 + spot % 2) for spot in range(size)]


def reduce_tokens(split, gradient, bound):
    size = lax.axis_size("dp")
    groups = size // 2
    piece = split.shape[2] // groups
    mine = lax.axis_index("dp") // 2
    exponent = exponent_of(bound)
    came = lax.ppermute(
        narrow(contract_rows(split[0], gradient), exponent), "dp", pair_of(size)
    )
    ours = contract_rows(split[1], gradient)
    other = mark_of(came)
    widening = jnp.exp2(other - TOP)
    exponent = jnp.maximum(exponent, other) + 1.0

    def both(place):
        start = place * piece
        added = lax.dynamic_slice_in_dim(came, start, piece, 0).astype(jnp.float32) * widening
        return lax.dynamic_slice_in_dim(ours, start, piece, 0) + added

    total = both(mine)
    arrived = [
        lax.ppermute(narrow(both((mine + hops) % groups), exponent), "dp", shift_of(size, hops))
        for hops in range(1, groups)
    ]
    for packet in arrived:
        total = total + packet[:piece].astype(jnp.float32) * jnp.exp2(mark_of(packet) - TOP)
    return total


def pick(stacked, place):
    return lax.dynamic_index_in_dim(stacked, place, 0, keepdims=False)


def scatter_plain(theirs, ours, axis, wire):
    size = lax.axis_size(axis)
    groups = size // 2
    mine = lax.axis_index(axis) // 2
    came = lax.ppermute(theirs, axis, pair_of(size))
    total = pick(ours, mine) + pick(came, mine)
    arrived = []
    for hops in range(1, groups):
        place = (mine + hops) % groups
        piece = (pick(ours, place) + pick(came, place)).astype(wire)
        arrived.append(lax.ppermute(piece, axis, shift_of(size, hops)))
    for piece in arrived:
        total = total + piece.astype(jnp.float32)
    return total


def features_kernel(place, gate, value, small, w_gate, w_value, w_small, out):
    total = dot_lanes(gate[...], w_gate[...])
    total = total + dot_lanes(value[...], w_value[...])
    out[0] = total + dot_lanes(small[...], w_small[...])


def back_features(place, gradients, weights, groups):
    rows = gradients[0].shape[0]
    features = weights[0].shape[0]
    piece = features // (2 * groups)
    return pl.pallas_call(
        features_kernel,
        grid_spec=pltpu.PrefetchScalarGridSpec(
            num_scalar_prefetch=1,
            grid=(groups, rows // 512),
            in_specs=[pl.BlockSpec((512, array.shape[1]), lambda g, t, at: (t, 0)) for array in gradients]
            + [
                pl.BlockSpec((piece, array.shape[1]), lambda g, t, at: (2 * g + at[0], 0))
                for array in weights
            ],
            out_specs=pl.BlockSpec((1, 512, piece), lambda g, t, at: (g, t, 0)),
        ),
        out_shape=jax.ShapeDtypeStruct((groups, rows, piece), jnp.float32),
        compiler_params=settings(40, 2),
        name="features",
    )(place, *gradients, *weights)


def sum_all(values, axis):
    size = lax.axis_size(axis)
    step = 1
    while step < size:
        values = values + lax.ppermute(values, axis, [(spot, spot ^ step) for spot in range(size)])
        step *= 2
    return values


def pack(arrays):
    flat = jnp.concatenate([array.reshape(-1) for array in arrays])
    length = flat.shape[0]
    whole = -(-length // 1024) * 1024
    return jnp.pad(flat, (0, whole - length)).reshape(whole // LANES, LANES)


def unpack(packed, likes):
    flat = packed.reshape(-1)
    out, start = [], 0
    for like in likes:
        count = like.size
        out.append(flat[start : start + count].reshape(like.shape))
        start += count
    return out


def layout(start_flags, token_rows):
    seq_numbers = jnp.repeat(jnp.cumsum(start_flags), SPAN, total_repeat_length=token_rows)
    same_links = []
    for back_steps in range(1, CONV):
        earlier = jnp.concatenate(
            [jnp.full((back_steps,), -1, jnp.int32), seq_numbers[:-back_steps]]
        )
        same_links.append((earlier == seq_numbers).astype(jnp.float32))
    return same_links


def conv_silu(pre_act, kernel, bias_vec, same_links):
    running_sum = bias_vec[None, :] + kernel[CONV - 1][None, :] * pre_act
    for back_steps in range(1, CONV):
        shifted = jnp.concatenate(
            [jnp.zeros((back_steps, pre_act.shape[1]), jnp.float32), pre_act[:-back_steps]], axis=0
        )
        running_sum = (
            running_sum
            + kernel[CONV - 1 - back_steps][None, :] * shifted * same_links[back_steps - 1][:, None]
        )
    return jax.nn.silu(running_sum)


def contract_rows(left_arr, right_arr):
    return lax.dot_general(
        left_arr, right_arr, (((0,), (0,)), ((), ())), preferred_element_type=jnp.float32
    )


def contract_cols(left_arr, right_arr):
    return lax.dot_general(
        left_arr, right_arr, (((1,), (1,)), ((), ())), preferred_element_type=jnp.float32
    )


def widen_lanes(vector):
    return jnp.pad(vector, (0, LANES - vector.shape[0]))[None, :]


def on_device(
    hidden_in,
    cotangent,
    span_starts,
    span_fill,
    norm_gain,
    w_gate,
    w_value,
    w_select,
    w_step,
    conv_value,
    conv_value_bias,
    conv_select,
    conv_select_bias,
    step_bias,
    decay_log,
    skip_gain,
    gate_gain,
    w_out,
):
    token_rows = hidden_in.shape[0]
    model_width = norm_gain.shape[0]
    inner_cols = w_gate.shape[1]
    local_heads = w_step.shape[1]
    head_dim = inner_cols // local_heads
    select_width = w_select.shape[1]
    model_parts = lax.axis_size("mp")
    model_groups = model_parts // 2
    data_parts = lax.axis_size("dp")
    inner_total = inner_cols * model_parts
    feature_piece = model_width // model_parts
    data_piece = model_width // data_parts
    part = select_width // model_parts
    model_spot = lax.axis_index("mp")
    model_side = model_spot % 2
    data_side = (lax.axis_index("dp") % 2).reshape(1)
    offset = model_spot * feature_piece
    select_start = model_spot * part

    gain_row = gate_gain[None, :]
    skip_row = jnp.repeat(skip_gain, head_dim, total_repeat_length=inner_cols)[None, :]
    bias_step = widen_lanes(step_bias)
    decay_row = widen_lanes(decay_log)
    wide_step = jnp.pad(w_step, ((0, 0), (0, LANES - local_heads)))
    own_select = lax.dynamic_slice_in_dim(w_select, select_start, part, 1)
    w_small = jnp.concatenate(
        [w_step, own_select, jnp.zeros((model_width, -(local_heads + part) % LANES), jnp.bfloat16)],
        axis=1,
    )

    whole_in = lax.all_gather(hidden_in, "mp", axis=1, tiled=True)
    whole_upstream = lax.all_gather(cotangent, "mp", axis=1, tiled=True)
    normed, normed_split, input_scale = normalize(whole_in, norm_gain[None, :], data_side, data_piece)
    gate_pre = jnp.dot(normed, w_gate, preferred_element_type=jnp.float32)
    value_pre = jnp.dot(normed, w_value, preferred_element_type=jnp.float32)
    step_pre = jnp.dot(normed, wide_step, preferred_element_type=jnp.float32)
    select_pre = jnp.dot(normed, w_select, preferred_element_type=jnp.float32)
    grad_scaled = contract_cols(whole_upstream, w_out)
    upstream_split = split_columns(whole_upstream, data_side, data_piece)

    values, selects, scan, delta, sums, states, row_part = run_forward(
        span_starts,
        span_fill,
        (value_pre, gate_pre, grad_scaled, select_pre, step_pre),
        (
            conv_value,
            conv_value_bias[None, :],
            conv_select,
            conv_select_bias[None, :],
            bias_step,
            decay_row,
            skip_row,
            gain_row,
        ),
    )
    row_sums = lax.psum(row_part, "mp")
    scaled, grad_gate, grad_scan, gate_rows, gate_stats = run_gate(
        span_fill, gate_pre, scan, grad_scaled, row_sums, gain_row, inner_total
    )
    scaled_bound = jnp.max(jnp.abs(gate_gain)) * (float(inner_total) ** 0.5 * token_rows)
    upstream_top = jnp.max(jnp.abs(whole_upstream)).astype(jnp.float32)
    grad_w_out = reduce_tokens(upstream_split, scaled, scaled_bound * upstream_top).T
    normed_bound = jnp.max(jnp.abs(norm_gain)) * (float(model_width) ** 0.5 * token_rows)
    grad_w_gate = reduce_tokens(normed_split, grad_gate, normed_bound * jnp.max(gate_stats[1]))
    mixed_share = lax.psum_scatter(
        jnp.dot(scaled, w_out, preferred_element_type=jnp.float32),
        "mp",
        scatter_dimension=1,
        tiled=True,
    )
    own_in = hidden_in.astype(jnp.float32)
    output = (own_in + mixed_share).astype(jnp.bfloat16)

    grad_value, select_parts, grad_step, value_rows, value_stats, small_stats = run_backward(
        span_starts,
        span_fill,
        (grad_scan, scan, values, value_pre, selects, delta, sums, step_pre),
        states,
        (conv_value, conv_value_bias[None, :], bias_step, decay_row, skip_row),
        model_parts,
    )
    grad_w_value = reduce_tokens(
        normed_split, grad_value, normed_bound * jnp.max(value_stats[CONV + 2])
    )
    same_links = layout(span_starts, token_rows)
    select_blocks = select_parts.reshape(model_groups, 2, token_rows, part)
    grad_selects = scatter_plain(
        lax.dynamic_index_in_dim(select_blocks, 1 - model_side, 1, keepdims=False),
        lax.dynamic_index_in_dim(select_blocks, model_side, 1, keepdims=False),
        "mp",
        jnp.float32,
    )
    select_own_pre = lax.dynamic_slice_in_dim(select_pre, select_start, part, 1)
    _, select_pull = jax.vjp(
        lambda pre_act, kernel, bias_vec: conv_silu(pre_act, kernel, bias_vec, same_links),
        select_own_pre,
        lax.dynamic_slice_in_dim(conv_select, select_start, part, 1),
        lax.dynamic_slice_in_dim(conv_select_bias, select_start, part, 0),
    )
    grad_select_pre, grad_conv_select_own, grad_conv_select_bias_own = select_pull(grad_selects)
    grad_select_low = grad_select_pre.astype(jnp.bfloat16)
    small_low = jnp.concatenate(
        [
            grad_step[:, :local_heads],
            grad_select_low,
            jnp.zeros((token_rows, -(local_heads + part) % LANES), jnp.bfloat16),
        ],
        axis=1,
    )
    small_top = jnp.maximum(
        jnp.max(small_stats[2]), jnp.max(jnp.abs(grad_select_low)).astype(jnp.float32)
    )
    grad_w_small = reduce_tokens(normed_split, small_low, normed_bound * small_top)
    grad_w_step = grad_w_small[:, :local_heads]
    grad_w_select = lax.all_gather(
        grad_w_small[:, local_heads : local_heads + part], "mp", axis=1, tiled=True
    )
    norm_dot = lax.psum(
        gate_rows[0]
        + value_rows[0]
        + jnp.sum(grad_select_low.astype(jnp.float32) * select_own_pre, axis=1),
        "mp",
    )
    back = [
        back_features(
            spot.reshape(1), (grad_gate, grad_value, small_low), (w_gate, w_value, w_small), model_groups
        )
        for spot in (1 - model_side, model_side)
    ]
    grad_normed = scatter_plain(back[0], back[1], "mp", jnp.bfloat16)
    own_gain = lax.dynamic_slice_in_dim(norm_gain, offset, feature_piece, 0)
    own_scale = input_scale[:, :1]
    weighted_in = grad_normed * own_gain[None, :]
    grad_hidden_in = (
        cotangent.astype(jnp.float32)
        + weighted_in * own_scale
        - own_in * own_scale**2 * norm_dot[:, None] / model_width
    )
    grad_norm_gain = jnp.sum(grad_normed * own_in * own_scale, axis=0)
    place = jnp.zeros((CONV + 1, model_parts, part), jnp.float32)
    select_small = lax.dynamic_update_slice_in_dim(
        place,
        jnp.concatenate([grad_conv_select_own, grad_conv_select_bias_own[None, :]], axis=0)[:, None, :],
        model_spot,
        1,
    ).reshape(CONV + 1, -1)
    select_small = lax.psum(select_small, "mp")
    likes = (
        grad_norm_gain,
        value_stats[:CONV],
        value_stats[CONV],
        select_small[:CONV],
        select_small[CONV],
        small_stats[0, :local_heads],
        small_stats[1, :local_heads],
        jnp.sum(value_stats[CONV + 1].reshape(local_heads, head_dim), axis=1),
        gate_stats[0],
    )
    small_sums = unpack(sum_all(pack(likes), "dp"), likes)
    return (
        output,
        grad_hidden_in,
        small_sums[0],
        grad_w_gate,
        grad_w_value,
        grad_w_select,
        grad_w_step,
        small_sums[1],
        small_sums[2],
        small_sums[3],
        small_sums[4],
        small_sums[5],
        small_sums[6],
        small_sums[7],
        small_sums[8],
        grad_w_out,
    )


def solution(mesh):
    in_specs = (
        P("dp", "mp"),
        P("dp", "mp"),
        P("dp"),
        P("dp"),
        P(),
        P(None, "mp"),
        P(None, "mp"),
        P(),
        P(None, "mp"),
        P(None, "mp"),
        P("mp"),
        P(),
        P(),
        P("mp"),
        P("mp"),
        P("mp"),
        P("mp"),
        P("mp", None),
    )
    out_specs = (
        P("dp", "mp"),
        P("dp", "mp"),
        P("mp"),
        P("dp", "mp"),
        P("dp", "mp"),
        P("dp", None),
        P("dp", "mp"),
        P(None, "mp"),
        P("mp"),
        P(),
        P(),
        P("mp"),
        P("mp"),
        P("mp"),
        P("mp"),
        P("mp", "dp"),
    )
    return jax.shard_map(
        on_device, mesh=mesh, in_specs=in_specs, out_specs=out_specs, check_vma=False
    )
```

```python
import functools

import jax
import jax.numpy as jnp
from jax import lax
from jax.experimental import pallas as pl
from jax.experimental.pallas import tpu as pltpu
from jax.sharding import PartitionSpec as P

CONV = 4
SPAN = 256
LANES = 128
EXTRA = 8
TOP = 15.0
FAR = -1e30
PARTS = 2
epsilon = 1e-05
exact_mode = lax.Precision.HIGHEST


def settings(mebibytes, axes=1):
    return pltpu.CompilerParams(
        dimension_semantics=("arbitrary",) * axes, vmem_limit_bytes=mebibytes << 20
    )


def scalars():
    return pl.BlockSpec(memory_space=pltpu.SMEM)


def fixed(shape):
    return pl.BlockSpec(shape, lambda *_: (0,) * len(shape))


def split_bits(value):
    high = value.astype(jnp.bfloat16)
    low = (value - high.astype(jnp.float32)).astype(jnp.bfloat16)
    return high, low


def dot(left, right):
    return lax.dot_general(left, right, (((1,), (0,)), ((), ())), preferred_element_type=jnp.float32)


def dot_lanes(left, right):
    return lax.dot_general(left, right, (((1,), (1,)), ((), ())), preferred_element_type=jnp.float32)


def dot_rows(left, right):
    return lax.dot_general(left, right, (((0,), (0,)), ((), ())), preferred_element_type=jnp.float32)


def exact(left, right):
    return jnp.dot(left, right, precision=exact_mode, preferred_element_type=jnp.float32)


def beside(*pieces):
    return jnp.concatenate(pieces, axis=1)


def above(*pieces):
    return jnp.concatenate(pieces, axis=0)


def sigmoid(value):
    return 1.0 / (1.0 + jnp.exp(-value))


def iota(shape, axis):
    return lax.broadcasted_iota(jnp.int32, shape, axis)


def two_heads(columns, pair, in_first):
    first = columns[:, 2 * pair : 2 * pair + 1]
    second = columns[:, 2 * pair + 1 : 2 * pair + 2]
    return jnp.where(in_first, first, second)


def row_of(columns):
    return jnp.sum(jnp.transpose(columns), axis=0, keepdims=True)


def live_rows(fill, width):
    return (iota((SPAN, width), 0) < fill).astype(jnp.float32)


def wide_lanes(start, width):
    return pl.ds(pl.multiple_of(start * width, min(width, LANES)), width)


def store_ours(side, block, spot, ours_out, piece):
    for index in range(block.shape[1] // (2 * piece)):
        first = block[:, 2 * index * piece : (2 * index + 1) * piece]
        second = block[:, (2 * index + 1) * piece : (2 * index + 2) * piece]
        group = spot * (block.shape[1] // (2 * piece)) + index
        ours_out[pl.ds(group, 1)] = jnp.where(side == 0, first, second)[None]


def guess(flops, moved, exps=0):
    return pl.CostEstimate(flops=1, bytes_accessed=1, transcendentals=0)


def conv_of(extended, kernel, bias, lanes):
    total = bias[:, lanes]
    for back in range(CONV):
        tap = kernel[CONV - 1 - back : CONV - back, lanes]
        total = total + tap * extended[EXTRA - back : EXTRA - back + SPAN, lanes]
    return total


def forward_kernel(
    side,
    spots,
    starts,
    fills,
    norm_gain,
    w_value,
    w_gate,
    w_select,
    w_step,
    conv_value,
    conv_value_bias,
    conv_select,
    conv_select_bias,
    step_bias,
    decay_log,
    skip,
    *refs,
    piece,
):
    blocks = refs[:-18]
    (
        ours_out,
        scale_out,
        scale_columns_out,
        value_pre,
        gate_pre,
        select_pre,
        step_pre,
        values_out,
        selects_out,
        scan_out,
        gated_out,
        delta_out,
        sum_out,
        state_out,
        rows_out,
        extended,
        extended_select,
        state,
    ) = refs[-18:]
    step = pl.program_id(0)
    fresh = starts[step] == 1
    width = value_pre.shape[1]
    state_dim = select_pre.shape[1] // 2

    part_width = blocks[0].shape[1]
    total = jnp.zeros((SPAN, LANES), jnp.float32)
    for block in blocks:
        for start in range(0, part_width, LANES):
            part = block[:, start : start + LANES].astype(jnp.float32)
            total = total + part * part
    mean = jnp.sum(total, axis=1, keepdims=True) / (part_width * len(blocks))
    scale = lax.rsqrt(mean + epsilon)
    scale_columns_out[...] = jnp.broadcast_to(scale, (SPAN, LANES))
    scale_out[...] = jnp.transpose(scale_columns_out[...])[:1, :]
    sums = [None] * 4
    for index, block in enumerate(blocks):
        spot = spots[index]
        window = wide_lanes(spot, part_width)
        own_gain = norm_gain[:, window]
        normed = (block[...].astype(jnp.float32) * scale * own_gain).astype(jnp.bfloat16)
        store_ours(side[0], normed, spot, ours_out, piece)
        for at, weights in enumerate((w_select, w_step, w_value, w_gate)):
            product = dot(normed, weights[window, :])
            sums[at] = product if index == 0 else sums[at] + product
    select_pre[...], step_pre[...], value_pre[...], gate_pre[...] = sums

    @pl.when(fresh)
    def _():
        extended[:EXTRA, :] = jnp.zeros((EXTRA, width), jnp.float32)
        extended_select[:EXTRA, :] = jnp.zeros((EXTRA, 2 * state_dim), jnp.float32)
        state[...] = jnp.zeros(state.shape, jnp.float32)

    @pl.when(jnp.logical_not(fresh))
    def _():
        extended[:EXTRA, :] = extended[SPAN:, :]
        extended_select[:EXTRA, :] = extended_select[SPAN:, :]

    extended[EXTRA:, :] = value_pre[...]
    extended_select[EXTRA:, :] = select_pre[...]
    state_out[0] = state[...]

    live = live_rows(fills[step], LANES)
    pre_step = step_pre[...] + step_bias[...]
    delta = live * (jnp.maximum(pre_step, 0.0) + jnp.log1p(jnp.exp(-jnp.abs(pre_step))))
    rate = -jnp.exp(decay_log[...])
    lower = (iota((SPAN, SPAN), 0) >= iota((SPAN, SPAN), 1)).astype(jnp.float32)
    cumulative = exact(lower, delta * rate)
    delta_out[...] = delta
    sum_out[...] = cumulative
    sums_across = jnp.transpose(cumulative)
    delta_across = jnp.transpose(delta)
    grown = jnp.exp(cumulative)
    tail = delta * jnp.exp(cumulative[SPAN - 1 : SPAN, :] - cumulative)

    halves = []
    for half in range(2):
        lanes = slice(half * state_dim, (half + 1) * state_dim)
        mixed = conv_of(extended_select, conv_select, conv_select_bias, lanes)
        chosen = (mixed * sigmoid(mixed)).astype(jnp.bfloat16)
        selects_out[:, lanes] = chosen
        halves.append(chosen)
    inflow, readout = halves
    inflow_across = jnp.transpose(inflow.astype(jnp.float32)).astype(jnp.bfloat16)
    scores = dot_lanes(readout, inflow)
    past = iota((SPAN, SPAN), 0) >= iota((SPAN, SPAN), 1)
    in_first = iota((SPAN, LANES), 1) < LANES // 2
    row_first = iota((1, LANES), 1) < LANES // 2
    readout_twice = beside(readout, readout)
    squares = jnp.zeros((SPAN, LANES), jnp.float32)
    for pair in range(width // LANES):
        lanes = slice(pair * LANES, (pair + 1) * LANES)
        mixed = conv_of(extended, conv_value, conv_value_bias, lanes)
        value_low = (mixed * sigmoid(mixed)).astype(jnp.bfloat16)
        values_out[:, lanes] = value_low
        value = value_low.astype(jnp.float32)
        entering = state[:, lanes]
        scan = dot(readout_twice, above(*split_bits(entering))) * two_heads(grown, pair, in_first)
        scan = scan + two_heads(skip[...], pair, row_first) * value
        for which in range(2):
            head = 2 * pair + which
            gaps = cumulative[:, head : head + 1] - sums_across[head : head + 1, :]
            weights = jnp.exp(jnp.where(past, gaps, FAR))
            mixing = scores * weights * delta_across[head : head + 1, :]
            own = jnp.where(in_first == (which == 0), value_low, jnp.zeros_like(value_low))
            high, low = split_bits(mixing)
            scan = scan + dot(high, own) + dot(low, own)
        scan_out[:, lanes] = scan
        gate = gate_pre[:, lanes]
        gated = live * scan * gate * sigmoid(gate)
        squares = squares + gated * gated
        gated_out[:, lanes] = gated
        weighted = value * two_heads(tail, pair, in_first)
        high, low = split_bits(weighted)
        last = two_heads(grown[SPAN - 1 : SPAN, :], pair, row_first)
        state[:, lanes] = entering * last + dot(inflow_across, high) + dot(inflow_across, low)
    rows_out[...] = row_of(squares)


def resident(shape):
    return pl.BlockSpec(shape, lambda *_: (0,) * len(shape), pipeline_mode=pl.Buffered(1))


def run_forward(side, spots, starts, fills, blocks, gain, weights, vectors, piece):
    rows, part_width = blocks[0].shape
    groups = part_width * len(blocks) // (2 * piece)
    w_value, w_gate, w_select, w_step = weights
    width = w_value.shape[1]
    spans = rows // SPAN
    select_width = w_select.shape[1]

    def tile(columns):
        return pl.BlockSpec((SPAN, columns), lambda i: (i, 0))

    def like(columns, dtype):
        return jax.ShapeDtypeStruct((rows, columns), dtype)

    strip = pl.BlockSpec((1, SPAN), lambda i: (0, i))
    return pl.pallas_call(
        functools.partial(forward_kernel, piece=piece),
        grid=(spans,),
        in_specs=[scalars()] * 4
        + [fixed(gain.shape)]
        + [resident(array.shape) for array in weights]
        + [fixed(array.shape) for array in vectors]
        + [tile(part_width)] * len(blocks),
        out_specs=[
            pl.BlockSpec((groups, SPAN, piece), lambda i: (0, i, 0)),
            strip,
            tile(LANES),
            tile(width),
            tile(width),
            tile(select_width),
            tile(LANES),
            tile(width),
            tile(select_width),
            tile(width),
            tile(width),
            tile(LANES),
            tile(LANES),
            pl.BlockSpec((1, select_width // 2, width), lambda i: (i, 0, 0)),
            strip,
        ],
        out_shape=[
            jax.ShapeDtypeStruct((groups, rows, piece), jnp.bfloat16),
            jax.ShapeDtypeStruct((1, rows), jnp.float32),
            like(LANES, jnp.float32),
            like(width, jnp.float32),
            like(width, jnp.float32),
            like(select_width, jnp.float32),
            like(LANES, jnp.float32),
            like(width, jnp.bfloat16),
            like(select_width, jnp.bfloat16),
            like(width, jnp.float32),
            like(width, jnp.float32),
            like(LANES, jnp.float32),
            like(LANES, jnp.float32),
            jax.ShapeDtypeStruct((spans, select_width // 2, width), jnp.float32),
            jax.ShapeDtypeStruct((1, rows), jnp.float32),
        ],
        scratch_shapes=[
            pltpu.VMEM((SPAN + EXTRA, width), jnp.float32),
            pltpu.VMEM((SPAN + EXTRA, select_width), jnp.float32),
            pltpu.VMEM((select_width // 2, width), jnp.float32),
        ],
        compiler_params=settings(50),
        cost_estimate=guess(0, 0),
        name="forward",
    )(side, spots, starts, fills, gain, *weights, *vectors, *blocks)


def scale_column(rows, total_width):
    turned = jnp.transpose(above(rows[...], jnp.zeros((LANES - 1, SPAN), jnp.float32)))
    return lax.rsqrt(turned[:, 0:1] / total_width + epsilon)


def scale_kernel(gated_in, squares, gain, scaled_out, *, total_width):
    width = gated_in.shape[1]
    scale = jnp.broadcast_to(scale_column(squares, total_width), (SPAN, LANES))
    for start in range(0, width, LANES):
        lanes = slice(start, start + LANES)
        scaled_out[:, lanes] = (gated_in[:, lanes] * scale * gain[:, lanes]).astype(jnp.bfloat16)


def run_scale(gated, squares, gain, total_width):
    rows, width = gated.shape
    return pl.pallas_call(
        functools.partial(scale_kernel, total_width=total_width),
        grid=(rows // SPAN,),
        in_specs=[
            pl.BlockSpec((SPAN, width), lambda i: (i, 0)),
            pl.BlockSpec((1, SPAN), lambda i: (0, i)),
            fixed((1, width)),
        ],
        out_specs=pl.BlockSpec((SPAN, width), lambda i: (i, 0)),
        out_shape=jax.ShapeDtypeStruct((rows, width), jnp.bfloat16),
        compiler_params=settings(32),
        cost_estimate=guess(6 * rows * width, 6 * rows * width),
        name="scale",
    )(gated, squares, gain)


def cotangent_kernel(
    side, spots, rows, norm_gain, gain, w_out, gated_in, *refs, piece
):
    blocks = refs[:-5]
    grad_out, rows_out, ours_out, other_normed_out, other_out = refs[-5:]
    width = blocks[0].shape[1] // 2
    cross = width // 2
    turned = jnp.transpose(above(rows[...], jnp.zeros((LANES - 1, SPAN), jnp.float32)))
    scale = turned[:, 0:1]
    each = cross // piece
    total = None
    for index, block in enumerate(blocks):
        spot = spots[index]
        upstream = block[:, :width]
        product = dot_lanes(upstream, w_out[:, wide_lanes(spot, width)])
        total = product if index == 0 else total + product
        store_ours(side[0], upstream, spot, ours_out, piece)
        for inner in range(each):
            group = spot * each + inner
            own_gain = norm_gain[pl.ds(2 * group + side[0], 1), :]
            start = width + inner * piece
            hidden = block[:, start : start + piece].astype(jnp.float32)
            other_normed_out[pl.ds(group, 1)] = (hidden * scale * own_gain).astype(jnp.bfloat16)[None]
            start = width + cross + inner * piece
            other_out[pl.ds(group, 1)] = block[:, start : start + piece][None]
    grad_out[...] = total
    products = jnp.zeros((SPAN, LANES), jnp.float32)
    for start in range(0, gated_in.shape[1], LANES):
        lanes = slice(start, start + LANES)
        products = products + grad_out[:, lanes] * gain[:, lanes] * gated_in[:, lanes]
    rows_out[...] = row_of(products)


def run_cotangent(side, spots, rows_in, norm_gain, gain, w_out, gated, blocks, piece):
    rows, width = gated.shape
    features = w_out.shape[1]
    groups = features // (2 * piece)
    strip = pl.BlockSpec((1, SPAN), lambda i: (0, i))

    def tile(columns):
        return pl.BlockSpec((SPAN, columns), lambda i: (i, 0))

    pieces = pl.BlockSpec((groups, SPAN, piece), lambda i: (0, i, 0))
    pieces_shape = jax.ShapeDtypeStruct((groups, rows, piece), jnp.bfloat16)
    return pl.pallas_call(
        functools.partial(cotangent_kernel, piece=piece),
        grid=(rows // SPAN,),
        in_specs=[
            scalars(),
            scalars(),
            strip,
            fixed((2 * groups, piece)),
            fixed(gain.shape),
            resident(w_out.shape),
            tile(width),
        ]
        + [tile(block.shape[1]) for block in blocks],
        out_specs=[tile(width), strip, pieces, pieces, pieces],
        out_shape=[
            jax.ShapeDtypeStruct((rows, width), jnp.float32),
            jax.ShapeDtypeStruct((1, rows), jnp.float32),
            pieces_shape,
            pieces_shape,
            pieces_shape,
        ],
        compiler_params=settings(48),
        cost_estimate=guess(0, 0),
        name="cotangent",
    )(
        side,
        spots,
        rows_in,
        norm_gain.reshape(2 * groups, piece),
        gain,
        w_out,
        gated,
        *blocks,
    )


def mixed_kernel(place, scaled, w_out, *outs):
    product = dot(scaled[...], w_out[...])
    for index, out in enumerate(outs):

        @pl.when(pl.program_id(0) == index)
        def _():
            out[...] = product


def run_mixed(place, scaled, w_out, groups):
    rows, width = scaled.shape
    piece = w_out.shape[1] // (2 * groups)

    def column(g, at):
        side = jnp.where(g < groups, 1 - at[1], at[1])
        return 0, 2 * ((at[0] + g) % groups) + side

    return pl.pallas_call(
        mixed_kernel,
        grid_spec=pltpu.PrefetchScalarGridSpec(
            num_scalar_prefetch=1,
            grid=(2 * groups,),
            in_specs=[resident((rows, width)), pl.BlockSpec((width, piece), column)],
            out_specs=[resident((rows, piece))] * (2 * groups),
        ),
        out_shape=[jax.ShapeDtypeStruct((rows, piece), jnp.float32)] * (2 * groups),
        compiler_params=settings(40),
        cost_estimate=guess(0, 0),
        name="mixed",
    )(place, scaled, w_out)


def backward_kernel(
    starts,
    fills,
    gate_pre,
    grad_scaled,
    scan_in,
    values_in,
    value_pre,
    value_before,
    selects_in,
    delta_in,
    sum_in,
    step_pre,
    state_in,
    conv_value,
    conv_value_bias,
    gain,
    squares,
    products,
    step_bias,
    decay_log,
    skip,
    model_place,
    *rest,
    spans,
    first_head,
    adds,
    total_width,
):
    if adds:
        before_theirs, before_ours, rest = rest[0], rest[1], rest[2:]
    (
        value_out,
        theirs_out,
        ours_out,
        step_out,
        rows_out,
        stat_out,
        small_out,
        extended,
        shifted,
        state,
        carried,
    ) = rest
    step = pl.program_id(0)
    span = spans - 1 - step
    width = values_in.shape[1]
    state_dim = selects_in.shape[1] // 2
    following = jnp.minimum(span + 1, spans - 1)
    joined = jnp.logical_and(step > 0, starts[following] == 0)

    @pl.when(jnp.logical_not(joined))
    def _():
        shifted[SPAN:, :] = jnp.zeros((EXTRA, width), jnp.float32)
        state[...] = jnp.zeros(state.shape, jnp.float32)
        carried[...] = jnp.zeros(carried.shape, jnp.float32)

    @pl.when(joined)
    def _():
        shifted[SPAN:, :] = shifted[:EXTRA, :]

    @pl.when(step == 0)
    def _():
        stat_out[...] = jnp.zeros(stat_out.shape, jnp.float32)
        small_out[...] = jnp.zeros(small_out.shape, jnp.float32)

    fresh = starts[span] == 1

    @pl.when(fresh)
    def _():
        extended[:EXTRA, :] = jnp.zeros((EXTRA, width), jnp.float32)

    @pl.when(jnp.logical_not(fresh))
    def _():
        extended[:EXTRA, :] = value_before[...]

    extended[EXTRA:, :] = value_pre[...]

    delta = delta_in[...]
    cumulative = sum_in[...]
    sums_across = jnp.transpose(cumulative)
    grown = jnp.exp(cumulative)
    tail = jnp.exp(cumulative[SPAN - 1 : SPAN, :] - cumulative)
    delta_tail = delta * tail
    inflow = selects_in[:, :state_dim]
    readout = selects_in[:, state_dim:]
    readout_across = jnp.transpose(readout.astype(jnp.float32)).astype(jnp.bfloat16)
    scores = dot_lanes(inflow, readout)
    ahead = iota((SPAN, SPAN), 1) >= iota((SPAN, SPAN), 0)
    in_first = iota((SPAN, LANES), 1) < LANES // 2
    row_first = iota((1, LANES), 1) < LANES // 2
    live = live_rows(fills[span], LANES)
    turned = jnp.transpose(above(products[...], jnp.zeros((LANES - 1, SPAN), jnp.float32)))
    norm_scale = scale_column(squares, total_width)
    norm_pull = norm_scale * norm_scale * norm_scale * turned[:, 0:1] / total_width
    norm_scale = jnp.broadcast_to(norm_scale, (SPAN, LANES))
    norm_pull = jnp.broadcast_to(norm_pull, (SPAN, LANES))
    inflow_twice = beside(inflow, inflow)
    grad_scores = jnp.zeros((SPAN, SPAN), jnp.float32)
    grad_inflow = jnp.zeros((SPAN, state_dim), jnp.float32)
    grad_readout = jnp.zeros((SPAN, state_dim), jnp.float32)
    change = jnp.zeros((SPAN, LANES), jnp.float32)
    direct = jnp.zeros((SPAN, LANES), jnp.float32)
    jump = jnp.zeros((8, LANES), jnp.float32)
    dots = jnp.zeros((SPAN, LANES), jnp.float32)
    for own_pair in range(width // LANES):
        lanes = slice(own_pair * LANES, (own_pair + 1) * LANES)
        pair = first_head // 2 + own_pair
        gate = gate_pre[:, lanes]
        scan = scan_in[:, lanes]
        before_norm = grad_scaled[:, lanes]
        own_gain = gain[:, lanes]
        sig = sigmoid(gate)
        opened = live * gate * sig
        gated = scan * opened
        grad_gated = before_norm * own_gain * norm_scale - gated * norm_pull
        grad_gate = grad_gated * live * scan * sig * (1.0 + gate * (1.0 - sig))
        gate_low = grad_gate.astype(jnp.bfloat16)
        value_out[:, lanes] = gate_low
        dots = dots + gate_low.astype(jnp.float32) * gate
        stat_out[CONV + 2 : CONV + 3, lanes] += jnp.sum(
            before_norm * gated * norm_scale, axis=0, keepdims=True
        )
        upstream = grad_gated * opened
        up_high, up_low = split_bits(upstream)
        value_low = values_in[:, lanes]
        value = value_low.astype(jnp.float32)
        own_skip = two_heads(skip[...], pair, row_first)
        arriving = state[:, lanes]
        arriving_high, arriving_low = split_bits(arriving)
        entering = state_in[0, :, lanes]
        entering_high, entering_low = split_bits(entering)
        pulled = dot(inflow_twice, above(arriving_high, arriving_low)) * two_heads(tail, pair, in_first)
        up_both = beside(up_high, up_low)
        for which in range(2):
            head = 2 * pair + which
            mine = in_first == (which == 0)
            nothing = jnp.zeros_like(value_low)
            gaps = sums_across[head : head + 1, :] - cumulative[:, head : head + 1]
            weights = jnp.exp(jnp.where(ahead, gaps, FAR))
            high, low = split_bits(scores * weights)
            own_high = jnp.where(mine, up_high, nothing)
            own_low = jnp.where(mine, up_low, nothing)
            pulled = pulled + dot(high, own_high) + dot(high, own_low) + dot(low, own_high)
            own_value = jnp.where(mine, value_low, nothing)
            outer = dot_lanes(beside(own_value, own_value), up_both)
            grad_scores = grad_scores + outer * weights * delta[:, head : head + 1]
        delta_both = two_heads(delta, pair, in_first)
        grad_value = own_skip * upstream + delta_both * pulled
        pull_value = value * pulled
        spread = (
            iota((LANES, LANES), 1) == 2 * pair + iota((LANES, LANES), 0) // (LANES // 2)
        ).astype(jnp.bfloat16)
        spread_twice = above(spread, spread)
        moved = upstream * (scan - own_skip * value) - delta_both * pull_value
        change = change + dot(beside(*split_bits(moved)), spread_twice)
        direct = direct + dot(beside(*split_bits(pull_value)), spread_twice)
        grown_up = upstream * two_heads(grown, pair, in_first)
        high, low = split_bits(grown_up)
        grad_readout = grad_readout + dot_lanes(
            beside(high, low, high), beside(entering_high, entering_high, entering_low)
        )
        last = two_heads(grown[SPAN - 1 : SPAN, :], pair, row_first)
        leaving = arriving * last + dot(readout_across, high) + dot(readout_across, low)
        tail_value = value * two_heads(delta_tail, pair, in_first)
        high, low = split_bits(tail_value)
        grad_inflow = grad_inflow + dot_lanes(
            beside(high, low, high), beside(arriving_high, arriving_high, arriving_low)
        )
        jump = jump + exact(carried[:, lanes], spread.astype(jnp.float32))
        state[:, lanes] = leaving
        carried[:, lanes] = jnp.broadcast_to(
            jnp.sum(leaving * entering, axis=0, keepdims=True), (8, LANES)
        )
        mixed = conv_of(extended, conv_value, conv_value_bias, lanes)
        sig = sigmoid(mixed)
        inner = grad_value * sig * (1.0 + mixed * (1.0 - sig))
        shifted[:SPAN, lanes] = inner
        grad_pre = jnp.zeros((SPAN, LANES), jnp.float32)
        for back in range(CONV):
            tap = conv_value[CONV - 1 - back : CONV - back, lanes]
            grad_pre = grad_pre + tap * shifted[back : back + SPAN, lanes]
            stat_out[CONV - 1 - back : CONV - back, lanes] += jnp.sum(
                inner * extended[EXTRA - back : EXTRA - back + SPAN, lanes], axis=0, keepdims=True
            )
        stat_out[CONV : CONV + 1, lanes] += jnp.sum(inner, axis=0, keepdims=True)
        stat_out[CONV + 1 : CONV + 2, lanes] += jnp.sum(value * upstream, axis=0, keepdims=True)
        grad_low = grad_pre.astype(jnp.bfloat16)
        value_out[:, width + own_pair * LANES : width + (own_pair + 1) * LANES] = grad_low
        wide = grad_low.astype(jnp.float32)
        dots = dots + wide * extended[EXTRA:, lanes]
    high, low = split_bits(grad_scores)
    grad_inflow = grad_inflow + dot(high, readout) + dot(low, readout)
    high, low = split_bits(jnp.transpose(grad_scores))
    grad_readout = grad_readout + dot(high, inflow) + dot(low, inflow)
    groups, _, part = theirs_out.shape
    both = (grad_inflow, grad_readout)
    for index in range(groups):
        slot = pl.ds(lax.rem(index - model_place[0] + groups, groups), 1)
        pieces = []
        for side in range(2):
            start = (2 * index + side) * part
            pieces.append(both[start // state_dim][:, start % state_dim : start % state_dim + part])
        own = jnp.where(model_place[1] == 0, pieces[0], pieces[1])
        other = jnp.where(model_place[1] == 0, pieces[1], pieces[0])
        if adds:
            own = own + before_ours[slot][0]
            other = other + before_theirs[slot][0]
        ours_out[slot] = own[None]
        theirs_out[slot] = other[None]
    upper = (iota((SPAN, SPAN), 1) >= iota((SPAN, SPAN), 0)).astype(jnp.float32)
    flow = exact(upper, change) + jump[0:1, :]
    rate = -jnp.exp(decay_log[...])
    grad_delta = direct + rate * flow
    pre_step = step_pre[...]
    grad_step = grad_delta * live * sigmoid(pre_step + step_bias[...])
    column = iota((SPAN, LANES), 1)
    last_head = first_head + width // (LANES // 2)
    grad_step = jnp.where(jnp.logical_and(column >= first_head, column < last_head), grad_step, 0.0)
    step_low = grad_step.astype(jnp.bfloat16)
    step_out[...] = step_low
    wide = step_low.astype(jnp.float32)
    dots = dots + wide * pre_step
    small_out[0:1, :] += jnp.sum(grad_step, axis=0, keepdims=True)
    small_out[1:2, :] += rate * jnp.sum(delta * flow, axis=0, keepdims=True)
    rows_out[...] = row_of(dots)


def run_backward(
    starts, fills, tiles, strips, states, vectors, parts, at_part, model_place, previous, total_width
):
    gate_pre, grad_scaled, scan, values, value_pre, selects, delta, sums, step_pre = tiles
    conv_value, conv_value_bias, gain, step_bias, decay_log, skip = vectors
    rows, whole = value_pre.shape
    width = whole // PARTS
    heads = width // (LANES // 2)
    spans = rows // SPAN
    select_width = selects.shape[1]
    half = at_part

    def tile(columns, at=0):
        return pl.BlockSpec((SPAN, columns), lambda i: (spans - 1 - i, at))

    def out_tile(columns):
        return pl.BlockSpec((SPAN, columns), lambda i: (spans - 1 - i, 0))

    select_tile = pl.BlockSpec(
        (parts // 2, SPAN, select_width // parts), lambda i: (0, spans - 1 - i, 0)
    )
    strip = pl.BlockSpec((1, SPAN), lambda i: (0, spans - 1 - i))
    before = pl.BlockSpec(
        (EXTRA, width), lambda i: (jnp.maximum((spans - 1 - i) * (SPAN // EXTRA) - 1, 0), half)
    )
    return pl.pallas_call(
        functools.partial(
            backward_kernel,
            spans=spans,
            first_head=half * heads,
            adds=previous is not None,
            total_width=total_width,
        ),
        grid=(spans,),
        in_specs=[
            scalars(),
            scalars(),
            tile(width, half),
            tile(width, half),
            tile(width, half),
            tile(width, half),
            tile(width, half),
            before,
            tile(select_width),
            tile(LANES),
            tile(LANES),
            tile(LANES),
            pl.BlockSpec((1, select_width // 2, width), lambda i: (spans - 1 - i, 0, half)),
            pl.BlockSpec((CONV, width), lambda i: (0, half)),
            pl.BlockSpec((1, width), lambda i: (0, half)),
            pl.BlockSpec((1, width), lambda i: (0, half)),
            strip,
            strip,
            fixed((1, LANES)),
            fixed((1, LANES)),
            fixed((1, LANES)),
            scalars(),
        ]
        + ([] if previous is None else [select_tile, select_tile]),
        out_specs=[
            out_tile(2 * width),
            select_tile,
            select_tile,
            out_tile(LANES),
            pl.BlockSpec((1, SPAN), lambda i: (0, spans - 1 - i)),
            fixed((8, width)),
            fixed((8, LANES)),
        ],
        out_shape=[
            jax.ShapeDtypeStruct((rows, 2 * width), jnp.bfloat16),
            jax.ShapeDtypeStruct((parts // 2, rows, select_width // parts), jnp.float32),
            jax.ShapeDtypeStruct((parts // 2, rows, select_width // parts), jnp.float32),
            jax.ShapeDtypeStruct((rows, LANES), jnp.bfloat16),
            jax.ShapeDtypeStruct((1, rows), jnp.float32),
            jax.ShapeDtypeStruct((8, width), jnp.float32),
            jax.ShapeDtypeStruct((8, LANES), jnp.float32),
        ],
        scratch_shapes=[
            pltpu.VMEM((SPAN + EXTRA, width), jnp.float32),
            pltpu.VMEM((SPAN + EXTRA, width), jnp.float32),
            pltpu.VMEM((select_width // 2, width), jnp.float32),
            pltpu.VMEM((8, width), jnp.float32),
        ],
        compiler_params=settings(52),
        cost_estimate=guess(20000 * rows * width, 20 * rows * width, 300 * rows * width),
        name="backward",
    )(
        starts,
        fills,
        gate_pre,
        grad_scaled,
        scan,
        values,
        value_pre,
        value_pre,
        selects,
        delta,
        sums,
        step_pre,
        states,
        conv_value,
        conv_value_bias,
        gain,
        *strips,
        step_bias,
        decay_log,
        skip,
        model_place,
        *([] if previous is None else previous),
    )


def pair_kernel(*refs):
    groups = len(refs) // 3
    for index in range(groups):
        out = refs[2 * groups + index]
        out[...] = (refs[index][...] + refs[groups + index][...]).astype(out.dtype)


def run_pair(ours, came, wire):
    rows, columns = ours[0].shape
    groups = len(ours)
    tile = pl.BlockSpec((SPAN, columns), lambda i: (i, 0))
    return pl.pallas_call(
        pair_kernel,
        grid=(rows // SPAN,),
        in_specs=[tile] * (2 * groups),
        out_specs=[tile] * groups,
        out_shape=[jax.ShapeDtypeStruct((rows, columns), jnp.float32)]
        + [jax.ShapeDtypeStruct((rows, columns), wire)] * (groups - 1),
        compiler_params=settings(40),
        cost_estimate=guess(0, 0),
        name="pair",
    )(*ours, *came)


def select_kernel(starts, spot, select_pre, kernel, bias, *refs, count):
    grads, steps_in = refs[:count], refs[count:-4]
    low_out, rows_out, stat_out, ahead = refs[-4:]
    rows = select_pre.shape[0]
    part = grads[0].shape[1]
    upstream = grads[0][...]
    for grad in grads[1:]:
        upstream = upstream + grad[...]
    pre = select_pre[:, :part]
    taps = kernel[:, :part]
    own_bias = bias[:, :part]
    for index in range(1, select_pre.shape[1] // part):
        lanes = slice(index * part, (index + 1) * part)
        here = spot[0] == index
        pre = jnp.where(here, select_pre[:, lanes], pre)
        taps = jnp.where(here, kernel[:, lanes], taps)
        own_bias = jnp.where(here, bias[:, lanes], own_bias)
    place = iota((rows, part), 0)
    joined = jnp.zeros((rows, part), jnp.int32)
    for span in range(rows // SPAN):
        joined = jnp.where(place // SPAN == span, 1 - starts[span], joined)
    inside = place % SPAN
    stat_out[...] = jnp.zeros(stat_out.shape, jnp.float32)
    ahead[...] = jnp.zeros(ahead.shape, jnp.float32)
    ahead[EXTRA : EXTRA + rows, :] = pre
    shifted = []
    mixed = own_bias
    for back in range(CONV):
        moved = ahead[EXTRA - back : EXTRA - back + rows, :]
        moved = jnp.where(jnp.logical_or(inside >= back, joined == 1), moved, 0.0)
        shifted.append(moved)
        mixed = mixed + taps[CONV - 1 - back : CONV - back, :] * moved
    sig = sigmoid(mixed)
    inner = upstream * sig * (1.0 + mixed * (1.0 - sig))
    total = jnp.zeros((rows, part), jnp.float32)
    tap_sums = []
    for back in range(CONV):
        tap = taps[CONV - 1 - back : CONV - back, :]
        tap_sums.append(jnp.sum(inner * shifted[back], axis=0, keepdims=True))
        ahead[EXTRA : EXTRA + rows, :] = jnp.where(
            jnp.logical_or(inside >= back, joined == 1), inner, 0.0
        )
        ahead[EXTRA + rows :, :] = jnp.zeros((EXTRA, part), jnp.float32)
        total = total + tap * ahead[EXTRA + back : EXTRA + back + rows, :]
    rows_here = tap_sums[::-1] + [jnp.sum(inner, axis=0, keepdims=True)]
    for index in range(select_pre.shape[1] // part):
        lanes = slice(index * part, (index + 1) * part)
        for at, row in enumerate(rows_here):
            stat_out[at : at + 1, lanes] = jnp.where(spot[0] == index, row, 0.0)
    low = total.astype(jnp.bfloat16)
    dots = jnp.sum(low.astype(jnp.float32) * pre, axis=1, keepdims=True)
    rows_out[...] = jnp.transpose(jnp.broadcast_to(dots, (rows, LANES)))[:1, :]
    steps = steps_in[0][...].astype(jnp.float32)
    for piece in steps_in[1:]:
        steps = steps + piece[...].astype(jnp.float32)
    pieces = [steps[:, : LANES // 2], low.astype(jnp.float32)]
    if part < LANES // 2:
        pieces.append(jnp.zeros((rows, LANES // 2 - part), jnp.float32))
    low_out[...] = jnp.concatenate(pieces, axis=1).astype(jnp.bfloat16)


def run_select(starts, spot, grads, select_pre, kernel, bias, steps):
    rows = select_pre.shape[0]
    part = grads[0].shape[1]
    inputs = (select_pre, kernel, bias, *grads, *steps)
    return pl.pallas_call(
        functools.partial(select_kernel, count=len(grads)),
        in_specs=[scalars(), scalars()] + [pl.BlockSpec(memory_space=pltpu.VMEM)] * len(inputs),
        out_shape=[
            jax.ShapeDtypeStruct((rows, LANES), jnp.bfloat16),
            jax.ShapeDtypeStruct((1, rows), jnp.float32),
            jax.ShapeDtypeStruct((8, select_pre.shape[1]), jnp.float32),
        ],
        scratch_shapes=[pltpu.VMEM((rows + 2 * EXTRA, part), jnp.float32)],
        compiler_params=pltpu.CompilerParams(vmem_limit_bytes=40 << 20),
        cost_estimate=guess(0, 0),
        name="select",
    )(starts, spot, *inputs)


def spread_kernel(place, own_left, other_left, *refs):
    rights, (sends_out, own_out) = refs[:-2], refs[-2:]
    start = 0
    for own_right, other_right in zip(rights[::2], rights[1::2]):
        lanes = slice(start, start + own_right.shape[1])
        start += own_right.shape[1]
        product = dot_rows(own_left[0], own_right[...]) + dot_rows(other_left[0], other_right[...])
        sends_out[0, :, lanes] = product.astype(jnp.bfloat16)

        @pl.when(pl.program_id(0) == place[0])
        def _():
            own_out[:, lanes] = product


def run_spread(place, own_left, other_left, *rights):
    groups, rows, piece = own_left.shape
    columns = sum(right.shape[1] for right in rights[::2])
    left = pl.BlockSpec((1, rows, piece), lambda g: (g, 0, 0))
    return pl.pallas_call(
        spread_kernel,
        grid=(groups,),
        in_specs=[scalars(), left, left] + [fixed(right.shape) for right in rights],
        out_specs=[
            pl.BlockSpec((1, piece, columns), lambda g: (g, 0, 0)),
            fixed((piece, columns)),
        ],
        out_shape=[
            jax.ShapeDtypeStruct((groups, piece, columns), jnp.bfloat16),
            jax.ShapeDtypeStruct((piece, columns), jnp.float32),
        ],
        compiler_params=settings(44),
        cost_estimate=guess(0, 0),
        name="spread",
    )(place, own_left, other_left, *rights)


def pair_of(size):
    return [(spot, spot ^ 1) for spot in range(size)]


def shift_of(size, hops):
    groups = size // 2
    return [(spot, ((spot // 2 + hops) % groups) * 2 + spot % 2) for spot in range(size)]


def swap_pair(array, axis):
    return lax.ppermute(array, axis, pair_of(lax.axis_size(axis)))


def exchange_groups(sends):
    size = lax.axis_size("dp")
    groups = [[2 * group + side for group in range(size // 2)] for side in range(2)]
    return lax.all_to_all(sends, "dp", 0, 0, axis_index_groups=groups)


def finish(total, arrived):
    mine = lax.axis_index("dp") // 2
    for index in range(arrived.shape[0]):
        total = total + jnp.where(index == mine, 0.0, arrived[index].astype(jnp.float32))
    return total


def send_far(pieces):
    size = lax.axis_size("mp")
    return [
        lax.ppermute(piece, "mp", shift_of(size, hops + 1)) for hops, piece in enumerate(pieces)
    ]


def features_kernel(place, *refs, groups):
    hiddens, outs, gain_out = refs[:groups], refs[-1 - groups : -1], refs[-1]
    scale, small, w_gate, w_value, w_small = refs[-6 - groups : -1 - groups]
    parts = refs[groups : -6 - groups]
    width = parts[0].shape[1] // 2
    total = dot_lanes(small[...], w_small[...])
    for index, part in enumerate(parts):
        lanes = slice(index * width, (index + 1) * width)
        total = total + dot_lanes(part[:, :width], w_gate[:, lanes])
        total = total + dot_lanes(part[:, width:], w_value[:, lanes])
    gain_out[...] = jnp.zeros(gain_out.shape, jnp.float32)
    for index, hidden in enumerate(hiddens):

        @pl.when(pl.program_id(0) == index)
        def _():
            out = outs[index]
            out[...] = total
            for start in range(0, total.shape[1], LANES):
                lanes = slice(start, start + LANES)
                pulled = out[:, lanes] * hidden[:, lanes].astype(jnp.float32) * scale[...]
                gain_out[0, 0:1, lanes] = jnp.sum(pulled, axis=0, keepdims=True)


def back_features(place, hiddens, scale, parts, small, weights, groups):
    rows = small.shape[0]
    features = weights[0].shape[0]
    piece = features // (2 * groups)
    return pl.pallas_call(
        functools.partial(features_kernel, groups=groups),
        grid_spec=pltpu.PrefetchScalarGridSpec(
            num_scalar_prefetch=1,
            grid=(groups,),
            in_specs=[resident(array.shape) for array in (*hiddens, *parts, scale, small)]
            + [
                pl.BlockSpec(
                    (piece, array.shape[1]), lambda g, at: (2 * ((at[0] + g) % groups) + at[1], 0)
                )
                for array in weights
            ],
            out_specs=[resident((rows, piece))] * groups
            + [pl.BlockSpec((1, 8, piece), lambda g, at: (g, 0, 0))],
        ),
        out_shape=[jax.ShapeDtypeStruct((rows, piece), jnp.float32)] * groups
        + [jax.ShapeDtypeStruct((groups, 8, piece), jnp.float32)],
        compiler_params=settings(52),
        cost_estimate=guess(0, 0),
        name="features",
    )(place, *hiddens, *parts, scale, small, *weights)


def sum_all(values, axis):
    size = lax.axis_size(axis)
    step = 1
    while step < size:
        values = values + lax.ppermute(values, axis, [(spot, spot ^ step) for spot in range(size)])
        step *= 2
    return values


def pack_kernel(*refs, head_dim):
    stats, smalls, gains = refs[:PARTS], refs[PARTS : 2 * PARTS], refs[2 * PARTS + 1 : -1]
    select, out, count = refs[2 * PARTS], refs[-1], PARTS
    gain = gains[0][0:1, :]
    for piece in gains[1:]:
        gain = gain + piece[0:1, :]
    width = stats[0].shape[1]
    whole = width * count
    out[...] = jnp.zeros(out.shape, jnp.float32)
    small = smalls[0][...]
    for piece in smalls[1:]:
        small = small + piece[...]
    for index, piece in enumerate(stats):
        out[:8, index * width : (index + 1) * width] = piece[...]
    heads = jnp.zeros((8, LANES), jnp.float32)
    for start in range(0, whole, LANES):
        owner = (
            iota((LANES, LANES), 1) == (start + iota((LANES, LANES), 0)) // head_dim
        ).astype(jnp.float32)
        heads = heads + exact(out[:8, start : start + LANES], owner)
    out[8:16, : select.shape[1]] = select[...]
    out[16:18, :LANES] = small[:2, :]
    out[18:19, :LANES] = heads[CONV + 1 : CONV + 2, :]
    for start in range(0, gain.shape[1], LANES):
        out[19 + start // LANES : 20 + start // LANES, :LANES] = gain[:, start : start + LANES]


def run_pack(stats, smalls, select, gains, head_dim):
    whole = stats[0].shape[1] * len(stats)
    rows = -(-(19 + gains[0].shape[1] // LANES) // 8) * 8
    return pl.pallas_call(
        functools.partial(pack_kernel, head_dim=head_dim),
        out_shape=jax.ShapeDtypeStruct((rows, whole), jnp.float32),
        cost_estimate=guess(0, 0),
        name="pack",
    )(*stats, *smalls, select, *gains)


def unpack_kernel(*refs):
    arrived, outs = refs[:-9], refs[-9:]
    total = arrived[0][...]
    for piece in arrived[1:]:
        total = total + piece[...]
    taps, bias, select, select_bias, step, decay, skip, gate_gain, gain = outs
    taps[...] = total[:CONV, :]
    bias[...] = total[CONV : CONV + 1, :]
    gate_gain[...] = total[CONV + 2 : CONV + 3, :]
    select[...] = total[8 : 8 + CONV, : select.shape[1]]
    select_bias[...] = total[8 + CONV : 9 + CONV, : select.shape[1]]
    heads = step.shape[1]
    step[...] = total[16:17, :heads]
    decay[...] = total[17:18, :heads]
    skip[...] = total[18:19, :heads]
    for start in range(0, gain.shape[1], LANES):
        gain[:, start : start + LANES] = total[19 + start // LANES : 20 + start // LANES, :LANES]


def run_unpack(arrived, select_width, heads, gain_width):
    whole = arrived[0].shape[1]
    shapes = [(CONV, whole), (1, whole), (CONV, select_width), (1, select_width)]
    shapes += [(1, heads)] * 3 + [(1, whole), (1, gain_width)]
    return pl.pallas_call(
        unpack_kernel,
        out_shape=[jax.ShapeDtypeStruct(shape, jnp.float32) for shape in shapes],
        cost_estimate=guess(0, 0),
        name="unpack",
    )(*arrived)


def sum_tokens(values):
    size = lax.axis_size("dp")
    both = values + swap_pair(values, "dp")
    return [both] + [
        lax.ppermute(both, "dp", shift_of(size, hops)) for hops in range(1, size // 2)
    ]


def widen_lanes(vector):
    return jnp.pad(vector, (0, LANES - vector.shape[0]))[None, :]


def on_device(
    hidden_in,
    cotangent,
    span_starts,
    span_fill,
    norm_gain,
    w_gate,
    w_value,
    w_select,
    w_step,
    conv_value,
    conv_value_bias,
    conv_select,
    conv_select_bias,
    step_bias,
    decay_log,
    skip_gain,
    gate_gain,
    w_out,
):
    token_rows = hidden_in.shape[0]
    model_width = norm_gain.shape[0]
    inner_cols = w_gate.shape[1]
    local_heads = w_step.shape[1]
    head_dim = inner_cols // local_heads
    select_width = w_select.shape[1]
    model_parts = lax.axis_size("mp")
    model_groups = model_parts // 2
    data_parts = lax.axis_size("dp")
    inner_total = inner_cols * model_parts
    feature_piece = model_width // model_parts
    data_piece = model_width // data_parts
    part = select_width // model_parts
    model_spot = lax.axis_index("mp")
    model_side = model_spot % 2
    data_side = (lax.axis_index("dp") % 2).reshape(1)
    offset = model_spot * feature_piece
    select_start = model_spot * part

    def after(array, *others):
        return lax.optimization_barrier((array, *others))[0]

    def gather_far(block):
        return [
            lax.ppermute(block, "mp", shift_of(model_parts, hops)) for hops in range(1, model_groups)
        ]

    def gather_near(block, far, *others):
        blocks = [block, swap_pair(block, "mp")]
        for same in far:
            same = after(same, *others) if others else same
            blocks += [same, swap_pair(same, "mp")]
        return blocks

    def theirs(block):
        pieces = []
        for index in range(0, block.shape[1] // data_piece, 2):
            first = block[:, index * data_piece : (index + 1) * data_piece]
            second = block[:, (index + 1) * data_piece : (index + 2) * data_piece]
            pieces.append(jnp.where(data_side[0] == 0, second, first))
        return pieces

    gain_row = gate_gain[None, :]
    skip_row = widen_lanes(skip_gain)
    bias_step = widen_lanes(step_bias)
    decay_row = widen_lanes(decay_log)
    half_lanes = LANES // 2
    wide_step = jnp.pad(w_step, ((0, 0), (0, LANES - local_heads)))
    own_select = lax.dynamic_slice_in_dim(w_select, select_start, part, 1)
    w_small = jnp.concatenate(
        [
            jnp.pad(w_step, ((0, 0), (0, half_lanes - local_heads))),
            jnp.pad(own_select, ((0, 0), (0, half_lanes - part))),
        ],
        axis=1,
    )
    spots = []
    for hops in range(model_groups):
        group = (model_spot // 2 - hops) % model_groups
        spots += [2 * group + model_side, 2 * group + 1 - model_side]
    spots = jnp.stack(spots)

    place = (lax.axis_index("dp") // 2).reshape(1)
    model_place = jnp.stack([model_spot // 2, model_side])
    other_place = jnp.stack([model_spot // 2, 1 - model_side])
    vectors = (conv_value, conv_value_bias[None, :])
    head_vectors = (bias_step, decay_row, skip_row)

    far_in = gather_far(hidden_in)
    cross = swap_pair(jnp.concatenate(theirs(hidden_in) + theirs(cotangent), axis=1), "dp")
    blocks_in = gather_near(hidden_in, far_in)
    combined = after(jnp.concatenate([cotangent, cross], axis=1), *far_in)
    far_up = gather_far(combined)

    (
        normed_own,
        scale_rows,
        scale_columns,
        value_pre,
        gate_pre,
        select_pre,
        step_pre,
        values,
        selects,
        scan,
        gated,
        delta,
        sums,
        states,
        square_part,
    ) = run_forward(
        data_side,
        spots,
        span_starts,
        span_fill,
        [after(blocks_in[0], cross)] + blocks_in[1:],
        norm_gain[None, :],
        (w_value, w_gate, w_select, wide_step),
        vectors + (conv_select, conv_select_bias[None, :]) + head_vectors,
        data_piece,
    )
    other_rows = swap_pair(scale_rows, "dp")
    blocks_up = gather_near(combined, far_up, square_part)
    squares = after(sum_all(square_part, "mp"), other_rows)
    scaled = run_scale(gated, squares, gain_row, inner_total)
    scaled_other = swap_pair(scaled, "dp")
    grad_scaled, product_part, up_own, normed_other, up_other = run_cotangent(
        data_side,
        spots,
        other_rows,
        norm_gain,
        gain_row,
        w_out,
        gated,
        blocks_up,
        data_piece,
    )
    products = sum_all(product_part, "mp")

    def backward(index, products, previous):
        return run_backward(
            span_starts,
            span_fill,
            (gate_pre, grad_scaled, scan, values, value_pre, selects, delta, sums, step_pre),
            (squares, products),
            states,
            vectors + (gain_row,) + head_vectors,
            model_parts,
            index,
            model_place,
            previous,
            inner_total,
        )

    parts, others, stats, smalls, steps, row_dots = [], [], [], [], [], []
    own_parts, out_parts = [], []
    previous = None
    gate = products
    last_other, last_out = scaled_other, None
    for index in range(PARTS):
        part_grads, *previous, step, rows, stat, small = backward(index, gate, previous)
        if index == 0:
            lefts, right = (up_own, up_other), scaled
        else:
            lefts, right = (normed_own, normed_other), parts[index - 1]
        if index == 1:
            mixed = run_mixed(model_place, after(scaled, sends), w_out, model_groups)
            mixed_theirs, mixed_ours = mixed[:model_groups], mixed[model_groups:]
            arrived = after(last_other, part_grads, mixed_theirs[0])
        else:
            arrived = after(last_other, part_grads)
        last_other = swap_pair(after(part_grads, arrived), "dp")
        sends, own = run_spread(place, *lefts, right, arrived)
        sends = sends if last_out is None else after(sends, last_out)
        last_out = exchange_groups(sends)
        own_parts.append(own)
        out_parts.append(last_out)
        gate = after(products, sends)
        parts.append(part_grads)
        others.append(last_other)
        steps.append(step)
        row_dots.append(rows)
        stats.append(stat)
        smalls.append(small)
    own_out, out_out = own_parts.pop(0), out_parts.pop(0)

    came = swap_pair(after(previous[0], others[-2]), "mp")
    mixed_came = [swap_pair(after(piece, parts[1]), "mp") for piece in mixed_theirs]
    came = after(came, sends)
    select_total, *select_pieces = run_pair(
        [previous[1][index] for index in range(model_groups)],
        [came[index] for index in range(model_groups)],
        jnp.float32,
    )
    select_arrived = send_far(select_pieces)
    mixed_total, *mixed_pieces = run_pair(
        mixed_ours, [after(mixed_came[0], *select_arrived, others[-1])] + mixed_came[1:], jnp.float32
    )
    mixed_arrived = send_far(mixed_pieces)
    small_low, select_rows, select_stats = run_select(
        span_starts,
        model_spot.reshape(1),
        [select_total] + select_arrived,
        select_pre,
        conv_select,
        conv_select_bias[None, :],
        steps,
    )
    select_sums = sum_all(select_stats, "mp")
    row_total = select_rows
    for rows in row_dots:
        row_total = row_total + rows
    norm_rows = sum_all(row_total, "mp")
    weights = (w_gate, w_value, w_small)
    hiddens = [
        [blocks_in[2 * ((model_groups - group) % model_groups) + side] for group in range(model_groups)]
        for side in range(2)
    ]
    small_other = swap_pair(after(small_low, others[-1]), "dp")
    sends_last, own_last = run_spread(
        place, normed_own, normed_other, parts[-1], others[-1], small_low, small_other
    )
    out_last = exchange_groups(after(sends_last, last_out))
    *back_theirs, gain_theirs = back_features(
        other_place,
        hiddens[1],
        scale_columns,
        parts,
        after(small_low, sends_last, *mixed_pieces),
        weights,
        model_groups,
    )
    back_came = [swap_pair(piece, "mp") for piece in back_theirs]
    *back_ours, gain_ours = back_features(
        model_place,
        hiddens[0],
        scale_columns,
        parts,
        after(small_low, back_theirs[0]),
        weights,
        model_groups,
    )
    back_total, *back_pieces = run_pair(
        back_ours, [after(back_came[0], *mixed_arrived)] + back_came[1:], jnp.bfloat16
    )
    gain_both = gain_ours + swap_pair(gain_theirs, "mp")
    gain_sums = [gain_both[0]] + send_far([gain_both[hops] for hops in range(1, model_groups)])
    back_pieces = [after(piece, *gain_sums, select_sums, norm_rows) for piece in back_pieces]
    back_arrived = send_far(back_pieces)
    own_parts.append(own_last)
    out_parts.append(out_last)
    for index in range(PARTS):
        out_parts[index] = after(out_parts[index], *back_pieces)
    out_out = after(out_out, *back_pieces)

    grad_normed = back_total
    for piece in back_arrived:
        grad_normed = grad_normed + piece.astype(jnp.float32)
    own_in = hidden_in.astype(jnp.float32)
    mixed_share = mixed_total
    for piece in mixed_arrived:
        mixed_share = mixed_share + piece
    output = (own_in + mixed_share).astype(jnp.bfloat16)
    own_gain = lax.dynamic_slice_in_dim(norm_gain, offset, feature_piece, 0)
    own_scale = scale_columns[:, :1]
    weighted_in = grad_normed * own_gain[None, :]
    grad_hidden_in = (
        cotangent.astype(jnp.float32)
        + weighted_in * own_scale
        - own_in * own_scale**2 * norm_rows[0][:, None] / model_width
    )
    packed = run_pack(stats, smalls, select_sums, gain_sums, head_dim)
    (
        grad_taps,
        grad_bias,
        grad_select_taps,
        grad_select_bias,
        grad_step_bias,
        grad_decay_log,
        grad_skip_gain,
        grad_gate_gain,
        gain_sum,
    ) = run_unpack(sum_tokens(after(packed, *back_pieces)), select_width, local_heads, feature_piece)

    grad_w_out = finish(own_out, out_out).T
    done = [finish(own, out) for own, out in zip(own_parts, out_parts)]
    width = inner_cols // PARTS
    grad_w_gate = jnp.concatenate([piece[:, :width] for piece in done], axis=1)
    grad_w_value = jnp.concatenate([piece[:, width : 2 * width] for piece in done], axis=1)
    grad_w_small = done[-1][:, 2 * width :]
    grad_w_step = grad_w_small[:, :local_heads]
    grad_w_select = lax.all_gather(
        grad_w_small[:, half_lanes : half_lanes + part], "mp", axis=1, tiled=True
    )
    return (
        output,
        grad_hidden_in,
        gain_sum[0],
        grad_w_gate,
        grad_w_value,
        grad_w_select,
        grad_w_step,
        grad_taps,
        grad_bias[0],
        grad_select_taps,
        grad_select_bias[0],
        grad_step_bias[0],
        grad_decay_log[0],
        grad_skip_gain[0],
        grad_gate_gain[0],
        grad_w_out,
    )


def solution(mesh):
    in_specs = (
        P("dp", "mp"),
        P("dp", "mp"),
        P("dp"),
        P("dp"),
        P(),
        P(None, "mp"),
        P(None, "mp"),
        P(),
        P(None, "mp"),
        P(None, "mp"),
        P("mp"),
        P(),
        P(),
        P("mp"),
        P("mp"),
        P("mp"),
        P("mp"),
        P("mp", None),
    )
    out_specs = (
        P("dp", "mp"),
        P("dp", "mp"),
        P("mp"),
        P("dp", "mp"),
        P("dp", "mp"),
        P("dp", None),
        P("dp", "mp"),
        P(None, "mp"),
        P("mp"),
        P(),
        P(),
        P("mp"),
        P("mp"),
        P("mp"),
        P("mp"),
        P("mp", "dp"),
    )
    return jax.shard_map(
        on_device, mesh=mesh, in_specs=in_specs, out_specs=out_specs, check_vma=False
    )
```

```python
import functools

import jax
import jax.numpy as jnp
from jax import lax
from jax.experimental import pallas as pl
from jax.experimental.pallas import tpu as pltpu
from jax.sharding import PartitionSpec as P

CONV = 4
SPAN = 256
LANES = 128
EXTRA = 8
TOP = 15.0
FAR = -1e30
PARTS = 2
epsilon = 1e-05
exact_mode = lax.Precision.HIGHEST


def settings(mebibytes, axes=1):
    return pltpu.CompilerParams(
        dimension_semantics=("arbitrary",) * axes, vmem_limit_bytes=mebibytes << 20
    )


def scalars():
    return pl.BlockSpec(memory_space=pltpu.SMEM)


def fixed(shape):
    return pl.BlockSpec(shape, lambda *_: (0,) * len(shape))


def split_bits(value):
    high = value.astype(jnp.bfloat16)
    low = (value - high.astype(jnp.float32)).astype(jnp.bfloat16)
    return high, low


def dot(left, right):
    return lax.dot_general(left, right, (((1,), (0,)), ((), ())), preferred_element_type=jnp.float32)


def dot_lanes(left, right):
    return lax.dot_general(left, right, (((1,), (1,)), ((), ())), preferred_element_type=jnp.float32)


def dot_rows(left, right):
    return lax.dot_general(left, right, (((0,), (0,)), ((), ())), preferred_element_type=jnp.float32)


def exact(left, right):
    return jnp.dot(left, right, precision=exact_mode, preferred_element_type=jnp.float32)


def beside(*pieces):
    return jnp.concatenate(pieces, axis=1)


def above(*pieces):
    return jnp.concatenate(pieces, axis=0)


def sigmoid(value):
    return 1.0 / (1.0 + jnp.exp(-value))


def iota(shape, axis):
    return lax.broadcasted_iota(jnp.int32, shape, axis)


def two_heads(columns, pair, in_first):
    first = columns[:, 2 * pair : 2 * pair + 1]
    second = columns[:, 2 * pair + 1 : 2 * pair + 2]
    return jnp.where(in_first, first, second)


def row_of(columns):
    return jnp.sum(jnp.transpose(columns), axis=0, keepdims=True)


def live_rows(fill, width):
    return (iota((SPAN, width), 0) < fill).astype(jnp.float32)


def wide_lanes(start, width):
    return pl.ds(pl.multiple_of(start * width, min(width, LANES)), width)


def store_ours(side, block, spot, ours_out, piece):
    for index in range(block.shape[1] // (2 * piece)):
        first = block[:, 2 * index * piece : (2 * index + 1) * piece]
        second = block[:, (2 * index + 1) * piece : (2 * index + 2) * piece]
        group = spot * (block.shape[1] // (2 * piece)) + index
        ours_out[pl.ds(group, 1)] = jnp.where(side == 0, first, second)[None]


def guess(flops, moved, exps=0):
    return pl.CostEstimate(flops=1, bytes_accessed=1, transcendentals=0)


def conv_of(extended, kernel, bias, lanes):
    total = bias[:, lanes]
    for back in range(CONV):
        tap = kernel[CONV - 1 - back : CONV - back, lanes]
        total = total + tap * extended[EXTRA - back : EXTRA - back + SPAN, lanes]
    return total


def forward_kernel(
    side,
    spots,
    starts,
    fills,
    norm_gain,
    w_value,
    w_gate,
    w_select,
    w_step,
    conv_value,
    conv_value_bias,
    conv_select,
    conv_select_bias,
    step_bias,
    decay_log,
    skip,
    *refs,
    piece,
):
    blocks = refs[:-19]
    (
        ours_out,
        scale_out,
        scale_columns_out,
        value_pre,
        gate_pre,
        select_pre,
        step_pre,
        values_out,
        selects_out,
        scan_out,
        gated_out,
        delta_out,
        sum_out,
        state_out,
        rows_out,
        extended,
        extended_select,
        state,
        whole,
    ) = refs[-19:]
    step = pl.program_id(0)
    fresh = starts[step] == 1
    width = value_pre.shape[1]
    state_dim = select_pre.shape[1] // 2

    part_width = blocks[0].shape[1]
    total = jnp.zeros((SPAN, LANES), jnp.float32)
    for block in blocks:
        for start in range(0, part_width, LANES):
            part = block[:, start : start + LANES].astype(jnp.float32)
            total = total + part * part
    mean = jnp.sum(total, axis=1, keepdims=True) / (part_width * len(blocks))
    scale = lax.rsqrt(mean + epsilon)
    scale_columns_out[...] = jnp.broadcast_to(scale, (SPAN, LANES))
    scale_out[...] = jnp.transpose(scale_columns_out[...])[:1, :]
    for index, block in enumerate(blocks):
        spot = spots[index]
        window = wide_lanes(spot, part_width)
        own_gain = norm_gain[:, window]
        normed = (block[...].astype(jnp.float32) * scale * own_gain).astype(jnp.bfloat16)
        store_ours(side[0], normed, spot, ours_out, piece)
        whole[:, window] = normed
    for out, weights in (
        (select_pre, w_select),
        (step_pre, w_step),
        (value_pre, w_value),
        (gate_pre, w_gate),
    ):
        out[...] = dot(whole[...], weights[...])

    @pl.when(fresh)
    def _():
        extended[:EXTRA, :] = jnp.zeros((EXTRA, width), jnp.float32)
        extended_select[:EXTRA, :] = jnp.zeros((EXTRA, 2 * state_dim), jnp.float32)
        state[...] = jnp.zeros(state.shape, jnp.float32)

    @pl.when(jnp.logical_not(fresh))
    def _():
        extended[:EXTRA, :] = extended[SPAN:, :]
        extended_select[:EXTRA, :] = extended_select[SPAN:, :]

    extended[EXTRA:, :] = value_pre[...]
    extended_select[EXTRA:, :] = select_pre[...]
    state_out[0] = state[...]

    live = live_rows(fills[step], LANES)
    pre_step = step_pre[...] + step_bias[...]
    delta = live * (jnp.maximum(pre_step, 0.0) + jnp.log1p(jnp.exp(-jnp.abs(pre_step))))
    rate = -jnp.exp(decay_log[...])
    lower = (iota((SPAN, SPAN), 0) >= iota((SPAN, SPAN), 1)).astype(jnp.float32)
    cumulative = exact(lower, delta * rate)
    delta_out[...] = delta
    sum_out[...] = cumulative
    sums_across = jnp.transpose(cumulative)
    delta_across = jnp.transpose(delta)
    grown = jnp.exp(cumulative)
    tail = delta * jnp.exp(cumulative[SPAN - 1 : SPAN, :] - cumulative)

    halves = []
    for half in range(2):
        lanes = slice(half * state_dim, (half + 1) * state_dim)
        mixed = conv_of(extended_select, conv_select, conv_select_bias, lanes)
        chosen = (mixed * sigmoid(mixed)).astype(jnp.bfloat16)
        selects_out[:, lanes] = chosen
        halves.append(chosen)
    inflow, readout = halves
    inflow_across = jnp.transpose(inflow.astype(jnp.float32)).astype(jnp.bfloat16)
    scores = dot_lanes(readout, inflow)
    middle = SPAN // 2
    past = iota((middle, middle), 0) >= iota((middle, middle), 1)
    later_past = iota((middle, SPAN), 0) + middle >= iota((middle, SPAN), 1)
    in_first = iota((SPAN, LANES), 1) < LANES // 2
    row_first = iota((1, LANES), 1) < LANES // 2
    readout_twice = beside(readout, readout)
    squares = jnp.zeros((SPAN, LANES), jnp.float32)
    for pair in range(width // LANES):
        lanes = slice(pair * LANES, (pair + 1) * LANES)
        mixed = conv_of(extended, conv_value, conv_value_bias, lanes)
        value_low = (mixed * sigmoid(mixed)).astype(jnp.bfloat16)
        values_out[:, lanes] = value_low
        value = value_low.astype(jnp.float32)
        entering = state[:, lanes]
        scan = dot(readout_twice, above(*split_bits(entering))) * two_heads(grown, pair, in_first)
        scan = scan + two_heads(skip[...], pair, row_first) * value
        for which in range(2):
            head = 2 * pair + which
            own = jnp.where(in_first == (which == 0), value_low, jnp.zeros_like(value_low))
            sums_row = sums_across[head : head + 1, :]
            delta_row = delta_across[head : head + 1, :]
            gaps = cumulative[:middle, head : head + 1] - sums_row[:, :middle]
            weights = jnp.exp(jnp.where(past, gaps, FAR))
            high, low = split_bits(scores[:middle, :middle] * weights * delta_row[:, :middle])
            early = dot(high, own[:middle]) + dot(low, own[:middle])
            gaps = cumulative[middle:, head : head + 1] - sums_row
            weights = jnp.exp(jnp.where(later_past, gaps, FAR))
            high, low = split_bits(scores[middle:] * weights * delta_row)
            scan = scan + above(early, dot(high, own) + dot(low, own))
        scan_out[:, lanes] = scan
        gate = gate_pre[:, lanes]
        gated = live * scan * gate * sigmoid(gate)
        squares = squares + gated * gated
        gated_out[:, lanes] = gated
        weighted = value * two_heads(tail, pair, in_first)
        high, low = split_bits(weighted)
        last = two_heads(grown[SPAN - 1 : SPAN, :], pair, row_first)
        state[:, lanes] = entering * last + dot(inflow_across, high) + dot(inflow_across, low)
    rows_out[...] = row_of(squares)


def resident(shape):
    return pl.BlockSpec(shape, lambda *_: (0,) * len(shape), pipeline_mode=pl.Buffered(1))


def run_forward(side, spots, starts, fills, blocks, gain, weights, vectors, piece):
    rows, part_width = blocks[0].shape
    groups = part_width * len(blocks) // (2 * piece)
    w_value, w_gate, w_select, w_step = weights
    width = w_value.shape[1]
    spans = rows // SPAN
    select_width = w_select.shape[1]

    def tile(columns):
        return pl.BlockSpec((SPAN, columns), lambda i: (i, 0))

    def like(columns, dtype):
        return jax.ShapeDtypeStruct((rows, columns), dtype)

    strip = pl.BlockSpec((1, SPAN), lambda i: (0, i))
    return pl.pallas_call(
        functools.partial(forward_kernel, piece=piece),
        grid=(spans,),
        in_specs=[scalars()] * 4
        + [fixed(gain.shape)]
        + [resident(array.shape) for array in weights]
        + [fixed(array.shape) for array in vectors]
        + [tile(part_width)] * len(blocks),
        out_specs=[
            pl.BlockSpec((groups, SPAN, piece), lambda i: (0, i, 0)),
            strip,
            tile(LANES),
            tile(width),
            tile(width),
            tile(select_width),
            tile(LANES),
            tile(width),
            tile(select_width),
            tile(width),
            tile(width),
            tile(LANES),
            tile(LANES),
            pl.BlockSpec((1, select_width // 2, width), lambda i: (i, 0, 0)),
            strip,
        ],
        out_shape=[
            jax.ShapeDtypeStruct((groups, rows, piece), jnp.bfloat16),
            jax.ShapeDtypeStruct((1, rows), jnp.float32),
            like(LANES, jnp.float32),
            like(width, jnp.float32),
            like(width, jnp.float32),
            like(select_width, jnp.float32),
            like(LANES, jnp.float32),
            like(width, jnp.bfloat16),
            like(select_width, jnp.bfloat16),
            like(width, jnp.float32),
            like(width, jnp.float32),
            like(LANES, jnp.float32),
            like(LANES, jnp.float32),
            jax.ShapeDtypeStruct((spans, select_width // 2, width), jnp.float32),
            jax.ShapeDtypeStruct((1, rows), jnp.float32),
        ],
        scratch_shapes=[
            pltpu.VMEM((SPAN + EXTRA, width), jnp.float32),
            pltpu.VMEM((SPAN + EXTRA, select_width), jnp.float32),
            pltpu.VMEM((select_width // 2, width), jnp.float32),
            pltpu.VMEM((SPAN, part_width * len(blocks)), jnp.bfloat16),
        ],
        compiler_params=settings(50),
        cost_estimate=guess(0, 0),
        name="forward",
    )(side, spots, starts, fills, gain, *weights, *vectors, *blocks)


def scale_column(rows, total_width):
    turned = jnp.transpose(above(rows[...], jnp.zeros((LANES - 1, SPAN), jnp.float32)))
    return lax.rsqrt(turned[:, 0:1] / total_width + epsilon)


def scale_kernel(gated_in, squares, gain, scaled_out, *, total_width):
    width = gated_in.shape[1]
    scale = jnp.broadcast_to(scale_column(squares, total_width), (SPAN, LANES))
    for start in range(0, width, LANES):
        lanes = slice(start, start + LANES)
        scaled_out[:, lanes] = (gated_in[:, lanes] * scale * gain[:, lanes]).astype(jnp.bfloat16)


def run_scale(gated, squares, gain, total_width):
    rows, width = gated.shape
    return pl.pallas_call(
        functools.partial(scale_kernel, total_width=total_width),
        grid=(rows // SPAN,),
        in_specs=[
            pl.BlockSpec((SPAN, width), lambda i: (i, 0)),
            pl.BlockSpec((1, SPAN), lambda i: (0, i)),
            fixed((1, width)),
        ],
        out_specs=pl.BlockSpec((SPAN, width), lambda i: (i, 0)),
        out_shape=jax.ShapeDtypeStruct((rows, width), jnp.bfloat16),
        compiler_params=settings(32),
        cost_estimate=guess(6 * rows * width, 6 * rows * width),
        name="scale",
    )(gated, squares, gain)


def cotangent_kernel(
    side, spots, rows, norm_gain, gain, w_out, gated_in, *refs, piece
):
    blocks = refs[:-5]
    grad_out, rows_out, ours_out, other_normed_out, other_out = refs[-5:]
    width = blocks[0].shape[1] // 2
    cross = width // 2
    turned = jnp.transpose(above(rows[...], jnp.zeros((LANES - 1, SPAN), jnp.float32)))
    scale = turned[:, 0:1]
    each = cross // piece
    total = None
    for index, block in enumerate(blocks):
        spot = spots[index]
        upstream = block[:, :width]
        product = dot_lanes(upstream, w_out[:, wide_lanes(spot, width)])
        total = product if index == 0 else total + product
        store_ours(side[0], upstream, spot, ours_out, piece)
        for inner in range(each):
            group = spot * each + inner
            own_gain = norm_gain[pl.ds(2 * group + side[0], 1), :]
            start = width + inner * piece
            hidden = block[:, start : start + piece].astype(jnp.float32)
            other_normed_out[pl.ds(group, 1)] = (hidden * scale * own_gain).astype(jnp.bfloat16)[None]
            start = width + cross + inner * piece
            other_out[pl.ds(group, 1)] = block[:, start : start + piece][None]
    grad_out[...] = total
    products = jnp.zeros((SPAN, LANES), jnp.float32)
    for start in range(0, gated_in.shape[1], LANES):
        lanes = slice(start, start + LANES)
        products = products + grad_out[:, lanes] * gain[:, lanes] * gated_in[:, lanes]
    rows_out[...] = row_of(products)


def run_cotangent(side, spots, rows_in, norm_gain, gain, w_out, gated, blocks, piece):
    rows, width = gated.shape
    features = w_out.shape[1]
    groups = features // (2 * piece)
    strip = pl.BlockSpec((1, SPAN), lambda i: (0, i))

    def tile(columns):
        return pl.BlockSpec((SPAN, columns), lambda i: (i, 0))

    pieces = pl.BlockSpec((groups, SPAN, piece), lambda i: (0, i, 0))
    pieces_shape = jax.ShapeDtypeStruct((groups, rows, piece), jnp.bfloat16)
    return pl.pallas_call(
        functools.partial(cotangent_kernel, piece=piece),
        grid=(rows // SPAN,),
        in_specs=[
            scalars(),
            scalars(),
            strip,
            fixed((2 * groups, piece)),
            fixed(gain.shape),
            resident(w_out.shape),
            tile(width),
        ]
        + [tile(block.shape[1]) for block in blocks],
        out_specs=[tile(width), strip, pieces, pieces, pieces],
        out_shape=[
            jax.ShapeDtypeStruct((rows, width), jnp.float32),
            jax.ShapeDtypeStruct((1, rows), jnp.float32),
            pieces_shape,
            pieces_shape,
            pieces_shape,
        ],
        compiler_params=settings(48),
        cost_estimate=guess(0, 0),
        name="cotangent",
    )(
        side,
        spots,
        rows_in,
        norm_gain.reshape(2 * groups, piece),
        gain,
        w_out,
        gated,
        *blocks,
    )


def mixed_kernel(place, scaled, w_out, *outs):
    product = dot(scaled[...], w_out[...])
    for index, out in enumerate(outs):

        @pl.when(pl.program_id(0) == index)
        def _():
            out[...] = product


def run_mixed(place, scaled, w_out, groups):
    rows, width = scaled.shape
    piece = w_out.shape[1] // (2 * groups)

    def column(g, at):
        side = jnp.where(g < groups, 1 - at[1], at[1])
        return 0, 2 * ((at[0] + g) % groups) + side

    return pl.pallas_call(
        mixed_kernel,
        grid_spec=pltpu.PrefetchScalarGridSpec(
            num_scalar_prefetch=1,
            grid=(2 * groups,),
            in_specs=[resident((rows, width)), pl.BlockSpec((width, piece), column)],
            out_specs=[resident((rows, piece))] * (2 * groups),
        ),
        out_shape=[jax.ShapeDtypeStruct((rows, piece), jnp.float32)] * (2 * groups),
        compiler_params=settings(40),
        cost_estimate=guess(0, 0),
        name="mixed",
    )(place, scaled, w_out)


def backward_kernel(
    starts,
    fills,
    gate_pre,
    grad_scaled,
    scan_in,
    values_in,
    value_pre,
    value_before,
    selects_in,
    delta_in,
    sum_in,
    step_pre,
    state_in,
    conv_value,
    conv_value_bias,
    gain,
    squares,
    products,
    step_bias,
    decay_log,
    skip,
    model_place,
    *rest,
    spans,
    first_head,
    adds,
    total_width,
    shared_groups,
):
    groups = shared_groups
    if adds:
        before, rest = rest[: 2 * groups], rest[2 * groups :]
    value_out, shared_outs, rest = rest[0], rest[1 : 1 + 2 * groups], rest[1 + 2 * groups :]
    (
        step_out,
        rows_out,
        stat_out,
        small_out,
        extended,
        shifted,
        state,
        carried,
    ) = rest
    step = pl.program_id(0)
    span = spans - 1 - step
    width = values_in.shape[1]
    state_dim = selects_in.shape[1] // 2
    following = jnp.minimum(span + 1, spans - 1)
    joined = jnp.logical_and(step > 0, starts[following] == 0)

    @pl.when(jnp.logical_not(joined))
    def _():
        shifted[SPAN:, :] = jnp.zeros((EXTRA, width), jnp.float32)
        state[...] = jnp.zeros(state.shape, jnp.float32)
        carried[...] = jnp.zeros(carried.shape, jnp.float32)

    @pl.when(joined)
    def _():
        shifted[SPAN:, :] = shifted[:EXTRA, :]

    @pl.when(step == 0)
    def _():
        stat_out[...] = jnp.zeros(stat_out.shape, jnp.float32)
        small_out[...] = jnp.zeros(small_out.shape, jnp.float32)

    fresh = starts[span] == 1

    @pl.when(fresh)
    def _():
        extended[:EXTRA, :] = jnp.zeros((EXTRA, width), jnp.float32)

    @pl.when(jnp.logical_not(fresh))
    def _():
        extended[:EXTRA, :] = value_before[...]

    extended[EXTRA:, :] = value_pre[...]

    delta = delta_in[...]
    cumulative = sum_in[...]
    sums_across = jnp.transpose(cumulative)
    grown = jnp.exp(cumulative)
    tail = jnp.exp(cumulative[SPAN - 1 : SPAN, :] - cumulative)
    delta_tail = delta * tail
    inflow = selects_in[:, :state_dim]
    readout = selects_in[:, state_dim:]
    readout_across = jnp.transpose(readout.astype(jnp.float32)).astype(jnp.bfloat16)
    scores = dot_lanes(inflow, readout)
    ahead = iota((SPAN, SPAN), 1) >= iota((SPAN, SPAN), 0)
    in_first = iota((SPAN, LANES), 1) < LANES // 2
    row_first = iota((1, LANES), 1) < LANES // 2
    live = live_rows(fills[span], LANES)
    turned = jnp.transpose(above(products[...], jnp.zeros((LANES - 1, SPAN), jnp.float32)))
    norm_scale = scale_column(squares, total_width)
    norm_pull = norm_scale * norm_scale * norm_scale * turned[:, 0:1] / total_width
    norm_scale = jnp.broadcast_to(norm_scale, (SPAN, LANES))
    norm_pull = jnp.broadcast_to(norm_pull, (SPAN, LANES))
    inflow_twice = beside(inflow, inflow)
    grad_scores = jnp.zeros((SPAN, SPAN), jnp.float32)
    grad_inflow = jnp.zeros((SPAN, state_dim), jnp.float32)
    grad_readout = jnp.zeros((SPAN, state_dim), jnp.float32)
    change = jnp.zeros((SPAN, LANES), jnp.float32)
    direct = jnp.zeros((SPAN, LANES), jnp.float32)
    jump = jnp.zeros((8, LANES), jnp.float32)
    dots = jnp.zeros((SPAN, LANES), jnp.float32)
    for own_pair in range(width // LANES):
        lanes = slice(own_pair * LANES, (own_pair + 1) * LANES)
        pair = first_head // 2 + own_pair
        gate = gate_pre[:, lanes]
        scan = scan_in[:, lanes]
        before_norm = grad_scaled[:, lanes]
        own_gain = gain[:, lanes]
        sig = sigmoid(gate)
        opened = live * gate * sig
        gated = scan * opened
        grad_gated = before_norm * own_gain * norm_scale - gated * norm_pull
        grad_gate = grad_gated * live * scan * sig * (1.0 + gate * (1.0 - sig))
        gate_low = grad_gate.astype(jnp.bfloat16)
        value_out[:, lanes] = gate_low
        dots = dots + gate_low.astype(jnp.float32) * gate
        stat_out[CONV + 2 : CONV + 3, lanes] += jnp.sum(
            before_norm * gated * norm_scale, axis=0, keepdims=True
        )
        upstream = grad_gated * opened
        up_high, up_low = split_bits(upstream)
        value_low = values_in[:, lanes]
        value = value_low.astype(jnp.float32)
        own_skip = two_heads(skip[...], pair, row_first)
        arriving = state[:, lanes]
        arriving_high, arriving_low = split_bits(arriving)
        entering = state_in[0, :, lanes]
        entering_high, entering_low = split_bits(entering)
        pulled = dot(inflow_twice, above(arriving_high, arriving_low)) * two_heads(tail, pair, in_first)
        up_both = beside(up_high, up_low)
        for which in range(2):
            head = 2 * pair + which
            mine = in_first == (which == 0)
            nothing = jnp.zeros_like(value_low)
            gaps = sums_across[head : head + 1, :] - cumulative[:, head : head + 1]
            weights = jnp.exp(jnp.where(ahead, gaps, FAR))
            high, low = split_bits(scores * weights)
            own_high = jnp.where(mine, up_high, nothing)
            own_low = jnp.where(mine, up_low, nothing)
            pulled = pulled + dot(high, own_high) + dot(high, own_low) + dot(low, own_high)
            own_value = jnp.where(mine, value_low, nothing)
            outer = dot_lanes(beside(own_value, own_value), up_both)
            grad_scores = grad_scores + outer * weights * delta[:, head : head + 1]
        delta_both = two_heads(delta, pair, in_first)
        grad_value = own_skip * upstream + delta_both * pulled
        pull_value = value * pulled
        spread = (
            iota((LANES, LANES), 1) == 2 * pair + iota((LANES, LANES), 0) // (LANES // 2)
        ).astype(jnp.bfloat16)
        spread_twice = above(spread, spread)
        moved = upstream * (scan - own_skip * value) - delta_both * pull_value
        change = change + dot(beside(*split_bits(moved)), spread_twice)
        direct = direct + dot(beside(*split_bits(pull_value)), spread_twice)
        grown_up = upstream * two_heads(grown, pair, in_first)
        high, low = split_bits(grown_up)
        grad_readout = grad_readout + dot_lanes(
            beside(high, low, high), beside(entering_high, entering_high, entering_low)
        )
        last = two_heads(grown[SPAN - 1 : SPAN, :], pair, row_first)
        leaving = arriving * last + dot(readout_across, high) + dot(readout_across, low)
        tail_value = value * two_heads(delta_tail, pair, in_first)
        high, low = split_bits(tail_value)
        grad_inflow = grad_inflow + dot_lanes(
            beside(high, low, high), beside(arriving_high, arriving_high, arriving_low)
        )
        jump = jump + exact(carried[:, lanes], spread.astype(jnp.float32))
        state[:, lanes] = leaving
        carried[:, lanes] = jnp.broadcast_to(
            jnp.sum(leaving * entering, axis=0, keepdims=True), (8, LANES)
        )
        mixed = conv_of(extended, conv_value, conv_value_bias, lanes)
        sig = sigmoid(mixed)
        inner = grad_value * sig * (1.0 + mixed * (1.0 - sig))
        shifted[:SPAN, lanes] = inner
        grad_pre = jnp.zeros((SPAN, LANES), jnp.float32)
        for back in range(CONV):
            tap = conv_value[CONV - 1 - back : CONV - back, lanes]
            grad_pre = grad_pre + tap * shifted[back : back + SPAN, lanes]
            stat_out[CONV - 1 - back : CONV - back, lanes] += jnp.sum(
                inner * extended[EXTRA - back : EXTRA - back + SPAN, lanes], axis=0, keepdims=True
            )
        stat_out[CONV : CONV + 1, lanes] += jnp.sum(inner, axis=0, keepdims=True)
        stat_out[CONV + 1 : CONV + 2, lanes] += jnp.sum(value * upstream, axis=0, keepdims=True)
        grad_low = grad_pre.astype(jnp.bfloat16)
        value_out[:, width + own_pair * LANES : width + (own_pair + 1) * LANES] = grad_low
        wide = grad_low.astype(jnp.float32)
        dots = dots + wide * extended[EXTRA:, lanes]
    high, low = split_bits(grad_scores)
    grad_inflow = grad_inflow + dot(high, readout) + dot(low, readout)
    high, low = split_bits(jnp.transpose(grad_scores))
    grad_readout = grad_readout + dot(high, inflow) + dot(low, inflow)
    part = 2 * state_dim // (2 * groups)
    folds = LANES // part
    height = SPAN // folds
    both = (grad_inflow, grad_readout)
    for hops in range(groups):
        for side in range(2):
            chosen = None
            for index in range(2 * groups):
                start = index * part
                piece = both[start // state_dim][:, start % state_dim : start % state_dim + part]
                here = jnp.logical_and(
                    lax.rem(model_place[0] + hops, groups) == index // 2,
                    jnp.where(model_place[1] == index % 2, 1, 0) == side,
                )
                chosen = piece if chosen is None else jnp.where(here, piece, chosen)
            chosen = beside(*[chosen[fold * height : (fold + 1) * height] for fold in range(folds)])
            at = side * groups + hops
            shared_outs[at][...] = chosen + before[at][...] if adds else chosen
    upper = (iota((SPAN, SPAN), 1) >= iota((SPAN, SPAN), 0)).astype(jnp.float32)
    flow = exact(upper, change) + jump[0:1, :]
    rate = -jnp.exp(decay_log[...])
    grad_delta = direct + rate * flow
    pre_step = step_pre[...]
    grad_step = grad_delta * live * sigmoid(pre_step + step_bias[...])
    column = iota((SPAN, LANES), 1)
    last_head = first_head + width // (LANES // 2)
    grad_step = jnp.where(jnp.logical_and(column >= first_head, column < last_head), grad_step, 0.0)
    step_low = grad_step.astype(jnp.bfloat16)
    step_out[...] = step_low
    wide = step_low.astype(jnp.float32)
    dots = dots + wide * pre_step
    small_out[0:1, :] += jnp.sum(grad_step, axis=0, keepdims=True)
    small_out[1:2, :] += rate * jnp.sum(delta * flow, axis=0, keepdims=True)
    rows_out[...] = row_of(dots)


def run_backward(
    starts, fills, tiles, strips, states, vectors, parts, at_part, model_place, previous, total_width
):
    gate_pre, grad_scaled, scan, values, value_pre, selects, delta, sums, step_pre = tiles
    conv_value, conv_value_bias, gain, step_bias, decay_log, skip = vectors
    rows, whole = value_pre.shape
    width = whole // PARTS
    heads = width // (LANES // 2)
    spans = rows // SPAN
    select_width = selects.shape[1]
    half = at_part

    def tile(columns, at=0):
        return pl.BlockSpec((SPAN, columns), lambda i: (spans - 1 - i, at))

    def out_tile(columns):
        return pl.BlockSpec((SPAN, columns), lambda i: (spans - 1 - i, 0))

    groups = parts // 2
    height = SPAN * (select_width // parts) // LANES
    shared = [pl.BlockSpec((height, LANES), lambda i: (spans - 1 - i, 0))] * (2 * groups)
    shared_shape = jax.ShapeDtypeStruct((spans * height, LANES), jnp.float32)
    strip = pl.BlockSpec((1, SPAN), lambda i: (0, spans - 1 - i))
    before = pl.BlockSpec(
        (EXTRA, width), lambda i: (jnp.maximum((spans - 1 - i) * (SPAN // EXTRA) - 1, 0), half)
    )
    return pl.pallas_call(
        functools.partial(
            backward_kernel,
            spans=spans,
            first_head=half * heads,
            adds=previous is not None,
            total_width=total_width,
            shared_groups=groups,
        ),
        grid=(spans,),
        in_specs=[
            scalars(),
            scalars(),
            tile(width, half),
            tile(width, half),
            tile(width, half),
            tile(width, half),
            tile(width, half),
            before,
            tile(select_width),
            tile(LANES),
            tile(LANES),
            tile(LANES),
            pl.BlockSpec((1, select_width // 2, width), lambda i: (spans - 1 - i, 0, half)),
            pl.BlockSpec((CONV, width), lambda i: (0, half)),
            pl.BlockSpec((1, width), lambda i: (0, half)),
            pl.BlockSpec((1, width), lambda i: (0, half)),
            strip,
            strip,
            fixed((1, LANES)),
            fixed((1, LANES)),
            fixed((1, LANES)),
            scalars(),
        ]
        + ([] if previous is None else shared),
        out_specs=[
            out_tile(2 * width),
            *shared,
            out_tile(LANES),
            pl.BlockSpec((1, SPAN), lambda i: (0, spans - 1 - i)),
            fixed((8, width)),
            fixed((8, LANES)),
        ],
        out_shape=[
            jax.ShapeDtypeStruct((rows, 2 * width), jnp.bfloat16),
            *[shared_shape] * (2 * groups),
            jax.ShapeDtypeStruct((rows, LANES), jnp.bfloat16),
            jax.ShapeDtypeStruct((1, rows), jnp.float32),
            jax.ShapeDtypeStruct((8, width), jnp.float32),
            jax.ShapeDtypeStruct((8, LANES), jnp.float32),
        ],
        scratch_shapes=[
            pltpu.VMEM((SPAN + EXTRA, width), jnp.float32),
            pltpu.VMEM((SPAN + EXTRA, width), jnp.float32),
            pltpu.VMEM((select_width // 2, width), jnp.float32),
            pltpu.VMEM((8, width), jnp.float32),
        ],
        compiler_params=settings(52),
        cost_estimate=guess(20000 * rows * width, 20 * rows * width, 300 * rows * width),
        name="backward",
    )(
        starts,
        fills,
        gate_pre,
        grad_scaled,
        scan,
        values,
        value_pre,
        value_pre,
        selects,
        delta,
        sums,
        step_pre,
        states,
        conv_value,
        conv_value_bias,
        gain,
        *strips,
        step_bias,
        decay_log,
        skip,
        model_place,
        *([] if previous is None else previous),
    )


def pair_kernel(*refs):
    groups = len(refs) // 3
    for index in range(groups):
        out = refs[2 * groups + index]
        out[...] = (refs[index][...] + refs[groups + index][...]).astype(out.dtype)


def run_pair(ours, came, wire):
    rows, columns = ours[0].shape
    groups = len(ours)
    tile = pl.BlockSpec((SPAN, columns), lambda i: (i, 0))
    return pl.pallas_call(
        pair_kernel,
        grid=(rows // SPAN,),
        in_specs=[tile] * (2 * groups),
        out_specs=[tile] * groups,
        out_shape=[jax.ShapeDtypeStruct((rows, columns), jnp.float32)]
        + [jax.ShapeDtypeStruct((rows, columns), wire)] * (groups - 1),
        compiler_params=settings(40),
        cost_estimate=guess(0, 0),
        name="pair",
    )(*ours, *came)


def select_kernel(starts, spot, select_pre, kernel, bias, *refs, count):
    grads, steps_in = refs[:count], refs[count:-5]
    low_out, rows_out, stat_out, ahead, unfolded = refs[-5:]
    rows, part = unfolded.shape
    folds = LANES // part
    height = SPAN // folds
    folded = grads[0][...]
    for grad in grads[1:]:
        folded = folded + grad[...]
    for span in range(rows // SPAN):
        for fold in range(folds):
            start = span * SPAN + fold * height
            unfolded[start : start + height, :] = folded[
                span * height : (span + 1) * height, fold * part : (fold + 1) * part
            ]
    upstream = unfolded[...]
    pre = select_pre[:, :part]
    taps = kernel[:, :part]
    own_bias = bias[:, :part]
    for index in range(1, select_pre.shape[1] // part):
        lanes = slice(index * part, (index + 1) * part)
        here = spot[0] == index
        pre = jnp.where(here, select_pre[:, lanes], pre)
        taps = jnp.where(here, kernel[:, lanes], taps)
        own_bias = jnp.where(here, bias[:, lanes], own_bias)
    place = iota((rows, part), 0)
    joined = jnp.zeros((rows, part), jnp.int32)
    for span in range(rows // SPAN):
        joined = jnp.where(place // SPAN == span, 1 - starts[span], joined)
    inside = place % SPAN
    stat_out[...] = jnp.zeros(stat_out.shape, jnp.float32)
    ahead[...] = jnp.zeros(ahead.shape, jnp.float32)
    ahead[EXTRA : EXTRA + rows, :] = pre
    shifted = []
    mixed = own_bias
    for back in range(CONV):
        moved = ahead[EXTRA - back : EXTRA - back + rows, :]
        moved = jnp.where(jnp.logical_or(inside >= back, joined == 1), moved, 0.0)
        shifted.append(moved)
        mixed = mixed + taps[CONV - 1 - back : CONV - back, :] * moved
    sig = sigmoid(mixed)
    inner = upstream * sig * (1.0 + mixed * (1.0 - sig))
    total = jnp.zeros((rows, part), jnp.float32)
    tap_sums = []
    for back in range(CONV):
        tap = taps[CONV - 1 - back : CONV - back, :]
        tap_sums.append(jnp.sum(inner * shifted[back], axis=0, keepdims=True))
        ahead[EXTRA : EXTRA + rows, :] = jnp.where(
            jnp.logical_or(inside >= back, joined == 1), inner, 0.0
        )
        ahead[EXTRA + rows :, :] = jnp.zeros((EXTRA, part), jnp.float32)
        total = total + tap * ahead[EXTRA + back : EXTRA + back + rows, :]
    rows_here = tap_sums[::-1] + [jnp.sum(inner, axis=0, keepdims=True)]
    for index in range(select_pre.shape[1] // part):
        lanes = slice(index * part, (index + 1) * part)
        for at, row in enumerate(rows_here):
            stat_out[at : at + 1, lanes] = jnp.where(spot[0] == index, row, 0.0)
    low = total.astype(jnp.bfloat16)
    dots = jnp.sum(low.astype(jnp.float32) * pre, axis=1, keepdims=True)
    rows_out[...] = jnp.transpose(jnp.broadcast_to(dots, (rows, LANES)))[:1, :]
    steps = steps_in[0][...].astype(jnp.float32)
    for piece in steps_in[1:]:
        steps = steps + piece[...].astype(jnp.float32)
    pieces = [steps[:, : LANES // 2], low.astype(jnp.float32)]
    if part < LANES // 2:
        pieces.append(jnp.zeros((rows, LANES // 2 - part), jnp.float32))
    low_out[...] = jnp.concatenate(pieces, axis=1).astype(jnp.bfloat16)


def run_select(starts, spot, grads, select_pre, kernel, bias, steps):
    rows = select_pre.shape[0]
    part = grads[0].shape[0] * LANES // rows
    inputs = (select_pre, kernel, bias, *grads, *steps)
    return pl.pallas_call(
        functools.partial(select_kernel, count=len(grads)),
        in_specs=[scalars(), scalars()] + [pl.BlockSpec(memory_space=pltpu.VMEM)] * len(inputs),
        out_shape=[
            jax.ShapeDtypeStruct((rows, LANES), jnp.bfloat16),
            jax.ShapeDtypeStruct((1, rows), jnp.float32),
            jax.ShapeDtypeStruct((8, select_pre.shape[1]), jnp.float32),
        ],
        scratch_shapes=[
            pltpu.VMEM((rows + 2 * EXTRA, part), jnp.float32),
            pltpu.VMEM((rows, part), jnp.float32),
        ],
        compiler_params=pltpu.CompilerParams(vmem_limit_bytes=40 << 20),
        cost_estimate=guess(0, 0),
        name="select",
    )(starts, spot, *inputs)


def spread_kernel(place, own_left, other_left, *refs):
    rights, (sends_out, own_out) = refs[:-2], refs[-2:]
    start = 0
    for own_right, other_right in zip(rights[::2], rights[1::2]):
        lanes = slice(start, start + own_right.shape[1])
        start += own_right.shape[1]
        product = dot_rows(own_left[0], own_right[...]) + dot_rows(other_left[0], other_right[...])
        sends_out[0, :, lanes] = product.astype(jnp.bfloat16)

        @pl.when(pl.program_id(0) == place[0])
        def _():
            own_out[:, lanes] = product


def run_spread(place, own_left, other_left, *rights):
    groups, rows, piece = own_left.shape
    columns = sum(right.shape[1] for right in rights[::2])
    left = pl.BlockSpec((1, rows, piece), lambda g: (g, 0, 0))
    return pl.pallas_call(
        spread_kernel,
        grid=(groups,),
        in_specs=[scalars(), left, left] + [fixed(right.shape) for right in rights],
        out_specs=[
            pl.BlockSpec((1, piece, columns), lambda g: (g, 0, 0)),
            fixed((piece, columns)),
        ],
        out_shape=[
            jax.ShapeDtypeStruct((groups, piece, columns), jnp.bfloat16),
            jax.ShapeDtypeStruct((piece, columns), jnp.float32),
        ],
        compiler_params=settings(44),
        cost_estimate=guess(0, 0),
        name="spread",
    )(place, own_left, other_left, *rights)


def pair_of(size):
    return [(spot, spot ^ 1) for spot in range(size)]


def shift_of(size, hops):
    groups = size // 2
    return [(spot, ((spot // 2 + hops) % groups) * 2 + spot % 2) for spot in range(size)]


def swap_pair(array, axis):
    return lax.ppermute(array, axis, pair_of(lax.axis_size(axis)))


def exchange_groups(sends):
    size = lax.axis_size("dp")
    groups = [[2 * group + side for group in range(size // 2)] for side in range(2)]
    return lax.all_to_all(sends, "dp", 0, 0, axis_index_groups=groups)


def finish(total, arrived):
    mine = lax.axis_index("dp") // 2
    for index in range(arrived.shape[0]):
        total = total + jnp.where(index == mine, 0.0, arrived[index].astype(jnp.float32))
    return total


def send_far(pieces):
    size = lax.axis_size("mp")
    return [
        lax.ppermute(piece, "mp", shift_of(size, hops + 1)) for hops, piece in enumerate(pieces)
    ]


def features_kernel(place, *refs, groups):
    hiddens, outs, gain_out = refs[:groups], refs[-1 - groups : -1], refs[-1]
    scale, small, w_gate, w_value, w_small = refs[-6 - groups : -1 - groups]
    parts = refs[groups : -6 - groups]
    width = parts[0].shape[1] // 2
    total = dot_lanes(small[...], w_small[...])
    for index, part in enumerate(parts):
        lanes = slice(index * width, (index + 1) * width)
        total = total + dot_lanes(part[:, :width], w_gate[:, lanes])
        total = total + dot_lanes(part[:, width:], w_value[:, lanes])
    gain_out[...] = jnp.zeros(gain_out.shape, jnp.float32)
    for index, hidden in enumerate(hiddens):

        @pl.when(pl.program_id(0) == index)
        def _():
            out = outs[index]
            out[...] = total
            for start in range(0, total.shape[1], LANES):
                lanes = slice(start, start + LANES)
                pulled = out[:, lanes] * hidden[:, lanes].astype(jnp.float32) * scale[...]
                gain_out[0, 0:1, lanes] = jnp.sum(pulled, axis=0, keepdims=True)


def back_features(place, hiddens, scale, parts, small, weights, groups):
    rows = small.shape[0]
    features = weights[0].shape[0]
    piece = features // (2 * groups)
    return pl.pallas_call(
        functools.partial(features_kernel, groups=groups),
        grid_spec=pltpu.PrefetchScalarGridSpec(
            num_scalar_prefetch=1,
            grid=(groups,),
            in_specs=[resident(array.shape) for array in (*hiddens, *parts, scale, small)]
            + [
                pl.BlockSpec(
                    (piece, array.shape[1]), lambda g, at: (2 * ((at[0] + g) % groups) + at[1], 0)
                )
                for array in weights
            ],
            out_specs=[resident((rows, piece))] * groups
            + [pl.BlockSpec((1, 8, piece), lambda g, at: (g, 0, 0))],
        ),
        out_shape=[jax.ShapeDtypeStruct((rows, piece), jnp.float32)] * groups
        + [jax.ShapeDtypeStruct((groups, 8, piece), jnp.float32)],
        compiler_params=settings(52),
        cost_estimate=guess(0, 0),
        name="features",
    )(place, *hiddens, *parts, scale, small, *weights)


def sum_all(values, axis):
    size = lax.axis_size(axis)
    step = 1
    while step < size:
        values = values + lax.ppermute(values, axis, [(spot, spot ^ step) for spot in range(size)])
        step *= 2
    return values


def pack_kernel(*refs, head_dim):
    stats, smalls, gains = refs[:PARTS], refs[PARTS : 2 * PARTS], refs[2 * PARTS + 1 : -1]
    select, out, count = refs[2 * PARTS], refs[-1], PARTS
    gain = gains[0][0:1, :]
    for piece in gains[1:]:
        gain = gain + piece[0:1, :]
    width = stats[0].shape[1]
    whole = width * count
    out[...] = jnp.zeros(out.shape, jnp.float32)
    small = smalls[0][...]
    for piece in smalls[1:]:
        small = small + piece[...]
    for index, piece in enumerate(stats):
        out[:8, index * width : (index + 1) * width] = piece[...]
    heads = jnp.zeros((8, LANES), jnp.float32)
    for start in range(0, whole, LANES):
        owner = (
            iota((LANES, LANES), 1) == (start + iota((LANES, LANES), 0)) // head_dim
        ).astype(jnp.float32)
        heads = heads + exact(out[:8, start : start + LANES], owner)
    out[8:16, : select.shape[1]] = select[...]
    out[16:18, :LANES] = small[:2, :]
    out[18:19, :LANES] = heads[CONV + 1 : CONV + 2, :]
    for start in range(0, gain.shape[1], LANES):
        out[19 + start // LANES : 20 + start // LANES, :LANES] = gain[:, start : start + LANES]


def run_pack(stats, smalls, select, gains, head_dim):
    whole = stats[0].shape[1] * len(stats)
    rows = -(-(19 + gains[0].shape[1] // LANES) // 8) * 8
    return pl.pallas_call(
        functools.partial(pack_kernel, head_dim=head_dim),
        out_shape=jax.ShapeDtypeStruct((rows, whole), jnp.float32),
        cost_estimate=guess(0, 0),
        name="pack",
    )(*stats, *smalls, select, *gains)


def unpack_kernel(*refs):
    arrived, outs = refs[:-9], refs[-9:]
    total = arrived[0][...]
    for piece in arrived[1:]:
        total = total + piece[...]
    taps, bias, select, select_bias, step, decay, skip, gate_gain, gain = outs
    taps[...] = total[:CONV, :]
    bias[...] = total[CONV : CONV + 1, :]
    gate_gain[...] = total[CONV + 2 : CONV + 3, :]
    select[...] = total[8 : 8 + CONV, : select.shape[1]]
    select_bias[...] = total[8 + CONV : 9 + CONV, : select.shape[1]]
    heads = step.shape[1]
    step[...] = total[16:17, :heads]
    decay[...] = total[17:18, :heads]
    skip[...] = total[18:19, :heads]
    for start in range(0, gain.shape[1], LANES):
        gain[:, start : start + LANES] = total[19 + start // LANES : 20 + start // LANES, :LANES]


def run_unpack(arrived, select_width, heads, gain_width):
    whole = arrived[0].shape[1]
    shapes = [(CONV, whole), (1, whole), (CONV, select_width), (1, select_width)]
    shapes += [(1, heads)] * 3 + [(1, whole), (1, gain_width)]
    return pl.pallas_call(
        unpack_kernel,
        out_shape=[jax.ShapeDtypeStruct(shape, jnp.float32) for shape in shapes],
        cost_estimate=guess(0, 0),
        name="unpack",
    )(*arrived)


def sum_tokens(values):
    size = lax.axis_size("dp")
    both = values + swap_pair(values, "dp")
    return [both] + [
        lax.ppermute(both, "dp", shift_of(size, hops)) for hops in range(1, size // 2)
    ]


def widen_lanes(vector):
    return jnp.pad(vector, (0, LANES - vector.shape[0]))[None, :]


def on_device(
    hidden_in,
    cotangent,
    span_starts,
    span_fill,
    norm_gain,
    w_gate,
    w_value,
    w_select,
    w_step,
    conv_value,
    conv_value_bias,
    conv_select,
    conv_select_bias,
    step_bias,
    decay_log,
    skip_gain,
    gate_gain,
    w_out,
):
    token_rows = hidden_in.shape[0]
    model_width = norm_gain.shape[0]
    inner_cols = w_gate.shape[1]
    local_heads = w_step.shape[1]
    head_dim = inner_cols // local_heads
    select_width = w_select.shape[1]
    model_parts = lax.axis_size("mp")
    model_groups = model_parts // 2
    data_parts = lax.axis_size("dp")
    inner_total = inner_cols * model_parts
    feature_piece = model_width // model_parts
    data_piece = model_width // data_parts
    part = select_width // model_parts
    model_spot = lax.axis_index("mp")
    model_side = model_spot % 2
    data_side = (lax.axis_index("dp") % 2).reshape(1)
    offset = model_spot * feature_piece
    select_start = model_spot * part

    def after(array, *others):
        return lax.optimization_barrier((array, *others))[0]

    def gather_far(block):
        return [
            lax.ppermute(block, "mp", shift_of(model_parts, hops)) for hops in range(1, model_groups)
        ]

    def gather_near(block, far, *others):
        blocks = [block, swap_pair(block, "mp")]
        for same in far:
            same = after(same, *others) if others else same
            blocks += [same, swap_pair(same, "mp")]
        return blocks

    def theirs(block):
        pieces = []
        for index in range(0, block.shape[1] // data_piece, 2):
            first = block[:, index * data_piece : (index + 1) * data_piece]
            second = block[:, (index + 1) * data_piece : (index + 2) * data_piece]
            pieces.append(jnp.where(data_side[0] == 0, second, first))
        return pieces

    gain_row = gate_gain[None, :]
    skip_row = widen_lanes(skip_gain)
    bias_step = widen_lanes(step_bias)
    decay_row = widen_lanes(decay_log)
    half_lanes = LANES // 2
    wide_step = jnp.pad(w_step, ((0, 0), (0, LANES - local_heads)))
    spots = []
    for hops in range(model_groups):
        group = (model_spot // 2 - hops) % model_groups
        spots += [2 * group + model_side, 2 * group + 1 - model_side]
    spots = jnp.stack(spots)

    place = (lax.axis_index("dp") // 2).reshape(1)
    model_place = jnp.stack([model_spot // 2, model_side])
    other_place = jnp.stack([model_spot // 2, 1 - model_side])
    vectors = (conv_value, conv_value_bias[None, :])
    head_vectors = (bias_step, decay_row, skip_row)

    far_in = gather_far(hidden_in)
    cross = swap_pair(jnp.concatenate(theirs(hidden_in) + theirs(cotangent), axis=1), "dp")
    blocks_in = gather_near(hidden_in, far_in)
    combined = after(jnp.concatenate([cotangent, cross], axis=1), *far_in)
    far_up = gather_far(combined)

    (
        normed_own,
        scale_rows,
        scale_columns,
        value_pre,
        gate_pre,
        select_pre,
        step_pre,
        values,
        selects,
        scan,
        gated,
        delta,
        sums,
        states,
        square_part,
    ) = run_forward(
        data_side,
        spots,
        span_starts,
        span_fill,
        [after(blocks_in[0], cross)] + blocks_in[1:],
        norm_gain[None, :],
        (w_value, w_gate, w_select, wide_step),
        vectors + (conv_select, conv_select_bias[None, :]) + head_vectors,
        data_piece,
    )
    other_rows = swap_pair(scale_rows, "dp")
    blocks_up = gather_near(combined, far_up, square_part)
    squares = after(sum_all(square_part, "mp"), other_rows)
    scaled = run_scale(gated, squares, gain_row, inner_total)
    late_select, late_step = lax.optimization_barrier((w_select, w_step, scaled))[:2]
    own_select = lax.dynamic_slice_in_dim(late_select, select_start, part, 1)
    w_small = jnp.concatenate(
        [
            jnp.pad(late_step, ((0, 0), (0, half_lanes - local_heads))),
            jnp.pad(own_select, ((0, 0), (0, half_lanes - part))),
        ],
        axis=1,
    )
    scaled_other = swap_pair(scaled, "dp")
    grad_scaled, product_part, up_own, normed_other, up_other = run_cotangent(
        data_side,
        spots,
        other_rows,
        norm_gain,
        gain_row,
        w_out,
        gated,
        blocks_up,
        data_piece,
    )
    products = sum_all(product_part, "mp")

    def backward(index, products, previous):
        return run_backward(
            span_starts,
            span_fill,
            (gate_pre, grad_scaled, scan, values, value_pre, selects, delta, sums, step_pre),
            (squares, products),
            states,
            vectors + (gain_row,) + head_vectors,
            model_parts,
            index,
            model_place,
            previous,
            inner_total,
        )

    parts, others, stats, smalls, steps, row_dots = [], [], [], [], [], []
    own_parts, out_parts = [], []
    previous = None
    gate = products
    last_other, last_out = scaled_other, None
    for index in range(PARTS):
        part_grads, *previous, step, rows, stat, small = backward(index, gate, previous)
        if index == 0:
            lefts, right = (up_own, up_other), scaled
        else:
            lefts, right = (normed_own, normed_other), parts[index - 1]
        if index == 1:
            mixed = run_mixed(model_place, after(scaled, sends), w_out, model_groups)
            mixed_came = [swap_pair(piece, "mp") for piece in mixed[:model_groups]]
            arrived = after(last_other, part_grads, mixed[0])
        else:
            arrived = after(last_other, part_grads)
        last_other = swap_pair(after(part_grads, arrived), "dp")
        sends, own = run_spread(place, *lefts, right, arrived)
        sends = sends if last_out is None else after(sends, last_out)
        last_out = exchange_groups(sends)
        own_parts.append(own)
        out_parts.append(last_out)
        gate = after(products, sends)
        parts.append(part_grads)
        others.append(last_other)
        steps.append(step)
        row_dots.append(rows)
        stats.append(stat)
        smalls.append(small)
    own_out, out_out = own_parts.pop(0), out_parts.pop(0)

    mixed_total, *mixed_pieces = run_pair(
        mixed[model_groups:], [after(mixed_came[0], sends)] + mixed_came[1:], jnp.float32
    )
    came = [swap_pair(after(piece, others[-2]), "mp") for piece in previous[:model_groups]]
    select_total, *select_pieces = run_pair(
        previous[model_groups:], [after(came[0], mixed_total)] + came[1:], jnp.float32
    )
    select_arrived = send_far(select_pieces)
    mixed_arrived = send_far([after(piece, *select_arrived) for piece in mixed_pieces])
    small_low, select_rows, select_stats = run_select(
        span_starts,
        model_spot.reshape(1),
        [select_total] + select_arrived,
        select_pre,
        conv_select,
        conv_select_bias[None, :],
        steps,
    )
    select_sums = sum_all(select_stats, "mp")
    row_total = select_rows
    for rows in row_dots:
        row_total = row_total + rows
    norm_rows = sum_all(row_total, "mp")
    weights = (w_gate, w_value, w_small)
    hiddens = [
        [blocks_in[2 * ((model_groups - group) % model_groups) + side] for group in range(model_groups)]
        for side in range(2)
    ]
    *back_theirs, gain_theirs = back_features(
        other_place,
        hiddens[1],
        scale_columns,
        parts,
        small_low,
        weights,
        model_groups,
    )
    last_arrived = after(others[-1], back_theirs[0])
    small_other = swap_pair(after(small_low, last_arrived), "dp")
    back_came = [swap_pair(after(piece, last_arrived), "mp") for piece in back_theirs]
    sends_last, own_last = run_spread(
        place, normed_own, normed_other, parts[-1], last_arrived, small_low, small_other
    )
    out_last = exchange_groups(after(sends_last, last_out))
    *back_ours, gain_ours = back_features(
        model_place,
        hiddens[0],
        scale_columns,
        parts,
        after(small_low, sends_last, *mixed_arrived),
        weights,
        model_groups,
    )
    back_total, *back_pieces = run_pair(
        back_ours, [after(back_came[0], *mixed_arrived)] + back_came[1:], jnp.bfloat16
    )
    gain_both = gain_ours + swap_pair(gain_theirs, "mp")
    gain_sums = [gain_both[0]] + send_far([gain_both[hops] for hops in range(1, model_groups)])
    back_pieces = [after(piece, *gain_sums, select_sums, norm_rows) for piece in back_pieces]
    back_arrived = send_far(back_pieces)
    own_parts.append(own_last)
    out_parts.append(out_last)
    for index in range(PARTS):
        out_parts[index] = after(out_parts[index], *back_pieces)
    out_out = after(out_out, *back_pieces)

    grad_normed = back_total
    for piece in back_arrived:
        grad_normed = grad_normed + piece.astype(jnp.float32)
    own_in = hidden_in.astype(jnp.float32)
    mixed_share = mixed_total
    for piece in mixed_arrived:
        mixed_share = mixed_share + piece
    output = (own_in + mixed_share).astype(jnp.bfloat16)
    own_gain = lax.dynamic_slice_in_dim(norm_gain, offset, feature_piece, 0)
    own_scale = scale_columns[:, :1]
    weighted_in = grad_normed * own_gain[None, :]
    grad_hidden_in = (
        cotangent.astype(jnp.float32)
        + weighted_in * own_scale
        - own_in * own_scale**2 * norm_rows[0][:, None] / model_width
    )
    packed = run_pack(stats, smalls, select_sums, gain_sums, head_dim)
    (
        grad_taps,
        grad_bias,
        grad_select_taps,
        grad_select_bias,
        grad_step_bias,
        grad_decay_log,
        grad_skip_gain,
        grad_gate_gain,
        gain_sum,
    ) = run_unpack(sum_tokens(after(packed, *back_pieces)), select_width, local_heads, feature_piece)

    grad_w_out = finish(own_out, out_out).T
    done = [finish(own, out) for own, out in zip(own_parts, out_parts)]
    width = inner_cols // PARTS
    grad_w_gate = jnp.concatenate([piece[:, :width] for piece in done], axis=1)
    grad_w_value = jnp.concatenate([piece[:, width : 2 * width] for piece in done], axis=1)
    grad_w_small = done[-1][:, 2 * width :]
    grad_w_step = grad_w_small[:, :local_heads]
    grad_w_select = lax.all_gather(
        grad_w_small[:, half_lanes : half_lanes + part], "mp", axis=1, tiled=True
    )
    return (
        output,
        grad_hidden_in,
        gain_sum[0],
        grad_w_gate,
        grad_w_value,
        grad_w_select,
        grad_w_step,
        grad_taps,
        grad_bias[0],
        grad_select_taps,
        grad_select_bias[0],
        grad_step_bias[0],
        grad_decay_log[0],
        grad_skip_gain[0],
        grad_gate_gain[0],
        grad_w_out,
    )


def solution(mesh):
    in_specs = (
        P("dp", "mp"),
        P("dp", "mp"),
        P("dp"),
        P("dp"),
        P(),
        P(None, "mp"),
        P(None, "mp"),
        P(),
        P(None, "mp"),
        P(None, "mp"),
        P("mp"),
        P(),
        P(),
        P("mp"),
        P("mp"),
        P("mp"),
        P("mp"),
        P("mp", None),
    )
    out_specs = (
        P("dp", "mp"),
        P("dp", "mp"),
        P("mp"),
        P("dp", "mp"),
        P("dp", "mp"),
        P("dp", None),
        P("dp", "mp"),
        P(None, "mp"),
        P("mp"),
        P(),
        P(),
        P("mp"),
        P("mp"),
        P("mp"),
        P("mp"),
        P("mp", "dp"),
    )
    return jax.shard_map(
        on_device, mesh=mesh, in_specs=in_specs, out_specs=out_specs, check_vma=False
    )
```

```python
import functools

import jax
import jax.numpy as jnp
from jax import lax
from jax.experimental import pallas as pl
from jax.experimental.pallas import tpu as pltpu
from jax.sharding import PartitionSpec as P

CONV = 4
SPAN = 256
LANES = 128
EXTRA = 8
TOP = 15.0
FAR = -1e30
PARTS = 2
epsilon = 1e-05
exact_mode = lax.Precision.HIGHEST


def settings(mebibytes, axes=1):
    return pltpu.CompilerParams(
        dimension_semantics=("arbitrary",) * axes, vmem_limit_bytes=mebibytes << 20
    )


def scalars():
    return pl.BlockSpec(memory_space=pltpu.SMEM)


def fixed(shape):
    return pl.BlockSpec(shape, lambda *_: (0,) * len(shape))


def split_bits(value):
    high = value.astype(jnp.bfloat16)
    low = (value - high.astype(jnp.float32)).astype(jnp.bfloat16)
    return high, low


def dot(left, right):
    return lax.dot_general(left, right, (((1,), (0,)), ((), ())), preferred_element_type=jnp.float32)


def dot_lanes(left, right):
    return lax.dot_general(left, right, (((1,), (1,)), ((), ())), preferred_element_type=jnp.float32)


def dot_rows(left, right):
    return lax.dot_general(left, right, (((0,), (0,)), ((), ())), preferred_element_type=jnp.float32)


def exact(left, right):
    return jnp.dot(left, right, precision=exact_mode, preferred_element_type=jnp.float32)


def beside(*pieces):
    return jnp.concatenate(pieces, axis=1)


def above(*pieces):
    return jnp.concatenate(pieces, axis=0)


def sigmoid(value):
    return 1.0 / (1.0 + jnp.exp(-value))


def iota(shape, axis):
    return lax.broadcasted_iota(jnp.int32, shape, axis)


def two_heads(columns, pair, in_first):
    first = columns[:, 2 * pair : 2 * pair + 1]
    second = columns[:, 2 * pair + 1 : 2 * pair + 2]
    return jnp.where(in_first, first, second)


def row_of(columns):
    return jnp.sum(jnp.transpose(columns), axis=0, keepdims=True)


def live_rows(fill, width):
    return (iota((SPAN, width), 0) < fill).astype(jnp.float32)


def wide_lanes(start, width):
    return pl.ds(pl.multiple_of(start * width, min(width, LANES)), width)


def store_ours(side, block, spot, ours_out, piece):
    for index in range(block.shape[1] // (2 * piece)):
        first = block[:, 2 * index * piece : (2 * index + 1) * piece]
        second = block[:, (2 * index + 1) * piece : (2 * index + 2) * piece]
        group = spot * (block.shape[1] // (2 * piece)) + index
        ours_out[pl.ds(group, 1)] = jnp.where(side == 0, first, second)[None]


def guess(flops, moved, exps=0):
    return pl.CostEstimate(flops=1, bytes_accessed=1, transcendentals=0)


def conv_of(extended, kernel, bias, lanes):
    total = bias[:, lanes]
    for back in range(CONV):
        tap = kernel[CONV - 1 - back : CONV - back, lanes]
        total = total + tap * extended[EXTRA - back : EXTRA - back + SPAN, lanes]
    return total


def forward_kernel(
    side,
    spots,
    starts,
    fills,
    norm_gain,
    w_value,
    w_gate,
    w_select,
    w_step,
    conv_value,
    conv_value_bias,
    conv_select,
    conv_select_bias,
    step_bias,
    decay_log,
    skip,
    *refs,
    piece,
):
    blocks = refs[:-19]
    (
        ours_out,
        scale_out,
        scale_columns_out,
        value_pre,
        gate_pre,
        select_pre,
        step_pre,
        values_out,
        selects_out,
        scan_out,
        gated_out,
        delta_out,
        sum_out,
        state_out,
        rows_out,
        extended,
        extended_select,
        state,
        whole,
    ) = refs[-19:]
    step = pl.program_id(0)
    fresh = starts[step] == 1
    width = value_pre.shape[1]
    state_dim = select_pre.shape[1] // 2

    part_width = blocks[0].shape[1]
    total = jnp.zeros((SPAN, LANES), jnp.float32)
    for block in blocks:
        for start in range(0, part_width, LANES):
            part = block[:, start : start + LANES].astype(jnp.float32)
            total = total + part * part
    mean = jnp.sum(total, axis=1, keepdims=True) / (part_width * len(blocks))
    scale = lax.rsqrt(mean + epsilon)
    scale_columns_out[...] = jnp.broadcast_to(scale, (SPAN, LANES))
    scale_out[...] = jnp.transpose(scale_columns_out[...])[:1, :]
    for index, block in enumerate(blocks):
        spot = spots[index]
        window = wide_lanes(spot, part_width)
        own_gain = norm_gain[:, window]
        normed = (block[...].astype(jnp.float32) * scale * own_gain).astype(jnp.bfloat16)
        store_ours(side[0], normed, spot, ours_out, piece)
        whole[:, window] = normed
    for out, weights in (
        (select_pre, w_select),
        (step_pre, w_step),
        (value_pre, w_value),
        (gate_pre, w_gate),
    ):
        out[...] = dot(whole[...], weights[...])

    @pl.when(fresh)
    def _():
        extended[:EXTRA, :] = jnp.zeros((EXTRA, width), jnp.float32)
        extended_select[:EXTRA, :] = jnp.zeros((EXTRA, 2 * state_dim), jnp.float32)
        state[...] = jnp.zeros(state.shape, jnp.float32)

    @pl.when(jnp.logical_not(fresh))
    def _():
        extended[:EXTRA, :] = extended[SPAN:, :]
        extended_select[:EXTRA, :] = extended_select[SPAN:, :]

    extended[EXTRA:, :] = value_pre[...]
    extended_select[EXTRA:, :] = select_pre[...]
    state_out[0] = state[...]

    live = live_rows(fills[step], LANES)
    pre_step = step_pre[...] + step_bias[...]
    delta = live * (jnp.maximum(pre_step, 0.0) + jnp.log1p(jnp.exp(-jnp.abs(pre_step))))
    rate = -jnp.exp(decay_log[...])
    lower = (iota((SPAN, SPAN), 0) >= iota((SPAN, SPAN), 1)).astype(jnp.float32)
    cumulative = exact(lower, delta * rate)
    delta_out[...] = delta
    sum_out[...] = cumulative
    sums_across = jnp.transpose(cumulative)
    delta_across = jnp.transpose(delta)
    grown = jnp.exp(cumulative)
    tail = delta * jnp.exp(cumulative[SPAN - 1 : SPAN, :] - cumulative)

    halves = []
    for half in range(2):
        lanes = slice(half * state_dim, (half + 1) * state_dim)
        mixed = conv_of(extended_select, conv_select, conv_select_bias, lanes)
        chosen = (mixed * sigmoid(mixed)).astype(jnp.bfloat16)
        selects_out[:, lanes] = chosen
        halves.append(chosen)
    inflow, readout = halves
    inflow_across = jnp.transpose(inflow.astype(jnp.float32)).astype(jnp.bfloat16)
    scores = dot_lanes(readout, inflow)
    middle = SPAN // 2
    past = iota((middle, middle), 0) >= iota((middle, middle), 1)
    later_past = iota((middle, SPAN), 0) + middle >= iota((middle, SPAN), 1)
    in_first = iota((SPAN, LANES), 1) < LANES // 2
    row_first = iota((1, LANES), 1) < LANES // 2
    readout_twice = beside(readout, readout)
    squares = jnp.zeros((SPAN, LANES), jnp.float32)
    for pair in range(width // LANES):
        lanes = slice(pair * LANES, (pair + 1) * LANES)
        mixed = conv_of(extended, conv_value, conv_value_bias, lanes)
        value_low = (mixed * sigmoid(mixed)).astype(jnp.bfloat16)
        values_out[:, lanes] = value_low
        value = value_low.astype(jnp.float32)
        entering = state[:, lanes]
        scan = dot(readout_twice, above(*split_bits(entering))) * two_heads(grown, pair, in_first)
        scan = scan + two_heads(skip[...], pair, row_first) * value
        for which in range(2):
            head = 2 * pair + which
            own = jnp.where(in_first == (which == 0), value_low, jnp.zeros_like(value_low))
            sums_row = sums_across[head : head + 1, :]
            delta_row = delta_across[head : head + 1, :]
            gaps = cumulative[:middle, head : head + 1] - sums_row[:, :middle]
            weights = jnp.exp(jnp.where(past, gaps, FAR))
            high, low = split_bits(scores[:middle, :middle] * weights * delta_row[:, :middle])
            early = dot(high, own[:middle]) + dot(low, own[:middle])
            gaps = cumulative[middle:, head : head + 1] - sums_row
            weights = jnp.exp(jnp.where(later_past, gaps, FAR))
            high, low = split_bits(scores[middle:] * weights * delta_row)
            scan = scan + above(early, dot(high, own) + dot(low, own))
        scan_out[:, lanes] = scan
        gate = gate_pre[:, lanes]
        gated = live * scan * gate * sigmoid(gate)
        squares = squares + gated * gated
        gated_out[:, lanes] = gated
        weighted = value * two_heads(tail, pair, in_first)
        high, low = split_bits(weighted)
        last = two_heads(grown[SPAN - 1 : SPAN, :], pair, row_first)
        state[:, lanes] = entering * last + dot(inflow_across, high) + dot(inflow_across, low)
    rows_out[...] = row_of(squares)


def resident(shape):
    return pl.BlockSpec(shape, lambda *_: (0,) * len(shape), pipeline_mode=pl.Buffered(1))


def run_forward(side, spots, starts, fills, blocks, gain, weights, vectors, piece):
    rows, part_width = blocks[0].shape
    groups = part_width * len(blocks) // (2 * piece)
    w_value, w_gate, w_select, w_step = weights
    width = w_value.shape[1]
    spans = rows // SPAN
    select_width = w_select.shape[1]

    def tile(columns):
        return pl.BlockSpec((SPAN, columns), lambda i: (i, 0))

    def like(columns, dtype):
        return jax.ShapeDtypeStruct((rows, columns), dtype)

    strip = pl.BlockSpec((1, SPAN), lambda i: (0, i))
    return pl.pallas_call(
        functools.partial(forward_kernel, piece=piece),
        grid=(spans,),
        in_specs=[scalars()] * 4
        + [fixed(gain.shape)]
        + [resident(array.shape) for array in weights]
        + [fixed(array.shape) for array in vectors]
        + [tile(part_width)] * len(blocks),
        out_specs=[
            pl.BlockSpec((groups, SPAN, piece), lambda i: (0, i, 0)),
            strip,
            tile(LANES),
            tile(width),
            tile(width),
            tile(select_width),
            tile(LANES),
            tile(width),
            tile(select_width),
            tile(width),
            tile(width),
            tile(LANES),
            tile(LANES),
            pl.BlockSpec((1, select_width // 2, width), lambda i: (i, 0, 0)),
            strip,
        ],
        out_shape=[
            jax.ShapeDtypeStruct((groups, rows, piece), jnp.bfloat16),
            jax.ShapeDtypeStruct((1, rows), jnp.float32),
            like(LANES, jnp.float32),
            like(width, jnp.float32),
            like(width, jnp.float32),
            like(select_width, jnp.float32),
            like(LANES, jnp.float32),
            like(width, jnp.bfloat16),
            like(select_width, jnp.bfloat16),
            like(width, jnp.float32),
            like(width, jnp.float32),
            like(LANES, jnp.float32),
            like(LANES, jnp.float32),
            jax.ShapeDtypeStruct((spans, select_width // 2, width), jnp.float32),
            jax.ShapeDtypeStruct((1, rows), jnp.float32),
        ],
        scratch_shapes=[
            pltpu.VMEM((SPAN + EXTRA, width), jnp.float32),
            pltpu.VMEM((SPAN + EXTRA, select_width), jnp.float32),
            pltpu.VMEM((select_width // 2, width), jnp.float32),
            pltpu.VMEM((SPAN, part_width * len(blocks)), jnp.bfloat16),
        ],
        compiler_params=settings(50),
        cost_estimate=guess(0, 0),
        name="forward",
    )(side, spots, starts, fills, gain, *weights, *vectors, *blocks)


def scale_column(rows, total_width):
    turned = jnp.transpose(above(rows[...], jnp.zeros((LANES - 1, SPAN), jnp.float32)))
    return lax.rsqrt(turned[:, 0:1] / total_width + epsilon)


def scale_kernel(gated_in, squares, gain, scaled_out, *, total_width):
    width = gated_in.shape[1]
    scale = jnp.broadcast_to(scale_column(squares, total_width), (SPAN, LANES))
    for start in range(0, width, LANES):
        lanes = slice(start, start + LANES)
        scaled_out[:, lanes] = (gated_in[:, lanes] * scale * gain[:, lanes]).astype(jnp.bfloat16)


def run_scale(gated, squares, gain, total_width):
    rows, width = gated.shape
    return pl.pallas_call(
        functools.partial(scale_kernel, total_width=total_width),
        grid=(rows // SPAN,),
        in_specs=[
            pl.BlockSpec((SPAN, width), lambda i: (i, 0)),
            pl.BlockSpec((1, SPAN), lambda i: (0, i)),
            fixed((1, width)),
        ],
        out_specs=pl.BlockSpec((SPAN, width), lambda i: (i, 0)),
        out_shape=jax.ShapeDtypeStruct((rows, width), jnp.bfloat16),
        compiler_params=settings(32),
        cost_estimate=guess(6 * rows * width, 6 * rows * width),
        name="scale",
    )(gated, squares, gain)


def cotangent_kernel(
    side, spots, rows, norm_gain, gain, w_out, gated_in, *refs, piece
):
    blocks = refs[:-5]
    grad_out, rows_out, ours_out, other_normed_out, other_out = refs[-5:]
    width = blocks[0].shape[1] // 2
    cross = width // 2
    turned = jnp.transpose(above(rows[...], jnp.zeros((LANES - 1, SPAN), jnp.float32)))
    scale = turned[:, 0:1]
    each = cross // piece
    total = None
    for index, block in enumerate(blocks):
        spot = spots[index]
        upstream = block[:, :width]
        product = dot_lanes(upstream, w_out[:, wide_lanes(spot, width)])
        total = product if index == 0 else total + product
        store_ours(side[0], upstream, spot, ours_out, piece)
        for inner in range(each):
            group = spot * each + inner
            own_gain = norm_gain[pl.ds(2 * group + side[0], 1), :]
            start = width + inner * piece
            hidden = block[:, start : start + piece].astype(jnp.float32)
            other_normed_out[pl.ds(group, 1)] = (hidden * scale * own_gain).astype(jnp.bfloat16)[None]
            start = width + cross + inner * piece
            other_out[pl.ds(group, 1)] = block[:, start : start + piece][None]
    grad_out[...] = total
    products = jnp.zeros((SPAN, LANES), jnp.float32)
    for start in range(0, gated_in.shape[1], LANES):
        lanes = slice(start, start + LANES)
        products = products + grad_out[:, lanes] * gain[:, lanes] * gated_in[:, lanes]
    rows_out[...] = row_of(products)


def run_cotangent(side, spots, rows_in, norm_gain, gain, w_out, gated, blocks, piece):
    rows, width = gated.shape
    features = w_out.shape[1]
    groups = features // (2 * piece)
    strip = pl.BlockSpec((1, SPAN), lambda i: (0, i))

    def tile(columns):
        return pl.BlockSpec((SPAN, columns), lambda i: (i, 0))

    pieces = pl.BlockSpec((groups, SPAN, piece), lambda i: (0, i, 0))
    pieces_shape = jax.ShapeDtypeStruct((groups, rows, piece), jnp.bfloat16)
    return pl.pallas_call(
        functools.partial(cotangent_kernel, piece=piece),
        grid=(rows // SPAN,),
        in_specs=[
            scalars(),
            scalars(),
            strip,
            fixed((2 * groups, piece)),
            fixed(gain.shape),
            resident(w_out.shape),
            tile(width),
        ]
        + [tile(block.shape[1]) for block in blocks],
        out_specs=[tile(width), strip, pieces, pieces, pieces],
        out_shape=[
            jax.ShapeDtypeStruct((rows, width), jnp.float32),
            jax.ShapeDtypeStruct((1, rows), jnp.float32),
            pieces_shape,
            pieces_shape,
            pieces_shape,
        ],
        compiler_params=settings(48),
        cost_estimate=guess(0, 0),
        name="cotangent",
    )(
        side,
        spots,
        rows_in,
        norm_gain.reshape(2 * groups, piece),
        gain,
        w_out,
        gated,
        *blocks,
    )


def mixed_kernel(place, scaled, w_out, *outs):
    product = dot(scaled[...], w_out[...])
    for index, out in enumerate(outs):

        @pl.when(pl.program_id(0) == index)
        def _():
            out[...] = product


def run_mixed(place, scaled, w_out, groups):
    rows, width = scaled.shape
    piece = w_out.shape[1] // (2 * groups)

    def column(g, at):
        side = jnp.where(g < groups, 1 - at[1], at[1])
        return 0, 2 * ((at[0] + g) % groups) + side

    return pl.pallas_call(
        mixed_kernel,
        grid_spec=pltpu.PrefetchScalarGridSpec(
            num_scalar_prefetch=1,
            grid=(2 * groups,),
            in_specs=[resident((rows, width)), pl.BlockSpec((width, piece), column)],
            out_specs=[resident((rows, piece))] * (2 * groups),
        ),
        out_shape=[jax.ShapeDtypeStruct((rows, piece), jnp.float32)] * (2 * groups),
        compiler_params=settings(40),
        cost_estimate=guess(0, 0),
        name="mixed",
    )(place, scaled, w_out)


def backward_kernel(
    starts,
    fills,
    gate_pre,
    grad_scaled,
    scan_in,
    values_in,
    value_pre,
    value_before,
    selects_in,
    delta_in,
    sum_in,
    step_pre,
    state_in,
    conv_value,
    conv_value_bias,
    gain,
    squares,
    products,
    step_bias,
    decay_log,
    skip,
    model_place,
    *rest,
    spans,
    first_head,
    adds,
    total_width,
    shared_groups,
):
    groups = shared_groups
    if adds:
        before, rest = rest[: 2 * groups], rest[2 * groups :]
    value_out, shared_outs, rest = rest[0], rest[1 : 1 + 2 * groups], rest[1 + 2 * groups :]
    (
        step_out,
        rows_out,
        stat_out,
        small_out,
        extended,
        shifted,
        state,
        carried,
    ) = rest
    step = pl.program_id(0)
    span = spans - 1 - step
    width = values_in.shape[1]
    state_dim = selects_in.shape[1] // 2
    following = jnp.minimum(span + 1, spans - 1)
    joined = jnp.logical_and(step > 0, starts[following] == 0)

    @pl.when(jnp.logical_not(joined))
    def _():
        shifted[SPAN:, :] = jnp.zeros((EXTRA, width), jnp.float32)
        state[...] = jnp.zeros(state.shape, jnp.float32)
        carried[...] = jnp.zeros(carried.shape, jnp.float32)

    @pl.when(joined)
    def _():
        shifted[SPAN:, :] = shifted[:EXTRA, :]

    @pl.when(step == 0)
    def _():
        stat_out[...] = jnp.zeros(stat_out.shape, jnp.float32)
        small_out[...] = jnp.zeros(small_out.shape, jnp.float32)

    fresh = starts[span] == 1

    @pl.when(fresh)
    def _():
        extended[:EXTRA, :] = jnp.zeros((EXTRA, width), jnp.float32)

    @pl.when(jnp.logical_not(fresh))
    def _():
        extended[:EXTRA, :] = value_before[...]

    extended[EXTRA:, :] = value_pre[...]

    delta = delta_in[...]
    cumulative = sum_in[...]
    sums_across = jnp.transpose(cumulative)
    grown = jnp.exp(cumulative)
    tail = jnp.exp(cumulative[SPAN - 1 : SPAN, :] - cumulative)
    delta_tail = delta * tail
    inflow = selects_in[:, :state_dim]
    readout = selects_in[:, state_dim:]
    readout_across = jnp.transpose(readout.astype(jnp.float32)).astype(jnp.bfloat16)
    scores = dot_lanes(inflow, readout)
    ahead = iota((SPAN, SPAN), 1) >= iota((SPAN, SPAN), 0)
    in_first = iota((SPAN, LANES), 1) < LANES // 2
    row_first = iota((1, LANES), 1) < LANES // 2
    live = live_rows(fills[span], LANES)
    turned = jnp.transpose(above(products[...], jnp.zeros((LANES - 1, SPAN), jnp.float32)))
    norm_scale = scale_column(squares, total_width)
    norm_pull = norm_scale * norm_scale * norm_scale * turned[:, 0:1] / total_width
    norm_scale = jnp.broadcast_to(norm_scale, (SPAN, LANES))
    norm_pull = jnp.broadcast_to(norm_pull, (SPAN, LANES))
    inflow_twice = beside(inflow, inflow)
    grad_scores = jnp.zeros((SPAN, SPAN), jnp.float32)
    grad_inflow = jnp.zeros((SPAN, state_dim), jnp.float32)
    grad_readout = jnp.zeros((SPAN, state_dim), jnp.float32)
    change = jnp.zeros((SPAN, LANES), jnp.float32)
    direct = jnp.zeros((SPAN, LANES), jnp.float32)
    jump = jnp.zeros((8, LANES), jnp.float32)
    dots = jnp.zeros((SPAN, LANES), jnp.float32)
    for own_pair in range(width // LANES):
        lanes = slice(own_pair * LANES, (own_pair + 1) * LANES)
        pair = first_head // 2 + own_pair
        gate = gate_pre[:, lanes]
        scan = scan_in[:, lanes]
        before_norm = grad_scaled[:, lanes]
        own_gain = gain[:, lanes]
        sig = sigmoid(gate)
        opened = live * gate * sig
        gated = scan * opened
        grad_gated = before_norm * own_gain * norm_scale - gated * norm_pull
        grad_gate = grad_gated * live * scan * sig * (1.0 + gate * (1.0 - sig))
        gate_low = grad_gate.astype(jnp.bfloat16)
        value_out[:, lanes] = gate_low
        dots = dots + gate_low.astype(jnp.float32) * gate
        stat_out[CONV + 2 : CONV + 3, lanes] += jnp.sum(
            before_norm * gated * norm_scale, axis=0, keepdims=True
        )
        upstream = grad_gated * opened
        up_high, up_low = split_bits(upstream)
        value_low = values_in[:, lanes]
        value = value_low.astype(jnp.float32)
        own_skip = two_heads(skip[...], pair, row_first)
        arriving = state[:, lanes]
        arriving_high, arriving_low = split_bits(arriving)
        entering = state_in[0, :, lanes]
        entering_high, entering_low = split_bits(entering)
        pulled = dot(inflow_twice, above(arriving_high, arriving_low)) * two_heads(tail, pair, in_first)
        up_both = beside(up_high, up_low)
        for which in range(2):
            head = 2 * pair + which
            mine = in_first == (which == 0)
            nothing = jnp.zeros_like(value_low)
            gaps = sums_across[head : head + 1, :] - cumulative[:, head : head + 1]
            weights = jnp.exp(jnp.where(ahead, gaps, FAR))
            high, low = split_bits(scores * weights)
            own_high = jnp.where(mine, up_high, nothing)
            own_low = jnp.where(mine, up_low, nothing)
            pulled = pulled + dot(high, own_high) + dot(high, own_low) + dot(low, own_high)
            own_value = jnp.where(mine, value_low, nothing)
            outer = dot_lanes(beside(own_value, own_value), up_both)
            grad_scores = grad_scores + outer * weights * delta[:, head : head + 1]
        delta_both = two_heads(delta, pair, in_first)
        grad_value = own_skip * upstream + delta_both * pulled
        pull_value = value * pulled
        spread = (
            iota((LANES, LANES), 1) == 2 * pair + iota((LANES, LANES), 0) // (LANES // 2)
        ).astype(jnp.bfloat16)
        spread_twice = above(spread, spread)
        moved = upstream * (scan - own_skip * value) - delta_both * pull_value
        change = change + dot(beside(*split_bits(moved)), spread_twice)
        direct = direct + dot(beside(*split_bits(pull_value)), spread_twice)
        grown_up = upstream * two_heads(grown, pair, in_first)
        high, low = split_bits(grown_up)
        grad_readout = grad_readout + dot_lanes(
            beside(high, low, high), beside(entering_high, entering_high, entering_low)
        )
        last = two_heads(grown[SPAN - 1 : SPAN, :], pair, row_first)
        leaving = arriving * last + dot(readout_across, high) + dot(readout_across, low)
        tail_value = value * two_heads(delta_tail, pair, in_first)
        high, low = split_bits(tail_value)
        grad_inflow = grad_inflow + dot_lanes(
            beside(high, low, high), beside(arriving_high, arriving_high, arriving_low)
        )
        jump = jump + exact(carried[:, lanes], spread.astype(jnp.float32))
        state[:, lanes] = leaving
        carried[:, lanes] = jnp.broadcast_to(
            jnp.sum(leaving * entering, axis=0, keepdims=True), (8, LANES)
        )
        mixed = conv_of(extended, conv_value, conv_value_bias, lanes)
        sig = sigmoid(mixed)
        inner = grad_value * sig * (1.0 + mixed * (1.0 - sig))
        shifted[:SPAN, lanes] = inner
        grad_pre = jnp.zeros((SPAN, LANES), jnp.float32)
        for back in range(CONV):
            tap = conv_value[CONV - 1 - back : CONV - back, lanes]
            grad_pre = grad_pre + tap * shifted[back : back + SPAN, lanes]
            stat_out[CONV - 1 - back : CONV - back, lanes] += jnp.sum(
                inner * extended[EXTRA - back : EXTRA - back + SPAN, lanes], axis=0, keepdims=True
            )
        stat_out[CONV : CONV + 1, lanes] += jnp.sum(inner, axis=0, keepdims=True)
        stat_out[CONV + 1 : CONV + 2, lanes] += jnp.sum(value * upstream, axis=0, keepdims=True)
        grad_low = grad_pre.astype(jnp.bfloat16)
        value_out[:, width + own_pair * LANES : width + (own_pair + 1) * LANES] = grad_low
        wide = grad_low.astype(jnp.float32)
        dots = dots + wide * extended[EXTRA:, lanes]
    high, low = split_bits(grad_scores)
    grad_inflow = grad_inflow + dot(high, readout) + dot(low, readout)
    high, low = split_bits(jnp.transpose(grad_scores))
    grad_readout = grad_readout + dot(high, inflow) + dot(low, inflow)
    part = 2 * state_dim // (2 * groups)
    folds = LANES // part
    height = SPAN // folds
    both = (grad_inflow, grad_readout)
    for hops in range(groups):
        for side in range(2):
            chosen = None
            for index in range(2 * groups):
                start = index * part
                piece = both[start // state_dim][:, start % state_dim : start % state_dim + part]
                here = jnp.logical_and(
                    lax.rem(model_place[0] + hops, groups) == index // 2,
                    jnp.where(model_place[1] == index % 2, 1, 0) == side,
                )
                chosen = piece if chosen is None else jnp.where(here, piece, chosen)
            chosen = beside(*[chosen[fold * height : (fold + 1) * height] for fold in range(folds)])
            at = side * groups + hops
            shared_outs[at][...] = chosen + before[at][...] if adds else chosen
    upper = (iota((SPAN, SPAN), 1) >= iota((SPAN, SPAN), 0)).astype(jnp.float32)
    flow = exact(upper, change) + jump[0:1, :]
    rate = -jnp.exp(decay_log[...])
    grad_delta = direct + rate * flow
    pre_step = step_pre[...]
    grad_step = grad_delta * live * sigmoid(pre_step + step_bias[...])
    column = iota((SPAN, LANES), 1)
    last_head = first_head + width // (LANES // 2)
    grad_step = jnp.where(jnp.logical_and(column >= first_head, column < last_head), grad_step, 0.0)
    step_low = grad_step.astype(jnp.bfloat16)
    step_out[...] = step_low
    wide = step_low.astype(jnp.float32)
    dots = dots + wide * pre_step
    small_out[0:1, :] += jnp.sum(grad_step, axis=0, keepdims=True)
    small_out[1:2, :] += rate * jnp.sum(delta * flow, axis=0, keepdims=True)
    rows_out[...] = row_of(dots)


def run_backward(
    starts, fills, tiles, strips, states, vectors, parts, at_part, model_place, previous, total_width
):
    gate_pre, grad_scaled, scan, values, value_pre, selects, delta, sums, step_pre = tiles
    conv_value, conv_value_bias, gain, step_bias, decay_log, skip = vectors
    rows, whole = value_pre.shape
    width = whole // PARTS
    heads = width // (LANES // 2)
    spans = rows // SPAN
    select_width = selects.shape[1]
    half = at_part

    def tile(columns, at=0):
        return pl.BlockSpec((SPAN, columns), lambda i: (spans - 1 - i, at))

    def out_tile(columns):
        return pl.BlockSpec((SPAN, columns), lambda i: (spans - 1 - i, 0))

    groups = parts // 2
    height = SPAN * (select_width // parts) // LANES
    shared = [pl.BlockSpec((height, LANES), lambda i: (spans - 1 - i, 0))] * (2 * groups)
    shared_shape = jax.ShapeDtypeStruct((spans * height, LANES), jnp.float32)
    strip = pl.BlockSpec((1, SPAN), lambda i: (0, spans - 1 - i))
    before = pl.BlockSpec(
        (EXTRA, width), lambda i: (jnp.maximum((spans - 1 - i) * (SPAN // EXTRA) - 1, 0), half)
    )
    return pl.pallas_call(
        functools.partial(
            backward_kernel,
            spans=spans,
            first_head=half * heads,
            adds=previous is not None,
            total_width=total_width,
            shared_groups=groups,
        ),
        grid=(spans,),
        in_specs=[
            scalars(),
            scalars(),
            tile(width, half),
            tile(width, half),
            tile(width, half),
            tile(width, half),
            tile(width, half),
            before,
            tile(select_width),
            tile(LANES),
            tile(LANES),
            tile(LANES),
            pl.BlockSpec((1, select_width // 2, width), lambda i: (spans - 1 - i, 0, half)),
            pl.BlockSpec((CONV, width), lambda i: (0, half)),
            pl.BlockSpec((1, width), lambda i: (0, half)),
            pl.BlockSpec((1, width), lambda i: (0, half)),
            strip,
            strip,
            fixed((1, LANES)),
            fixed((1, LANES)),
            fixed((1, LANES)),
            scalars(),
        ]
        + ([] if previous is None else shared),
        out_specs=[
            out_tile(2 * width),
            *shared,
            out_tile(LANES),
            pl.BlockSpec((1, SPAN), lambda i: (0, spans - 1 - i)),
            fixed((8, width)),
            fixed((8, LANES)),
        ],
        out_shape=[
            jax.ShapeDtypeStruct((rows, 2 * width), jnp.bfloat16),
            *[shared_shape] * (2 * groups),
            jax.ShapeDtypeStruct((rows, LANES), jnp.bfloat16),
            jax.ShapeDtypeStruct((1, rows), jnp.float32),
            jax.ShapeDtypeStruct((8, width), jnp.float32),
            jax.ShapeDtypeStruct((8, LANES), jnp.float32),
        ],
        scratch_shapes=[
            pltpu.VMEM((SPAN + EXTRA, width), jnp.float32),
            pltpu.VMEM((SPAN + EXTRA, width), jnp.float32),
            pltpu.VMEM((select_width // 2, width), jnp.float32),
            pltpu.VMEM((8, width), jnp.float32),
        ],
        compiler_params=settings(52),
        cost_estimate=guess(20000 * rows * width, 20 * rows * width, 300 * rows * width),
        name="backward",
    )(
        starts,
        fills,
        gate_pre,
        grad_scaled,
        scan,
        values,
        value_pre,
        value_pre,
        selects,
        delta,
        sums,
        step_pre,
        states,
        conv_value,
        conv_value_bias,
        gain,
        *strips,
        step_bias,
        decay_log,
        skip,
        model_place,
        *([] if previous is None else previous),
    )


def pair_kernel(*refs):
    groups = len(refs) // 3
    for index in range(groups):
        out = refs[2 * groups + index]
        out[...] = (refs[index][...] + refs[groups + index][...]).astype(out.dtype)


def run_pair(ours, came, wire):
    rows, columns = ours[0].shape
    groups = len(ours)
    tile = pl.BlockSpec((SPAN, columns), lambda i: (i, 0))
    return pl.pallas_call(
        pair_kernel,
        grid=(rows // SPAN,),
        in_specs=[tile] * (2 * groups),
        out_specs=[tile] * groups,
        out_shape=[jax.ShapeDtypeStruct((rows, columns), jnp.float32)]
        + [jax.ShapeDtypeStruct((rows, columns), wire)] * (groups - 1),
        compiler_params=settings(40),
        cost_estimate=guess(0, 0),
        name="pair",
    )(*ours, *came)


def select_kernel(starts, spot, select_pre, kernel, bias, *refs, count):
    grads, steps_in = refs[:count], refs[count:-5]
    low_out, rows_out, stat_out, ahead, unfolded = refs[-5:]
    rows, part = unfolded.shape
    folds = LANES // part
    height = SPAN // folds
    folded = grads[0][...]
    for grad in grads[1:]:
        folded = folded + grad[...]
    for span in range(rows // SPAN):
        for fold in range(folds):
            start = span * SPAN + fold * height
            unfolded[start : start + height, :] = folded[
                span * height : (span + 1) * height, fold * part : (fold + 1) * part
            ]
    upstream = unfolded[...]
    pre = select_pre[:, :part]
    taps = kernel[:, :part]
    own_bias = bias[:, :part]
    for index in range(1, select_pre.shape[1] // part):
        lanes = slice(index * part, (index + 1) * part)
        here = spot[0] == index
        pre = jnp.where(here, select_pre[:, lanes], pre)
        taps = jnp.where(here, kernel[:, lanes], taps)
        own_bias = jnp.where(here, bias[:, lanes], own_bias)
    place = iota((rows, part), 0)
    joined = jnp.zeros((rows, part), jnp.int32)
    for span in range(rows // SPAN):
        joined = jnp.where(place // SPAN == span, 1 - starts[span], joined)
    inside = place % SPAN
    stat_out[...] = jnp.zeros(stat_out.shape, jnp.float32)
    ahead[...] = jnp.zeros(ahead.shape, jnp.float32)
    ahead[EXTRA : EXTRA + rows, :] = pre
    shifted = []
    mixed = own_bias
    for back in range(CONV):
        moved = ahead[EXTRA - back : EXTRA - back + rows, :]
        moved = jnp.where(jnp.logical_or(inside >= back, joined == 1), moved, 0.0)
        shifted.append(moved)
        mixed = mixed + taps[CONV - 1 - back : CONV - back, :] * moved
    sig = sigmoid(mixed)
    inner = upstream * sig * (1.0 + mixed * (1.0 - sig))
    total = jnp.zeros((rows, part), jnp.float32)
    tap_sums = []
    for back in range(CONV):
        tap = taps[CONV - 1 - back : CONV - back, :]
        tap_sums.append(jnp.sum(inner * shifted[back], axis=0, keepdims=True))
        ahead[EXTRA : EXTRA + rows, :] = jnp.where(
            jnp.logical_or(inside >= back, joined == 1), inner, 0.0
        )
        ahead[EXTRA + rows :, :] = jnp.zeros((EXTRA, part), jnp.float32)
        total = total + tap * ahead[EXTRA + back : EXTRA + back + rows, :]
    rows_here = tap_sums[::-1] + [jnp.sum(inner, axis=0, keepdims=True)]
    for index in range(select_pre.shape[1] // part):
        lanes = slice(index * part, (index + 1) * part)
        for at, row in enumerate(rows_here):
            stat_out[at : at + 1, lanes] = jnp.where(spot[0] == index, row, 0.0)
    low = total.astype(jnp.bfloat16)
    dots = jnp.sum(low.astype(jnp.float32) * pre, axis=1, keepdims=True)
    rows_out[...] = jnp.transpose(jnp.broadcast_to(dots, (rows, LANES)))[:1, :]
    steps = steps_in[0][...].astype(jnp.float32)
    for piece in steps_in[1:]:
        steps = steps + piece[...].astype(jnp.float32)
    pieces = [steps[:, : LANES // 2], low.astype(jnp.float32)]
    if part < LANES // 2:
        pieces.append(jnp.zeros((rows, LANES // 2 - part), jnp.float32))
    low_out[...] = jnp.concatenate(pieces, axis=1).astype(jnp.bfloat16)


def run_select(starts, spot, grads, select_pre, kernel, bias, steps):
    rows = select_pre.shape[0]
    part = grads[0].shape[0] * LANES // rows
    inputs = (select_pre, kernel, bias, *grads, *steps)
    return pl.pallas_call(
        functools.partial(select_kernel, count=len(grads)),
        in_specs=[scalars(), scalars()] + [pl.BlockSpec(memory_space=pltpu.VMEM)] * len(inputs),
        out_shape=[
            jax.ShapeDtypeStruct((rows, LANES), jnp.bfloat16),
            jax.ShapeDtypeStruct((1, rows), jnp.float32),
            jax.ShapeDtypeStruct((8, select_pre.shape[1]), jnp.float32),
        ],
        scratch_shapes=[
            pltpu.VMEM((rows + 2 * EXTRA, part), jnp.float32),
            pltpu.VMEM((rows, part), jnp.float32),
        ],
        compiler_params=pltpu.CompilerParams(vmem_limit_bytes=40 << 20),
        cost_estimate=guess(0, 0),
        name="select",
    )(starts, spot, *inputs)


def spread_kernel(place, own_left, other_left, *refs):
    rights, (sends_out, own_out) = refs[:-2], refs[-2:]
    start = 0
    for own_right, other_right in zip(rights[::2], rights[1::2]):
        lanes = slice(start, start + own_right.shape[1])
        start += own_right.shape[1]
        product = dot_rows(own_left[0], own_right[...]) + dot_rows(other_left[0], other_right[...])
        sends_out[0, :, lanes] = product.astype(jnp.bfloat16)

        @pl.when(pl.program_id(0) == place[0])
        def _():
            own_out[:, lanes] = product


def run_spread(place, own_left, other_left, *rights):
    groups, rows, piece = own_left.shape
    columns = sum(right.shape[1] for right in rights[::2])
    left = pl.BlockSpec((1, rows, piece), lambda g: (g, 0, 0))
    return pl.pallas_call(
        spread_kernel,
        grid=(groups,),
        in_specs=[scalars(), left, left] + [fixed(right.shape) for right in rights],
        out_specs=[
            pl.BlockSpec((1, piece, columns), lambda g: (g, 0, 0)),
            fixed((piece, columns)),
        ],
        out_shape=[
            jax.ShapeDtypeStruct((groups, piece, columns), jnp.bfloat16),
            jax.ShapeDtypeStruct((piece, columns), jnp.float32),
        ],
        compiler_params=settings(44),
        cost_estimate=guess(0, 0),
        name="spread",
    )(place, own_left, other_left, *rights)


def pair_of(size):
    return [(spot, spot ^ 1) for spot in range(size)]


def shift_of(size, hops):
    groups = size // 2
    return [(spot, ((spot // 2 + hops) % groups) * 2 + spot % 2) for spot in range(size)]


def swap_pair(array, axis):
    return lax.ppermute(array, axis, pair_of(lax.axis_size(axis)))


def exchange_groups(sends):
    size = lax.axis_size("dp")
    groups = [[2 * group + side for group in range(size // 2)] for side in range(2)]
    return lax.all_to_all(sends, "dp", 0, 0, axis_index_groups=groups)


def send_groups(sends):
    size = lax.axis_size("dp")
    mine = lax.axis_index("dp") // 2
    arrived = []
    for hops in range(1, size // 2):
        place = (mine + hops) % (size // 2)
        piece = lax.dynamic_index_in_dim(sends, place, 0, keepdims=False)
        arrived.append(lax.ppermute(piece, "dp", shift_of(size, hops)))
    return arrived


def finish(total, arrived):
    mine = lax.axis_index("dp") // 2
    for index in range(arrived.shape[0]):
        total = total + jnp.where(index == mine, 0.0, arrived[index].astype(jnp.float32))
    return total


def send_far(pieces):
    size = lax.axis_size("mp")
    return [
        lax.ppermute(piece, "mp", shift_of(size, hops + 1)) for hops, piece in enumerate(pieces)
    ]


def features_kernel(place, *refs, groups):
    hiddens, outs, gain_out = refs[:groups], refs[-1 - groups : -1], refs[-1]
    scale, small, w_gate, w_value, w_small = refs[-6 - groups : -1 - groups]
    parts = refs[groups : -6 - groups]
    width = parts[0].shape[1] // 2
    total = dot_lanes(small[...], w_small[...])
    for index, part in enumerate(parts):
        lanes = slice(index * width, (index + 1) * width)
        total = total + dot_lanes(part[:, :width], w_gate[:, lanes])
        total = total + dot_lanes(part[:, width:], w_value[:, lanes])
    gain_out[...] = jnp.zeros(gain_out.shape, jnp.float32)
    for index, hidden in enumerate(hiddens):

        @pl.when(pl.program_id(0) == index)
        def _():
            out = outs[index]
            out[...] = total
            for start in range(0, total.shape[1], LANES):
                lanes = slice(start, start + LANES)
                pulled = out[:, lanes] * hidden[:, lanes].astype(jnp.float32) * scale[...]
                gain_out[0, 0:1, lanes] = jnp.sum(pulled, axis=0, keepdims=True)


def back_features(place, hiddens, scale, parts, small, weights, groups):
    rows = small.shape[0]
    features = weights[0].shape[0]
    piece = features // (2 * groups)
    return pl.pallas_call(
        functools.partial(features_kernel, groups=groups),
        grid_spec=pltpu.PrefetchScalarGridSpec(
            num_scalar_prefetch=1,
            grid=(groups,),
            in_specs=[resident(array.shape) for array in (*hiddens, *parts, scale, small)]
            + [
                pl.BlockSpec(
                    (piece, array.shape[1]), lambda g, at: (2 * ((at[0] + g) % groups) + at[1], 0)
                )
                for array in weights
            ],
            out_specs=[resident((rows, piece))] * groups
            + [pl.BlockSpec((1, 8, piece), lambda g, at: (g, 0, 0))],
        ),
        out_shape=[jax.ShapeDtypeStruct((rows, piece), jnp.float32)] * groups
        + [jax.ShapeDtypeStruct((groups, 8, piece), jnp.float32)],
        compiler_params=settings(52),
        cost_estimate=guess(0, 0),
        name="features",
    )(place, *hiddens, *parts, scale, small, *weights)


def sum_all(values, axis):
    size = lax.axis_size(axis)
    step = 1
    while step < size:
        values = values + lax.ppermute(values, axis, [(spot, spot ^ step) for spot in range(size)])
        step *= 2
    return values


def pack_kernel(*refs, head_dim):
    stats, smalls, gains = refs[:PARTS], refs[PARTS : 2 * PARTS], refs[2 * PARTS + 1 : -1]
    select, out, count = refs[2 * PARTS], refs[-1], PARTS
    gain = gains[0][0:1, :]
    for piece in gains[1:]:
        gain = gain + piece[0:1, :]
    width = stats[0].shape[1]
    whole = width * count
    out[...] = jnp.zeros(out.shape, jnp.float32)
    small = smalls[0][...]
    for piece in smalls[1:]:
        small = small + piece[...]
    for index, piece in enumerate(stats):
        out[:8, index * width : (index + 1) * width] = piece[...]
    heads = jnp.zeros((8, LANES), jnp.float32)
    for start in range(0, whole, LANES):
        owner = (
            iota((LANES, LANES), 1) == (start + iota((LANES, LANES), 0)) // head_dim
        ).astype(jnp.float32)
        heads = heads + exact(out[:8, start : start + LANES], owner)
    out[8:16, : select.shape[1]] = select[...]
    out[16:18, :LANES] = small[:2, :]
    out[18:19, :LANES] = heads[CONV + 1 : CONV + 2, :]
    for start in range(0, gain.shape[1], LANES):
        out[19 + start // LANES : 20 + start // LANES, :LANES] = gain[:, start : start + LANES]


def run_pack(stats, smalls, select, gains, head_dim):
    whole = stats[0].shape[1] * len(stats)
    rows = -(-(19 + gains[0].shape[1] // LANES) // 8) * 8
    return pl.pallas_call(
        functools.partial(pack_kernel, head_dim=head_dim),
        out_shape=jax.ShapeDtypeStruct((rows, whole), jnp.float32),
        cost_estimate=guess(0, 0),
        name="pack",
    )(*stats, *smalls, select, *gains)


def unpack_kernel(*refs):
    arrived, outs = refs[:-9], refs[-9:]
    total = arrived[0][...]
    for piece in arrived[1:]:
        total = total + piece[...]
    taps, bias, select, select_bias, step, decay, skip, gate_gain, gain = outs
    taps[...] = total[:CONV, :]
    bias[...] = total[CONV : CONV + 1, :]
    gate_gain[...] = total[CONV + 2 : CONV + 3, :]
    select[...] = total[8 : 8 + CONV, : select.shape[1]]
    select_bias[...] = total[8 + CONV : 9 + CONV, : select.shape[1]]
    heads = step.shape[1]
    step[...] = total[16:17, :heads]
    decay[...] = total[17:18, :heads]
    skip[...] = total[18:19, :heads]
    for start in range(0, gain.shape[1], LANES):
        gain[:, start : start + LANES] = total[19 + start // LANES : 20 + start // LANES, :LANES]


def run_unpack(arrived, select_width, heads, gain_width):
    whole = arrived[0].shape[1]
    shapes = [(CONV, whole), (1, whole), (CONV, select_width), (1, select_width)]
    shapes += [(1, heads)] * 3 + [(1, whole), (1, gain_width)]
    return pl.pallas_call(
        unpack_kernel,
        out_shape=[jax.ShapeDtypeStruct(shape, jnp.float32) for shape in shapes],
        cost_estimate=guess(0, 0),
        name="unpack",
    )(*arrived)


def sum_tokens(values):
    size = lax.axis_size("dp")
    both = values + swap_pair(values, "dp")
    return [both] + [
        lax.ppermute(both, "dp", shift_of(size, hops)) for hops in range(1, size // 2)
    ]


def widen_lanes(vector):
    return jnp.pad(vector, (0, LANES - vector.shape[0]))[None, :]


def on_device(
    hidden_in,
    cotangent,
    span_starts,
    span_fill,
    norm_gain,
    w_gate,
    w_value,
    w_select,
    w_step,
    conv_value,
    conv_value_bias,
    conv_select,
    conv_select_bias,
    step_bias,
    decay_log,
    skip_gain,
    gate_gain,
    w_out,
):
    token_rows = hidden_in.shape[0]
    model_width = norm_gain.shape[0]
    inner_cols = w_gate.shape[1]
    local_heads = w_step.shape[1]
    head_dim = inner_cols // local_heads
    select_width = w_select.shape[1]
    model_parts = lax.axis_size("mp")
    model_groups = model_parts // 2
    data_parts = lax.axis_size("dp")
    inner_total = inner_cols * model_parts
    feature_piece = model_width // model_parts
    data_piece = model_width // data_parts
    part = select_width // model_parts
    model_spot = lax.axis_index("mp")
    model_side = model_spot % 2
    data_side = (lax.axis_index("dp") % 2).reshape(1)
    offset = model_spot * feature_piece
    select_start = model_spot * part

    def after(array, *others):
        return lax.optimization_barrier((array, *others))[0]

    def gather_far(block):
        return [
            lax.ppermute(block, "mp", shift_of(model_parts, hops)) for hops in range(1, model_groups)
        ]

    def gather_near(block, far, *others):
        blocks = [block, swap_pair(block, "mp")]
        for same in far:
            same = after(same, *others) if others else same
            blocks += [same, swap_pair(same, "mp")]
        return blocks

    def theirs(block):
        pieces = []
        for index in range(0, block.shape[1] // data_piece, 2):
            first = block[:, index * data_piece : (index + 1) * data_piece]
            second = block[:, (index + 1) * data_piece : (index + 2) * data_piece]
            pieces.append(jnp.where(data_side[0] == 0, second, first))
        return pieces

    gain_row = gate_gain[None, :]
    skip_row = widen_lanes(skip_gain)
    bias_step = widen_lanes(step_bias)
    decay_row = widen_lanes(decay_log)
    half_lanes = LANES // 2
    wide_step = jnp.pad(w_step, ((0, 0), (0, LANES - local_heads)))
    spots = []
    for hops in range(model_groups):
        group = (model_spot // 2 - hops) % model_groups
        spots += [2 * group + model_side, 2 * group + 1 - model_side]
    spots = jnp.stack(spots)

    place = (lax.axis_index("dp") // 2).reshape(1)
    model_place = jnp.stack([model_spot // 2, model_side])
    other_place = jnp.stack([model_spot // 2, 1 - model_side])
    vectors = (conv_value, conv_value_bias[None, :])
    head_vectors = (bias_step, decay_row, skip_row)

    far_in = gather_far(hidden_in)
    cross = swap_pair(jnp.concatenate(theirs(hidden_in) + theirs(cotangent), axis=1), "dp")
    blocks_in = gather_near(hidden_in, far_in)
    combined = after(jnp.concatenate([cotangent, cross], axis=1), *far_in)
    far_up = gather_far(combined)

    (
        normed_own,
        scale_rows,
        scale_columns,
        value_pre,
        gate_pre,
        select_pre,
        step_pre,
        values,
        selects,
        scan,
        gated,
        delta,
        sums,
        states,
        square_part,
    ) = run_forward(
        data_side,
        spots,
        span_starts,
        span_fill,
        [after(blocks_in[0], cross)] + blocks_in[1:],
        norm_gain[None, :],
        (w_value, w_gate, w_select, wide_step),
        vectors + (conv_select, conv_select_bias[None, :]) + head_vectors,
        data_piece,
    )
    other_rows = swap_pair(scale_rows, "dp")
    blocks_up = gather_near(combined, far_up, square_part)
    squares = after(sum_all(square_part, "mp"), other_rows)
    scaled = run_scale(gated, squares, gain_row, inner_total)
    late_select, late_step = lax.optimization_barrier((w_select, w_step, scaled))[:2]
    own_select = lax.dynamic_slice_in_dim(late_select, select_start, part, 1)
    w_small = jnp.concatenate(
        [
            jnp.pad(late_step, ((0, 0), (0, half_lanes - local_heads))),
            jnp.pad(own_select, ((0, 0), (0, half_lanes - part))),
        ],
        axis=1,
    )
    scaled_other = swap_pair(scaled, "dp")
    grad_scaled, product_part, up_own, normed_other, up_other = run_cotangent(
        data_side,
        spots,
        other_rows,
        norm_gain,
        gain_row,
        w_out,
        gated,
        blocks_up,
        data_piece,
    )
    products = sum_all(product_part, "mp")

    def backward(index, products, previous):
        return run_backward(
            span_starts,
            span_fill,
            (gate_pre, grad_scaled, scan, values, value_pre, selects, delta, sums, step_pre),
            (squares, products),
            states,
            vectors + (gain_row,) + head_vectors,
            model_parts,
            index,
            model_place,
            previous,
            inner_total,
        )

    parts, others, stats, smalls, steps, row_dots = [], [], [], [], [], []
    own_parts, out_parts = [], []
    previous = None
    gate = products
    last_other, last_out = scaled_other, None
    for index in range(PARTS):
        part_grads, *previous, step, rows, stat, small = backward(index, gate, previous)
        if index == 0:
            lefts, right = (up_own, up_other), scaled
        else:
            lefts, right = (normed_own, normed_other), parts[index - 1]
        if index == 1:
            mixed = run_mixed(model_place, after(scaled, sends), w_out, model_groups)
            mixed_came = [swap_pair(piece, "mp") for piece in mixed[:model_groups]]
            arrived = after(last_other, part_grads, mixed[0])
        else:
            arrived = after(last_other, part_grads)
        last_other = swap_pair(after(part_grads, arrived), "dp")
        sends, own = run_spread(place, *lefts, right, arrived)
        if index == 0:
            last_out = send_groups(sends)
        else:
            waited = last_out if index == 1 else [last_out]
            last_out = exchange_groups(after(sends, *waited))
        own_parts.append(own)
        out_parts.append(last_out)
        gate = after(products, sends)
        parts.append(part_grads)
        others.append(last_other)
        steps.append(step)
        row_dots.append(rows)
        stats.append(stat)
        smalls.append(small)
    own_out, out_out = own_parts.pop(0), out_parts.pop(0)

    mixed_total, *mixed_pieces = run_pair(
        mixed[model_groups:], [after(mixed_came[0], sends)] + mixed_came[1:], jnp.float32
    )
    came = [swap_pair(after(piece, others[-2]), "mp") for piece in previous[:model_groups]]
    select_total, *select_pieces = run_pair(
        previous[model_groups:], [after(came[0], mixed_total)] + came[1:], jnp.float32
    )
    select_arrived = send_far(select_pieces)
    mixed_arrived = send_far([after(piece, *select_arrived) for piece in mixed_pieces])
    small_low, select_rows, select_stats = run_select(
        span_starts,
        model_spot.reshape(1),
        [select_total] + select_arrived,
        select_pre,
        conv_select,
        conv_select_bias[None, :],
        steps,
    )
    select_sums = sum_all(select_stats, "mp")
    row_total = select_rows
    for rows in row_dots:
        row_total = row_total + rows
    norm_rows = sum_all(row_total, "mp")
    weights = (w_gate, w_value, w_small)
    hiddens = [
        [blocks_in[2 * ((model_groups - group) % model_groups) + side] for group in range(model_groups)]
        for side in range(2)
    ]
    *back_theirs, gain_theirs = back_features(
        other_place,
        hiddens[1],
        scale_columns,
        parts,
        small_low,
        weights,
        model_groups,
    )
    last_arrived = after(others[-1], back_theirs[0])
    small_other = swap_pair(after(small_low, last_arrived), "dp")
    back_came = [swap_pair(after(piece, last_arrived), "mp") for piece in back_theirs]
    sends_last, own_last = run_spread(
        place, normed_own, normed_other, parts[-1], last_arrived, small_low, small_other
    )
    out_last = exchange_groups(after(sends_last, last_out))
    *back_ours, gain_ours = back_features(
        model_place,
        hiddens[0],
        scale_columns,
        parts,
        after(small_low, sends_last, *mixed_arrived),
        weights,
        model_groups,
    )
    back_total, *back_pieces = run_pair(
        back_ours, [after(back_came[0], *mixed_arrived)] + back_came[1:], jnp.bfloat16
    )
    gain_both = gain_ours + swap_pair(gain_theirs, "mp")
    gain_sums = [gain_both[0]] + send_far([gain_both[hops] for hops in range(1, model_groups)])
    back_pieces = [after(piece, *gain_sums, select_sums, norm_rows) for piece in back_pieces]
    back_arrived = send_far(back_pieces)
    own_parts.append(own_last)
    out_parts.append(out_last)
    for index in range(PARTS):
        out_parts[index] = after(out_parts[index], *back_pieces)
    out_out = [after(piece, *back_pieces) for piece in out_out]

    grad_normed = back_total
    for piece in back_arrived:
        grad_normed = grad_normed + piece.astype(jnp.float32)
    own_in = hidden_in.astype(jnp.float32)
    mixed_share = mixed_total
    for piece in mixed_arrived:
        mixed_share = mixed_share + piece
    output = (own_in + mixed_share).astype(jnp.bfloat16)
    own_gain = lax.dynamic_slice_in_dim(norm_gain, offset, feature_piece, 0)
    own_scale = scale_columns[:, :1]
    weighted_in = grad_normed * own_gain[None, :]
    grad_hidden_in = (
        cotangent.astype(jnp.float32)
        + weighted_in * own_scale
        - own_in * own_scale**2 * norm_rows[0][:, None] / model_width
    )
    packed = run_pack(stats, smalls, select_sums, gain_sums, head_dim)
    small_sums = sum_tokens(after(packed, *back_pieces))
    grad_w_out = own_out
    for piece in out_out:
        grad_w_out = grad_w_out + piece.astype(jnp.float32)
    grad_w_out = grad_w_out.T
    done = [finish(own, out) for own, out in zip(own_parts, out_parts)]
    width = inner_cols // PARTS
    grad_w_gate = jnp.concatenate([piece[:, :width] for piece in done], axis=1)
    grad_w_value = jnp.concatenate([piece[:, width : 2 * width] for piece in done], axis=1)
    grad_w_small = done[-1][:, 2 * width :]
    grad_w_step = grad_w_small[:, :local_heads]
    grad_w_select = lax.all_gather(
        grad_w_small[:, half_lanes : half_lanes + part], "mp", axis=1, tiled=True
    )
    (
        grad_taps,
        grad_bias,
        grad_select_taps,
        grad_select_bias,
        grad_step_bias,
        grad_decay_log,
        grad_skip_gain,
        grad_gate_gain,
        gain_sum,
    ) = run_unpack(
        [after(small_sums[0], grad_w_select)] + small_sums[1:], select_width, local_heads, feature_piece
    )
    return (
        output,
        grad_hidden_in,
        gain_sum[0],
        grad_w_gate,
        grad_w_value,
        grad_w_select,
        grad_w_step,
        grad_taps,
        grad_bias[0],
        grad_select_taps,
        grad_select_bias[0],
        grad_step_bias[0],
        grad_decay_log[0],
        grad_skip_gain[0],
        grad_gate_gain[0],
        grad_w_out,
    )


def solution(mesh):
    in_specs = (
        P("dp", "mp"),
        P("dp", "mp"),
        P("dp"),
        P("dp"),
        P(),
        P(None, "mp"),
        P(None, "mp"),
        P(),
        P(None, "mp"),
        P(None, "mp"),
        P("mp"),
        P(),
        P(),
        P("mp"),
        P("mp"),
        P("mp"),
        P("mp"),
        P("mp", None),
    )
    out_specs = (
        P("dp", "mp"),
        P("dp", "mp"),
        P("mp"),
        P("dp", "mp"),
        P("dp", "mp"),
        P("dp", None),
        P("dp", "mp"),
        P(None, "mp"),
        P("mp"),
        P(),
        P(),
        P("mp"),
        P("mp"),
        P("mp"),
        P("mp"),
        P("mp", "dp"),
    )
    return jax.shard_map(
        on_device, mesh=mesh, in_specs=in_specs, out_specs=out_specs, check_vma=False
    )
```

```python
import functools

import jax
import jax.numpy as jnp
from jax import lax
from jax.experimental import pallas as pl
from jax.experimental.pallas import tpu as pltpu
from jax.sharding import PartitionSpec as P

CONV = 4
SPAN = 256
LANES = 128
EXTRA = 8
TOP = 15.0
FAR = -1e30
PARTS = 2
epsilon = 1e-05
exact_mode = lax.Precision.HIGHEST


def settings(mebibytes, axes=1):
    return pltpu.CompilerParams(
        dimension_semantics=("arbitrary",) * axes, vmem_limit_bytes=mebibytes << 20
    )


def scalars():
    return pl.BlockSpec(memory_space=pltpu.SMEM)


def fixed(shape):
    return pl.BlockSpec(shape, lambda *_: (0,) * len(shape))


def split_bits(value):
    high = value.astype(jnp.bfloat16)
    low = (value - high.astype(jnp.float32)).astype(jnp.bfloat16)
    return high, low


def dot(left, right):
    return lax.dot_general(left, right, (((1,), (0,)), ((), ())), preferred_element_type=jnp.float32)


def dot_lanes(left, right):
    return lax.dot_general(left, right, (((1,), (1,)), ((), ())), preferred_element_type=jnp.float32)


def dot_rows(left, right):
    return lax.dot_general(left, right, (((0,), (0,)), ((), ())), preferred_element_type=jnp.float32)


def exact(left, right):
    return jnp.dot(left, right, precision=exact_mode, preferred_element_type=jnp.float32)


def beside(*pieces):
    return jnp.concatenate(pieces, axis=1)


def above(*pieces):
    return jnp.concatenate(pieces, axis=0)


def sigmoid(value):
    return 1.0 / (1.0 + jnp.exp(-value))


def iota(shape, axis):
    return lax.broadcasted_iota(jnp.int32, shape, axis)


def two_heads(columns, pair, in_first):
    first = columns[:, 2 * pair : 2 * pair + 1]
    second = columns[:, 2 * pair + 1 : 2 * pair + 2]
    return jnp.where(in_first, first, second)


def row_of(columns):
    return jnp.sum(jnp.transpose(columns), axis=0, keepdims=True)


def live_rows(fill, width):
    return (iota((SPAN, width), 0) < fill).astype(jnp.float32)


def wide_lanes(start, width):
    return pl.ds(pl.multiple_of(start * width, min(width, LANES)), width)


def store_ours(side, block, spot, ours_out, piece):
    for index in range(block.shape[1] // (2 * piece)):
        first = block[:, 2 * index * piece : (2 * index + 1) * piece]
        second = block[:, (2 * index + 1) * piece : (2 * index + 2) * piece]
        group = spot * (block.shape[1] // (2 * piece)) + index
        ours_out[pl.ds(group, 1)] = jnp.where(side == 0, first, second)[None]


def guess(flops, moved, exps=0):
    return pl.CostEstimate(flops=1, bytes_accessed=1, transcendentals=0)


def conv_of(extended, kernel, bias, lanes):
    total = bias[:, lanes]
    for back in range(CONV):
        tap = kernel[CONV - 1 - back : CONV - back, lanes]
        total = total + tap * extended[EXTRA - back : EXTRA - back + SPAN, lanes]
    return total


def forward_kernel(
    side,
    spots,
    starts,
    fills,
    norm_gain,
    w_value,
    w_gate,
    w_select,
    w_step,
    conv_value,
    conv_value_bias,
    conv_select,
    conv_select_bias,
    step_bias,
    decay_log,
    skip,
    *refs,
    piece,
):
    blocks = refs[:-19]
    (
        ours_out,
        scale_out,
        scale_columns_out,
        value_pre,
        gate_pre,
        select_pre,
        step_pre,
        values_out,
        selects_out,
        scan_out,
        gated_out,
        delta_out,
        sum_out,
        state_out,
        rows_out,
        extended,
        extended_select,
        state,
        whole,
    ) = refs[-19:]
    step = pl.program_id(0)
    fresh = starts[step] == 1
    width = value_pre.shape[1]
    state_dim = select_pre.shape[1] // 2

    part_width = blocks[0].shape[1]
    total = jnp.zeros((SPAN, LANES), jnp.float32)
    for block in blocks:
        for start in range(0, part_width, LANES):
            part = block[:, start : start + LANES].astype(jnp.float32)
            total = total + part * part
    mean = jnp.sum(total, axis=1, keepdims=True) / (part_width * len(blocks))
    scale = lax.rsqrt(mean + epsilon)
    scale_columns_out[...] = jnp.broadcast_to(scale, (SPAN, LANES))
    scale_out[...] = jnp.transpose(scale_columns_out[...])[:1, :]
    for index, block in enumerate(blocks):
        spot = spots[index]
        window = wide_lanes(spot, part_width)
        own_gain = norm_gain[:, window]
        normed = (block[...].astype(jnp.float32) * scale * own_gain).astype(jnp.bfloat16)
        store_ours(side[0], normed, spot, ours_out, piece)
        whole[:, window] = normed
    for out, weights in (
        (select_pre, w_select),
        (step_pre, w_step),
        (value_pre, w_value),
        (gate_pre, w_gate),
    ):
        out[...] = dot(whole[...], weights[...])

    @pl.when(fresh)
    def _():
        extended[:EXTRA, :] = jnp.zeros((EXTRA, width), jnp.float32)
        extended_select[:EXTRA, :] = jnp.zeros((EXTRA, 2 * state_dim), jnp.float32)
        state[...] = jnp.zeros(state.shape, jnp.float32)

    @pl.when(jnp.logical_not(fresh))
    def _():
        extended[:EXTRA, :] = extended[SPAN:, :]
        extended_select[:EXTRA, :] = extended_select[SPAN:, :]

    extended[EXTRA:, :] = value_pre[...]
    extended_select[EXTRA:, :] = select_pre[...]
    state_out[0] = state[...]

    live = live_rows(fills[step], LANES)
    pre_step = step_pre[...] + step_bias[...]
    delta = live * (jnp.maximum(pre_step, 0.0) + jnp.log1p(jnp.exp(-jnp.abs(pre_step))))
    rate = -jnp.exp(decay_log[...])
    lower = (iota((SPAN, SPAN), 0) >= iota((SPAN, SPAN), 1)).astype(jnp.float32)
    cumulative = exact(lower, delta * rate)
    delta_out[...] = delta
    sum_out[...] = cumulative
    sums_across = jnp.transpose(cumulative)
    delta_across = jnp.transpose(delta)
    grown = jnp.exp(cumulative)
    tail = delta * jnp.exp(cumulative[SPAN - 1 : SPAN, :] - cumulative)

    halves = []
    for half in range(2):
        lanes = slice(half * state_dim, (half + 1) * state_dim)
        mixed = conv_of(extended_select, conv_select, conv_select_bias, lanes)
        chosen = (mixed * sigmoid(mixed)).astype(jnp.bfloat16)
        selects_out[:, lanes] = chosen
        halves.append(chosen)
    inflow, readout = halves
    inflow_across = jnp.transpose(inflow.astype(jnp.float32)).astype(jnp.bfloat16)
    scores = dot_lanes(readout, inflow)
    middle = SPAN // 2
    past = iota((middle, middle), 0) >= iota((middle, middle), 1)
    later_past = iota((middle, SPAN), 0) + middle >= iota((middle, SPAN), 1)
    in_first = iota((SPAN, LANES), 1) < LANES // 2
    row_first = iota((1, LANES), 1) < LANES // 2
    readout_twice = beside(readout, readout)
    squares = jnp.zeros((SPAN, LANES), jnp.float32)
    for pair in range(width // LANES):
        lanes = slice(pair * LANES, (pair + 1) * LANES)
        mixed = conv_of(extended, conv_value, conv_value_bias, lanes)
        value_low = (mixed * sigmoid(mixed)).astype(jnp.bfloat16)
        values_out[:, lanes] = value_low
        value = value_low.astype(jnp.float32)
        entering = state[:, lanes]
        scan = dot(readout_twice, above(*split_bits(entering))) * two_heads(grown, pair, in_first)
        scan = scan + two_heads(skip[...], pair, row_first) * value
        for which in range(2):
            head = 2 * pair + which
            own = jnp.where(in_first == (which == 0), value_low, jnp.zeros_like(value_low))
            sums_row = sums_across[head : head + 1, :]
            delta_row = delta_across[head : head + 1, :]
            gaps = cumulative[:middle, head : head + 1] - sums_row[:, :middle]
            weights = jnp.exp(jnp.where(past, gaps, FAR))
            high, low = split_bits(scores[:middle, :middle] * weights * delta_row[:, :middle])
            early = dot(high, own[:middle]) + dot(low, own[:middle])
            gaps = cumulative[middle:, head : head + 1] - sums_row
            weights = jnp.exp(jnp.where(later_past, gaps, FAR))
            high, low = split_bits(scores[middle:] * weights * delta_row)
            scan = scan + above(early, dot(high, own) + dot(low, own))
        scan_out[:, lanes] = scan
        gate = gate_pre[:, lanes]
        gated = live * scan * gate * sigmoid(gate)
        squares = squares + gated * gated
        gated_out[:, lanes] = gated
        weighted = value * two_heads(tail, pair, in_first)
        high, low = split_bits(weighted)
        last = two_heads(grown[SPAN - 1 : SPAN, :], pair, row_first)
        state[:, lanes] = entering * last + dot(inflow_across, high) + dot(inflow_across, low)
    rows_out[...] = row_of(squares)


def resident(shape):
    return pl.BlockSpec(shape, lambda *_: (0,) * len(shape), pipeline_mode=pl.Buffered(1))


def run_forward(side, spots, starts, fills, blocks, gain, weights, vectors, piece):
    rows, part_width = blocks[0].shape
    groups = part_width * len(blocks) // (2 * piece)
    w_value, w_gate, w_select, w_step = weights
    width = w_value.shape[1]
    spans = rows // SPAN
    select_width = w_select.shape[1]

    def tile(columns):
        return pl.BlockSpec((SPAN, columns), lambda i: (i, 0))

    def like(columns, dtype):
        return jax.ShapeDtypeStruct((rows, columns), dtype)

    strip = pl.BlockSpec((1, SPAN), lambda i: (0, i))
    return pl.pallas_call(
        functools.partial(forward_kernel, piece=piece),
        grid=(spans,),
        in_specs=[scalars()] * 4
        + [fixed(gain.shape)]
        + [resident(array.shape) for array in weights]
        + [fixed(array.shape) for array in vectors]
        + [tile(part_width)] * len(blocks),
        out_specs=[
            pl.BlockSpec((groups, SPAN, piece), lambda i: (0, i, 0)),
            strip,
            tile(LANES),
            tile(width),
            tile(width),
            tile(select_width),
            tile(LANES),
            tile(width),
            tile(select_width),
            tile(width),
            tile(width),
            tile(LANES),
            tile(LANES),
            pl.BlockSpec((1, select_width // 2, width), lambda i: (i, 0, 0)),
            strip,
        ],
        out_shape=[
            jax.ShapeDtypeStruct((groups, rows, piece), jnp.bfloat16),
            jax.ShapeDtypeStruct((1, rows), jnp.float32),
            like(LANES, jnp.float32),
            like(width, jnp.float32),
            like(width, jnp.float32),
            like(select_width, jnp.float32),
            like(LANES, jnp.float32),
            like(width, jnp.bfloat16),
            like(select_width, jnp.bfloat16),
            like(width, jnp.float32),
            like(width, jnp.float32),
            like(LANES, jnp.float32),
            like(LANES, jnp.float32),
            jax.ShapeDtypeStruct((spans, select_width // 2, width), jnp.float32),
            jax.ShapeDtypeStruct((1, rows), jnp.float32),
        ],
        scratch_shapes=[
            pltpu.VMEM((SPAN + EXTRA, width), jnp.float32),
            pltpu.VMEM((SPAN + EXTRA, select_width), jnp.float32),
            pltpu.VMEM((select_width // 2, width), jnp.float32),
            pltpu.VMEM((SPAN, part_width * len(blocks)), jnp.bfloat16),
        ],
        compiler_params=settings(50),
        cost_estimate=guess(0, 0),
        name="forward",
    )(side, spots, starts, fills, gain, *weights, *vectors, *blocks)


def scale_column(rows, total_width):
    turned = jnp.transpose(above(rows[...], jnp.zeros((LANES - 1, SPAN), jnp.float32)))
    return lax.rsqrt(turned[:, 0:1] / total_width + epsilon)


def scale_kernel(gated_in, squares, gain, scaled_out, *, total_width):
    width = gated_in.shape[1]
    scale = jnp.broadcast_to(scale_column(squares, total_width), (SPAN, LANES))
    for start in range(0, width, LANES):
        lanes = slice(start, start + LANES)
        scaled_out[:, lanes] = (gated_in[:, lanes] * scale * gain[:, lanes]).astype(jnp.bfloat16)


def run_scale(gated, squares, gain, total_width):
    rows, width = gated.shape
    return pl.pallas_call(
        functools.partial(scale_kernel, total_width=total_width),
        grid=(rows // SPAN,),
        in_specs=[
            pl.BlockSpec((SPAN, width), lambda i: (i, 0)),
            pl.BlockSpec((1, SPAN), lambda i: (0, i)),
            fixed((1, width)),
        ],
        out_specs=pl.BlockSpec((SPAN, width), lambda i: (i, 0)),
        out_shape=jax.ShapeDtypeStruct((rows, width), jnp.bfloat16),
        compiler_params=settings(32),
        cost_estimate=guess(6 * rows * width, 6 * rows * width),
        name="scale",
    )(gated, squares, gain)


def cotangent_kernel(
    side, spots, rows, norm_gain, gain, w_out, gated_in, *refs, piece
):
    blocks = refs[:-5]
    grad_out, rows_out, ours_out, other_normed_out, other_out = refs[-5:]
    width = blocks[0].shape[1] // 2
    cross = width // 2
    turned = jnp.transpose(above(rows[...], jnp.zeros((LANES - 1, SPAN), jnp.float32)))
    scale = turned[:, 0:1]
    each = cross // piece
    total = None
    for index, block in enumerate(blocks):
        spot = spots[index]
        upstream = block[:, :width]
        product = dot_lanes(upstream, w_out[:, wide_lanes(spot, width)])
        total = product if index == 0 else total + product
        store_ours(side[0], upstream, spot, ours_out, piece)
        for inner in range(each):
            group = spot * each + inner
            own_gain = norm_gain[pl.ds(2 * group + side[0], 1), :]
            start = width + inner * piece
            hidden = block[:, start : start + piece].astype(jnp.float32)
            other_normed_out[pl.ds(group, 1)] = (hidden * scale * own_gain).astype(jnp.bfloat16)[None]
            start = width + cross + inner * piece
            other_out[pl.ds(group, 1)] = block[:, start : start + piece][None]
    grad_out[...] = total
    products = jnp.zeros((SPAN, LANES), jnp.float32)
    for start in range(0, gated_in.shape[1], LANES):
        lanes = slice(start, start + LANES)
        products = products + grad_out[:, lanes] * gain[:, lanes] * gated_in[:, lanes]
    rows_out[...] = row_of(products)


def run_cotangent(side, spots, rows_in, norm_gain, gain, w_out, gated, blocks, piece):
    rows, width = gated.shape
    features = w_out.shape[1]
    groups = features // (2 * piece)
    strip = pl.BlockSpec((1, SPAN), lambda i: (0, i))

    def tile(columns):
        return pl.BlockSpec((SPAN, columns), lambda i: (i, 0))

    pieces = pl.BlockSpec((groups, SPAN, piece), lambda i: (0, i, 0))
    pieces_shape = jax.ShapeDtypeStruct((groups, rows, piece), jnp.bfloat16)
    return pl.pallas_call(
        functools.partial(cotangent_kernel, piece=piece),
        grid=(rows // SPAN,),
        in_specs=[
            scalars(),
            scalars(),
            strip,
            fixed((2 * groups, piece)),
            fixed(gain.shape),
            resident(w_out.shape),
            tile(width),
        ]
        + [tile(block.shape[1]) for block in blocks],
        out_specs=[tile(width), strip, pieces, pieces, pieces],
        out_shape=[
            jax.ShapeDtypeStruct((rows, width), jnp.float32),
            jax.ShapeDtypeStruct((1, rows), jnp.float32),
            pieces_shape,
            pieces_shape,
            pieces_shape,
        ],
        compiler_params=settings(48),
        cost_estimate=guess(0, 0),
        name="cotangent",
    )(
        side,
        spots,
        rows_in,
        norm_gain.reshape(2 * groups, piece),
        gain,
        w_out,
        gated,
        *blocks,
    )


def mixed_kernel(place, scaled, w_out, *outs):
    product = dot(scaled[...], w_out[...])
    for index, out in enumerate(outs):

        @pl.when(pl.program_id(0) == index)
        def _():
            out[...] = product


def run_mixed(place, scaled, w_out, groups):
    rows, width = scaled.shape
    piece = w_out.shape[1] // (2 * groups)

    def column(g, at):
        side = jnp.where(g < groups, 1 - at[1], at[1])
        return 0, 2 * ((at[0] + g) % groups) + side

    return pl.pallas_call(
        mixed_kernel,
        grid_spec=pltpu.PrefetchScalarGridSpec(
            num_scalar_prefetch=1,
            grid=(2 * groups,),
            in_specs=[resident((rows, width)), pl.BlockSpec((width, piece), column)],
            out_specs=[resident((rows, piece))] * (2 * groups),
        ),
        out_shape=[jax.ShapeDtypeStruct((rows, piece), jnp.float32)] * (2 * groups),
        compiler_params=settings(40),
        cost_estimate=guess(0, 0),
        name="mixed",
    )(place, scaled, w_out)


def backward_kernel(
    starts,
    fills,
    gate_pre,
    grad_scaled,
    scan_in,
    values_in,
    value_pre,
    value_before,
    selects_in,
    delta_in,
    sum_in,
    step_pre,
    state_in,
    conv_value,
    conv_value_bias,
    gain,
    squares,
    products,
    step_bias,
    decay_log,
    skip,
    model_place,
    *rest,
    spans,
    first_head,
    adds,
    total_width,
    shared_groups,
):
    groups = shared_groups
    if adds:
        before, rest = rest[: 2 * groups], rest[2 * groups :]
    value_out, shared_outs, rest = rest[0], rest[1 : 1 + 2 * groups], rest[1 + 2 * groups :]
    (
        step_out,
        rows_out,
        stat_out,
        small_out,
        extended,
        shifted,
        state,
        carried,
    ) = rest
    step = pl.program_id(0)
    span = spans - 1 - step
    width = values_in.shape[1]
    state_dim = selects_in.shape[1] // 2
    following = jnp.minimum(span + 1, spans - 1)
    joined = jnp.logical_and(step > 0, starts[following] == 0)

    @pl.when(jnp.logical_not(joined))
    def _():
        shifted[SPAN:, :] = jnp.zeros((EXTRA, width), jnp.float32)
        state[...] = jnp.zeros(state.shape, jnp.float32)
        carried[...] = jnp.zeros(carried.shape, jnp.float32)

    @pl.when(joined)
    def _():
        shifted[SPAN:, :] = shifted[:EXTRA, :]

    @pl.when(step == 0)
    def _():
        stat_out[...] = jnp.zeros(stat_out.shape, jnp.float32)
        small_out[...] = jnp.zeros(small_out.shape, jnp.float32)

    fresh = starts[span] == 1

    @pl.when(fresh)
    def _():
        extended[:EXTRA, :] = jnp.zeros((EXTRA, width), jnp.float32)

    @pl.when(jnp.logical_not(fresh))
    def _():
        extended[:EXTRA, :] = value_before[...]

    extended[EXTRA:, :] = value_pre[...]

    delta = delta_in[...]
    cumulative = sum_in[...]
    sums_across = jnp.transpose(cumulative)
    grown = jnp.exp(cumulative)
    tail = jnp.exp(cumulative[SPAN - 1 : SPAN, :] - cumulative)
    delta_tail = delta * tail
    inflow = selects_in[:, :state_dim]
    readout = selects_in[:, state_dim:]
    readout_across = jnp.transpose(readout.astype(jnp.float32)).astype(jnp.bfloat16)
    scores = dot_lanes(inflow, readout)
    ahead = iota((SPAN, SPAN), 1) >= iota((SPAN, SPAN), 0)
    in_first = iota((SPAN, LANES), 1) < LANES // 2
    row_first = iota((1, LANES), 1) < LANES // 2
    live = live_rows(fills[span], LANES)
    turned = jnp.transpose(above(products[...], jnp.zeros((LANES - 1, SPAN), jnp.float32)))
    norm_scale = scale_column(squares, total_width)
    norm_pull = norm_scale * norm_scale * norm_scale * turned[:, 0:1] / total_width
    norm_scale = jnp.broadcast_to(norm_scale, (SPAN, LANES))
    norm_pull = jnp.broadcast_to(norm_pull, (SPAN, LANES))
    inflow_twice = beside(inflow, inflow)
    grad_scores = jnp.zeros((SPAN, SPAN), jnp.float32)
    grad_inflow = jnp.zeros((SPAN, state_dim), jnp.float32)
    grad_readout = jnp.zeros((SPAN, state_dim), jnp.float32)
    change = jnp.zeros((SPAN, LANES), jnp.float32)
    direct = jnp.zeros((SPAN, LANES), jnp.float32)
    jump = jnp.zeros((8, LANES), jnp.float32)
    dots = jnp.zeros((SPAN, LANES), jnp.float32)
    for own_pair in range(width // LANES):
        lanes = slice(own_pair * LANES, (own_pair + 1) * LANES)
        pair = first_head // 2 + own_pair
        gate = gate_pre[:, lanes]
        scan = scan_in[:, lanes]
        before_norm = grad_scaled[:, lanes]
        own_gain = gain[:, lanes]
        sig = sigmoid(gate)
        opened = live * gate * sig
        gated = scan * opened
        grad_gated = before_norm * own_gain * norm_scale - gated * norm_pull
        grad_gate = grad_gated * live * scan * sig * (1.0 + gate * (1.0 - sig))
        gate_low = grad_gate.astype(jnp.bfloat16)
        value_out[:, lanes] = gate_low
        dots = dots + gate_low.astype(jnp.float32) * gate
        stat_out[CONV + 2 : CONV + 3, lanes] += jnp.sum(
            before_norm * gated * norm_scale, axis=0, keepdims=True
        )
        upstream = grad_gated * opened
        up_high, up_low = split_bits(upstream)
        value_low = values_in[:, lanes]
        value = value_low.astype(jnp.float32)
        own_skip = two_heads(skip[...], pair, row_first)
        arriving = state[:, lanes]
        arriving_high, arriving_low = split_bits(arriving)
        entering = state_in[0, :, lanes]
        entering_high, entering_low = split_bits(entering)
        pulled = dot(inflow_twice, above(arriving_high, arriving_low)) * two_heads(tail, pair, in_first)
        up_both = beside(up_high, up_low)
        for which in range(2):
            head = 2 * pair + which
            mine = in_first == (which == 0)
            nothing = jnp.zeros_like(value_low)
            gaps = sums_across[head : head + 1, :] - cumulative[:, head : head + 1]
            weights = jnp.exp(jnp.where(ahead, gaps, FAR))
            high, low = split_bits(scores * weights)
            own_high = jnp.where(mine, up_high, nothing)
            own_low = jnp.where(mine, up_low, nothing)
            pulled = pulled + dot(high, own_high) + dot(high, own_low) + dot(low, own_high)
            own_value = jnp.where(mine, value_low, nothing)
            outer = dot_lanes(beside(own_value, own_value), up_both)
            grad_scores = grad_scores + outer * weights * delta[:, head : head + 1]
        delta_both = two_heads(delta, pair, in_first)
        grad_value = own_skip * upstream + delta_both * pulled
        pull_value = value * pulled
        spread = (
            iota((LANES, LANES), 1) == 2 * pair + iota((LANES, LANES), 0) // (LANES // 2)
        ).astype(jnp.bfloat16)
        spread_twice = above(spread, spread)
        moved = upstream * (scan - own_skip * value) - delta_both * pull_value
        change = change + dot(beside(*split_bits(moved)), spread_twice)
        direct = direct + dot(beside(*split_bits(pull_value)), spread_twice)
        grown_up = upstream * two_heads(grown, pair, in_first)
        high, low = split_bits(grown_up)
        grad_readout = grad_readout + dot_lanes(
            beside(high, low, high), beside(entering_high, entering_high, entering_low)
        )
        last = two_heads(grown[SPAN - 1 : SPAN, :], pair, row_first)
        leaving = arriving * last + dot(readout_across, high) + dot(readout_across, low)
        tail_value = value * two_heads(delta_tail, pair, in_first)
        high, low = split_bits(tail_value)
        grad_inflow = grad_inflow + dot_lanes(
            beside(high, low, high), beside(arriving_high, arriving_high, arriving_low)
        )
        jump = jump + exact(carried[:, lanes], spread.astype(jnp.float32))
        state[:, lanes] = leaving
        carried[:, lanes] = jnp.broadcast_to(
            jnp.sum(leaving * entering, axis=0, keepdims=True), (8, LANES)
        )
        mixed = conv_of(extended, conv_value, conv_value_bias, lanes)
        sig = sigmoid(mixed)
        inner = grad_value * sig * (1.0 + mixed * (1.0 - sig))
        shifted[:SPAN, lanes] = inner
        grad_pre = jnp.zeros((SPAN, LANES), jnp.float32)
        for back in range(CONV):
            tap = conv_value[CONV - 1 - back : CONV - back, lanes]
            grad_pre = grad_pre + tap * shifted[back : back + SPAN, lanes]
            stat_out[CONV - 1 - back : CONV - back, lanes] += jnp.sum(
                inner * extended[EXTRA - back : EXTRA - back + SPAN, lanes], axis=0, keepdims=True
            )
        stat_out[CONV : CONV + 1, lanes] += jnp.sum(inner, axis=0, keepdims=True)
        stat_out[CONV + 1 : CONV + 2, lanes] += jnp.sum(value * upstream, axis=0, keepdims=True)
        grad_low = grad_pre.astype(jnp.bfloat16)
        value_out[:, width + own_pair * LANES : width + (own_pair + 1) * LANES] = grad_low
        wide = grad_low.astype(jnp.float32)
        dots = dots + wide * extended[EXTRA:, lanes]
    high, low = split_bits(grad_scores)
    grad_inflow = grad_inflow + dot(high, readout) + dot(low, readout)
    high, low = split_bits(jnp.transpose(grad_scores))
    grad_readout = grad_readout + dot(high, inflow) + dot(low, inflow)
    part = 2 * state_dim // (2 * groups)
    folds = LANES // part
    height = SPAN // folds
    both = (grad_inflow, grad_readout)
    for hops in range(groups):
        for side in range(2):
            chosen = None
            for index in range(2 * groups):
                start = index * part
                piece = both[start // state_dim][:, start % state_dim : start % state_dim + part]
                here = jnp.logical_and(
                    lax.rem(model_place[0] + hops, groups) == index // 2,
                    jnp.where(model_place[1] == index % 2, 1, 0) == side,
                )
                chosen = piece if chosen is None else jnp.where(here, piece, chosen)
            chosen = beside(*[chosen[fold * height : (fold + 1) * height] for fold in range(folds)])
            at = side * groups + hops
            shared_outs[at][...] = chosen + before[at][...] if adds else chosen
    upper = (iota((SPAN, SPAN), 1) >= iota((SPAN, SPAN), 0)).astype(jnp.float32)
    flow = exact(upper, change) + jump[0:1, :]
    rate = -jnp.exp(decay_log[...])
    grad_delta = direct + rate * flow
    pre_step = step_pre[...]
    grad_step = grad_delta * live * sigmoid(pre_step + step_bias[...])
    column = iota((SPAN, LANES), 1)
    last_head = first_head + width // (LANES // 2)
    grad_step = jnp.where(jnp.logical_and(column >= first_head, column < last_head), grad_step, 0.0)
    step_low = grad_step.astype(jnp.bfloat16)
    step_out[...] = step_low
    wide = step_low.astype(jnp.float32)
    dots = dots + wide * pre_step
    small_out[0:1, :] += jnp.sum(grad_step, axis=0, keepdims=True)
    small_out[1:2, :] += rate * jnp.sum(delta * flow, axis=0, keepdims=True)
    rows_out[...] = row_of(dots)


def run_backward(
    starts, fills, tiles, strips, states, vectors, parts, at_part, model_place, previous, total_width
):
    gate_pre, grad_scaled, scan, values, value_pre, selects, delta, sums, step_pre = tiles
    conv_value, conv_value_bias, gain, step_bias, decay_log, skip = vectors
    rows, whole = value_pre.shape
    width = whole // PARTS
    heads = width // (LANES // 2)
    spans = rows // SPAN
    select_width = selects.shape[1]
    half = at_part

    def tile(columns, at=0):
        return pl.BlockSpec((SPAN, columns), lambda i: (spans - 1 - i, at))

    def out_tile(columns):
        return pl.BlockSpec((SPAN, columns), lambda i: (spans - 1 - i, 0))

    groups = parts // 2
    height = SPAN * (select_width // parts) // LANES
    shared = [pl.BlockSpec((height, LANES), lambda i: (spans - 1 - i, 0))] * (2 * groups)
    shared_shape = jax.ShapeDtypeStruct((spans * height, LANES), jnp.float32)
    strip = pl.BlockSpec((1, SPAN), lambda i: (0, spans - 1 - i))
    before = pl.BlockSpec(
        (EXTRA, width), lambda i: (jnp.maximum((spans - 1 - i) * (SPAN // EXTRA) - 1, 0), half)
    )
    return pl.pallas_call(
        functools.partial(
            backward_kernel,
            spans=spans,
            first_head=half * heads,
            adds=previous is not None,
            total_width=total_width,
            shared_groups=groups,
        ),
        grid=(spans,),
        in_specs=[
            scalars(),
            scalars(),
            tile(width, half),
            tile(width, half),
            tile(width, half),
            tile(width, half),
            tile(width, half),
            before,
            tile(select_width),
            tile(LANES),
            tile(LANES),
            tile(LANES),
            pl.BlockSpec((1, select_width // 2, width), lambda i: (spans - 1 - i, 0, half)),
            pl.BlockSpec((CONV, width), lambda i: (0, half)),
            pl.BlockSpec((1, width), lambda i: (0, half)),
            pl.BlockSpec((1, width), lambda i: (0, half)),
            strip,
            strip,
            fixed((1, LANES)),
            fixed((1, LANES)),
            fixed((1, LANES)),
            scalars(),
        ]
        + ([] if previous is None else shared),
        out_specs=[
            out_tile(2 * width),
            *shared,
            out_tile(LANES),
            pl.BlockSpec((1, SPAN), lambda i: (0, spans - 1 - i)),
            fixed((8, width)),
            fixed((8, LANES)),
        ],
        out_shape=[
            jax.ShapeDtypeStruct((rows, 2 * width), jnp.bfloat16),
            *[shared_shape] * (2 * groups),
            jax.ShapeDtypeStruct((rows, LANES), jnp.bfloat16),
            jax.ShapeDtypeStruct((1, rows), jnp.float32),
            jax.ShapeDtypeStruct((8, width), jnp.float32),
            jax.ShapeDtypeStruct((8, LANES), jnp.float32),
        ],
        scratch_shapes=[
            pltpu.VMEM((SPAN + EXTRA, width), jnp.float32),
            pltpu.VMEM((SPAN + EXTRA, width), jnp.float32),
            pltpu.VMEM((select_width // 2, width), jnp.float32),
            pltpu.VMEM((8, width), jnp.float32),
        ],
        compiler_params=settings(52),
        cost_estimate=guess(20000 * rows * width, 20 * rows * width, 300 * rows * width),
        name="backward",
    )(
        starts,
        fills,
        gate_pre,
        grad_scaled,
        scan,
        values,
        value_pre,
        value_pre,
        selects,
        delta,
        sums,
        step_pre,
        states,
        conv_value,
        conv_value_bias,
        gain,
        *strips,
        step_bias,
        decay_log,
        skip,
        model_place,
        *([] if previous is None else previous),
    )


def pair_kernel(*refs):
    groups = len(refs) // 3
    for index in range(groups):
        out = refs[2 * groups + index]
        out[...] = (refs[index][...] + refs[groups + index][...]).astype(out.dtype)


def run_pair(ours, came, wire):
    rows, columns = ours[0].shape
    groups = len(ours)
    tile = pl.BlockSpec((SPAN, columns), lambda i: (i, 0))
    return pl.pallas_call(
        pair_kernel,
        grid=(rows // SPAN,),
        in_specs=[tile] * (2 * groups),
        out_specs=[tile] * groups,
        out_shape=[jax.ShapeDtypeStruct((rows, columns), jnp.float32)]
        + [jax.ShapeDtypeStruct((rows, columns), wire)] * (groups - 1),
        compiler_params=settings(40),
        cost_estimate=guess(0, 0),
        name="pair",
    )(*ours, *came)


def select_kernel(starts, spot, select_pre, kernel, bias, *refs, count):
    grads, steps_in = refs[:count], refs[count:-5]
    low_out, rows_out, stat_out, ahead, unfolded = refs[-5:]
    rows, part = unfolded.shape
    folds = LANES // part
    height = SPAN // folds
    folded = grads[0][...]
    for grad in grads[1:]:
        folded = folded + grad[...]
    for span in range(rows // SPAN):
        for fold in range(folds):
            start = span * SPAN + fold * height
            unfolded[start : start + height, :] = folded[
                span * height : (span + 1) * height, fold * part : (fold + 1) * part
            ]
    upstream = unfolded[...]
    pre = select_pre[:, :part]
    taps = kernel[:, :part]
    own_bias = bias[:, :part]
    for index in range(1, select_pre.shape[1] // part):
        lanes = slice(index * part, (index + 1) * part)
        here = spot[0] == index
        pre = jnp.where(here, select_pre[:, lanes], pre)
        taps = jnp.where(here, kernel[:, lanes], taps)
        own_bias = jnp.where(here, bias[:, lanes], own_bias)
    place = iota((rows, part), 0)
    joined = jnp.zeros((rows, part), jnp.int32)
    for span in range(rows // SPAN):
        joined = jnp.where(place // SPAN == span, 1 - starts[span], joined)
    inside = place % SPAN
    stat_out[...] = jnp.zeros(stat_out.shape, jnp.float32)
    ahead[...] = jnp.zeros(ahead.shape, jnp.float32)
    ahead[EXTRA : EXTRA + rows, :] = pre
    shifted = []
    mixed = own_bias
    for back in range(CONV):
        moved = ahead[EXTRA - back : EXTRA - back + rows, :]
        moved = jnp.where(jnp.logical_or(inside >= back, joined == 1), moved, 0.0)
        shifted.append(moved)
        mixed = mixed + taps[CONV - 1 - back : CONV - back, :] * moved
    sig = sigmoid(mixed)
    inner = upstream * sig * (1.0 + mixed * (1.0 - sig))
    total = jnp.zeros((rows, part), jnp.float32)
    tap_sums = []
    for back in range(CONV):
        tap = taps[CONV - 1 - back : CONV - back, :]
        tap_sums.append(jnp.sum(inner * shifted[back], axis=0, keepdims=True))
        ahead[EXTRA : EXTRA + rows, :] = jnp.where(
            jnp.logical_or(inside >= back, joined == 1), inner, 0.0
        )
        ahead[EXTRA + rows :, :] = jnp.zeros((EXTRA, part), jnp.float32)
        total = total + tap * ahead[EXTRA + back : EXTRA + back + rows, :]
    rows_here = tap_sums[::-1] + [jnp.sum(inner, axis=0, keepdims=True)]
    for index in range(select_pre.shape[1] // part):
        lanes = slice(index * part, (index + 1) * part)
        for at, row in enumerate(rows_here):
            stat_out[at : at + 1, lanes] = jnp.where(spot[0] == index, row, 0.0)
    low = total.astype(jnp.bfloat16)
    dots = jnp.sum(low.astype(jnp.float32) * pre, axis=1, keepdims=True)
    rows_out[...] = jnp.transpose(jnp.broadcast_to(dots, (rows, LANES)))[:1, :]
    steps = steps_in[0][...].astype(jnp.float32)
    for piece in steps_in[1:]:
        steps = steps + piece[...].astype(jnp.float32)
    pieces = [steps[:, : LANES // 2], low.astype(jnp.float32)]
    if part < LANES // 2:
        pieces.append(jnp.zeros((rows, LANES // 2 - part), jnp.float32))
    low_out[...] = jnp.concatenate(pieces, axis=1).astype(jnp.bfloat16)


def run_select(starts, spot, grads, select_pre, kernel, bias, steps):
    rows = select_pre.shape[0]
    part = grads[0].shape[0] * LANES // rows
    inputs = (select_pre, kernel, bias, *grads, *steps)
    return pl.pallas_call(
        functools.partial(select_kernel, count=len(grads)),
        in_specs=[scalars(), scalars()] + [pl.BlockSpec(memory_space=pltpu.VMEM)] * len(inputs),
        out_shape=[
            jax.ShapeDtypeStruct((rows, LANES), jnp.bfloat16),
            jax.ShapeDtypeStruct((1, rows), jnp.float32),
            jax.ShapeDtypeStruct((8, select_pre.shape[1]), jnp.float32),
        ],
        scratch_shapes=[
            pltpu.VMEM((rows + 2 * EXTRA, part), jnp.float32),
            pltpu.VMEM((rows, part), jnp.float32),
        ],
        compiler_params=pltpu.CompilerParams(vmem_limit_bytes=40 << 20),
        cost_estimate=guess(0, 0),
        name="select",
    )(starts, spot, *inputs)


def spread_kernel(place, own_left, other_left, *refs):
    rights, (sends_out, own_out) = refs[:-2], refs[-2:]
    start = 0
    for own_right, other_right in zip(rights[::2], rights[1::2]):
        lanes = slice(start, start + own_right.shape[1])
        start += own_right.shape[1]
        product = dot_rows(own_left[0], own_right[...]) + dot_rows(other_left[0], other_right[...])
        sends_out[0, :, lanes] = product.astype(jnp.bfloat16)

        @pl.when(pl.program_id(0) == place[0])
        def _():
            own_out[:, lanes] = product


def run_spread(place, own_left, other_left, *rights):
    groups, rows, piece = own_left.shape
    columns = sum(right.shape[1] for right in rights[::2])
    left = pl.BlockSpec((1, rows, piece), lambda g: (g, 0, 0))
    return pl.pallas_call(
        spread_kernel,
        grid=(groups,),
        in_specs=[scalars(), left, left] + [fixed(right.shape) for right in rights],
        out_specs=[
            pl.BlockSpec((1, piece, columns), lambda g: (g, 0, 0)),
            fixed((piece, columns)),
        ],
        out_shape=[
            jax.ShapeDtypeStruct((groups, piece, columns), jnp.bfloat16),
            jax.ShapeDtypeStruct((piece, columns), jnp.float32),
        ],
        compiler_params=settings(44),
        cost_estimate=guess(0, 0),
        name="spread",
    )(place, own_left, other_left, *rights)


def pair_of(size):
    return [(spot, spot ^ 1) for spot in range(size)]


def shift_of(size, hops):
    groups = size // 2
    return [(spot, ((spot // 2 + hops) % groups) * 2 + spot % 2) for spot in range(size)]


def swap_pair(array, axis):
    return lax.ppermute(array, axis, pair_of(lax.axis_size(axis)))


def exchange_groups(sends):
    size = lax.axis_size("dp")
    groups = [[2 * group + side for group in range(size // 2)] for side in range(2)]
    return lax.all_to_all(sends, "dp", 0, 0, axis_index_groups=groups)


def send_groups(sends):
    size = lax.axis_size("dp")
    mine = lax.axis_index("dp") // 2
    arrived = []
    for hops in range(1, size // 2):
        place = (mine + hops) % (size // 2)
        piece = lax.dynamic_index_in_dim(sends, place, 0, keepdims=False)
        arrived.append(lax.ppermute(piece, "dp", shift_of(size, hops)))
    return arrived


def finish(total, arrived):
    mine = lax.axis_index("dp") // 2
    for index in range(arrived.shape[0]):
        total = total + jnp.where(index == mine, 0.0, arrived[index].astype(jnp.float32))
    return total


def send_far(pieces):
    size = lax.axis_size("mp")
    return [
        lax.ppermute(piece, "mp", shift_of(size, hops + 1)) for hops, piece in enumerate(pieces)
    ]


def features_kernel(place, *refs, groups):
    hiddens, outs, gain_out = refs[:groups], refs[-1 - groups : -1], refs[-1]
    scale, small, w_gate, w_value, w_small = refs[-6 - groups : -1 - groups]
    parts = refs[groups : -6 - groups]
    width = parts[0].shape[1] // 2
    total = dot_lanes(small[...], w_small[...])
    for index, part in enumerate(parts):
        lanes = slice(index * width, (index + 1) * width)
        total = total + dot_lanes(part[:, :width], w_gate[:, lanes])
        total = total + dot_lanes(part[:, width:], w_value[:, lanes])
    gain_out[...] = jnp.zeros(gain_out.shape, jnp.float32)
    for index, hidden in enumerate(hiddens):

        @pl.when(pl.program_id(0) == index)
        def _():
            out = outs[index]
            out[...] = total
            for start in range(0, total.shape[1], LANES):
                lanes = slice(start, start + LANES)
                pulled = out[:, lanes] * hidden[:, lanes].astype(jnp.float32) * scale[...]
                gain_out[0, 0:1, lanes] = jnp.sum(pulled, axis=0, keepdims=True)


def back_features(place, hiddens, scale, parts, small, weights, groups):
    rows = small.shape[0]
    features = weights[0].shape[0]
    piece = features // (2 * groups)
    return pl.pallas_call(
        functools.partial(features_kernel, groups=groups),
        grid_spec=pltpu.PrefetchScalarGridSpec(
            num_scalar_prefetch=1,
            grid=(groups,),
            in_specs=[resident(array.shape) for array in (*hiddens, *parts, scale, small)]
            + [
                pl.BlockSpec(
                    (piece, array.shape[1]), lambda g, at: (2 * ((at[0] + g) % groups) + at[1], 0)
                )
                for array in weights
            ],
            out_specs=[resident((rows, piece))] * groups
            + [pl.BlockSpec((1, 8, piece), lambda g, at: (g, 0, 0))],
        ),
        out_shape=[jax.ShapeDtypeStruct((rows, piece), jnp.float32)] * groups
        + [jax.ShapeDtypeStruct((groups, 8, piece), jnp.float32)],
        compiler_params=settings(52),
        cost_estimate=guess(0, 0),
        name="features",
    )(place, *hiddens, *parts, scale, small, *weights)


def sum_all(values, axis):
    size = lax.axis_size(axis)
    step = 1
    while step < size:
        values = values + lax.ppermute(values, axis, [(spot, spot ^ step) for spot in range(size)])
        step *= 2
    return values


def pack_kernel(*refs, head_dim):
    stats, smalls, gains = refs[:PARTS], refs[PARTS : 2 * PARTS], refs[2 * PARTS + 1 : -1]
    select, out, count = refs[2 * PARTS], refs[-1], PARTS
    gain = gains[0][0:1, :]
    for piece in gains[1:]:
        gain = gain + piece[0:1, :]
    width = stats[0].shape[1]
    whole = width * count
    out[...] = jnp.zeros(out.shape, jnp.float32)
    small = smalls[0][...]
    for piece in smalls[1:]:
        small = small + piece[...]
    for index, piece in enumerate(stats):
        out[:8, index * width : (index + 1) * width] = piece[...]
    heads = jnp.zeros((8, LANES), jnp.float32)
    for start in range(0, whole, LANES):
        owner = (
            iota((LANES, LANES), 1) == (start + iota((LANES, LANES), 0)) // head_dim
        ).astype(jnp.float32)
        heads = heads + exact(out[:8, start : start + LANES], owner)
    out[8:16, : select.shape[1]] = select[...]
    out[16:18, :LANES] = small[:2, :]
    out[18:19, :LANES] = heads[CONV + 1 : CONV + 2, :]
    for start in range(0, gain.shape[1], LANES):
        out[19 + start // LANES : 20 + start // LANES, :LANES] = gain[:, start : start + LANES]


def run_pack(stats, smalls, select, gains, head_dim):
    whole = stats[0].shape[1] * len(stats)
    rows = -(-(19 + gains[0].shape[1] // LANES) // 8) * 8
    return pl.pallas_call(
        functools.partial(pack_kernel, head_dim=head_dim),
        out_shape=jax.ShapeDtypeStruct((rows, whole), jnp.float32),
        cost_estimate=guess(0, 0),
        name="pack",
    )(*stats, *smalls, select, *gains)


def unpack_kernel(*refs):
    arrived, outs = refs[:-9], refs[-9:]
    total = arrived[0][...]
    for piece in arrived[1:]:
        total = total + piece[...]
    taps, bias, select, select_bias, step, decay, skip, gate_gain, gain = outs
    taps[...] = total[:CONV, :]
    bias[...] = total[CONV : CONV + 1, :]
    gate_gain[...] = total[CONV + 2 : CONV + 3, :]
    select[...] = total[8 : 8 + CONV, : select.shape[1]]
    select_bias[...] = total[8 + CONV : 9 + CONV, : select.shape[1]]
    heads = step.shape[1]
    step[...] = total[16:17, :heads]
    decay[...] = total[17:18, :heads]
    skip[...] = total[18:19, :heads]
    for start in range(0, gain.shape[1], LANES):
        gain[:, start : start + LANES] = total[19 + start // LANES : 20 + start // LANES, :LANES]


def run_unpack(arrived, select_width, heads, gain_width):
    whole = arrived[0].shape[1]
    shapes = [(CONV, whole), (1, whole), (CONV, select_width), (1, select_width)]
    shapes += [(1, heads)] * 3 + [(1, whole), (1, gain_width)]
    return pl.pallas_call(
        unpack_kernel,
        out_shape=[jax.ShapeDtypeStruct(shape, jnp.float32) for shape in shapes],
        cost_estimate=guess(0, 0),
        name="unpack",
    )(*arrived)


def sum_tokens(values):
    size = lax.axis_size("dp")
    both = values + swap_pair(values, "dp")
    return [both] + [
        lax.ppermute(both, "dp", shift_of(size, hops)) for hops in range(1, size // 2)
    ]


def widen_lanes(vector):
    return jnp.pad(vector, (0, LANES - vector.shape[0]))[None, :]


def on_device(
    hidden_in,
    cotangent,
    span_starts,
    span_fill,
    norm_gain,
    w_gate,
    w_value,
    w_select,
    w_step,
    conv_value,
    conv_value_bias,
    conv_select,
    conv_select_bias,
    step_bias,
    decay_log,
    skip_gain,
    gate_gain,
    w_out,
):
    token_rows = hidden_in.shape[0]
    model_width = norm_gain.shape[0]
    inner_cols = w_gate.shape[1]
    local_heads = w_step.shape[1]
    head_dim = inner_cols // local_heads
    select_width = w_select.shape[1]
    model_parts = lax.axis_size("mp")
    model_groups = model_parts // 2
    data_parts = lax.axis_size("dp")
    inner_total = inner_cols * model_parts
    feature_piece = model_width // model_parts
    data_piece = model_width // data_parts
    part = select_width // model_parts
    model_spot = lax.axis_index("mp")
    model_side = model_spot % 2
    data_side = (lax.axis_index("dp") % 2).reshape(1)
    offset = model_spot * feature_piece
    select_start = model_spot * part

    def after(array, *others):
        return lax.optimization_barrier((array, *others))[0]

    def gather_far(block):
        return [
            lax.ppermute(block, "mp", shift_of(model_parts, hops)) for hops in range(1, model_groups)
        ]

    def gather_near(block, far, *others):
        blocks = [block, swap_pair(block, "mp")]
        for same in far:
            same = after(same, *others) if others else same
            blocks += [same, swap_pair(same, "mp")]
        return blocks

    def theirs(block):
        pieces = []
        for index in range(0, block.shape[1] // data_piece, 2):
            first = block[:, index * data_piece : (index + 1) * data_piece]
            second = block[:, (index + 1) * data_piece : (index + 2) * data_piece]
            pieces.append(jnp.where(data_side[0] == 0, second, first))
        return pieces

    gain_row = gate_gain[None, :]
    skip_row = widen_lanes(skip_gain)
    bias_step = widen_lanes(step_bias)
    decay_row = widen_lanes(decay_log)
    half_lanes = LANES // 2
    wide_step = jnp.pad(w_step, ((0, 0), (0, LANES - local_heads)))
    spots = []
    for hops in range(model_groups):
        group = (model_spot // 2 - hops) % model_groups
        spots += [2 * group + model_side, 2 * group + 1 - model_side]
    spots = jnp.stack(spots)

    place = (lax.axis_index("dp") // 2).reshape(1)
    model_place = jnp.stack([model_spot // 2, model_side])
    other_place = jnp.stack([model_spot // 2, 1 - model_side])
    vectors = (conv_value, conv_value_bias[None, :])
    head_vectors = (bias_step, decay_row, skip_row)

    far_in = gather_far(hidden_in)
    cross = swap_pair(jnp.concatenate(theirs(hidden_in) + theirs(cotangent), axis=1), "dp")
    blocks_in = gather_near(hidden_in, far_in)
    combined = after(jnp.concatenate([cotangent, cross], axis=1), *far_in)
    far_up = gather_far(combined)

    (
        normed_own,
        scale_rows,
        scale_columns,
        value_pre,
        gate_pre,
        select_pre,
        step_pre,
        values,
        selects,
        scan,
        gated,
        delta,
        sums,
        states,
        square_part,
    ) = run_forward(
        data_side,
        spots,
        span_starts,
        span_fill,
        [after(blocks_in[0], cross)] + blocks_in[1:],
        norm_gain[None, :],
        (w_value, w_gate, w_select, wide_step),
        vectors + (conv_select, conv_select_bias[None, :]) + head_vectors,
        data_piece,
    )
    other_rows = swap_pair(scale_rows, "dp")
    blocks_up = gather_near(combined, far_up, square_part)
    squares = after(sum_all(square_part, "mp"), other_rows)
    scaled = run_scale(gated, squares, gain_row, inner_total)
    late_select, late_step = lax.optimization_barrier((w_select, w_step, square_part))[:2]
    own_select = lax.dynamic_slice_in_dim(late_select, select_start, part, 1)
    w_small = jnp.concatenate(
        [
            jnp.pad(late_step, ((0, 0), (0, half_lanes - local_heads))),
            jnp.pad(own_select, ((0, 0), (0, half_lanes - part))),
        ],
        axis=1,
    )
    scaled_other = swap_pair(scaled, "dp")
    grad_scaled, product_part, up_own, normed_other, up_other = run_cotangent(
        data_side,
        spots,
        other_rows,
        norm_gain,
        gain_row,
        w_out,
        gated,
        blocks_up,
        data_piece,
    )
    products = sum_all(product_part, "mp")

    def backward(index, products, previous):
        return run_backward(
            span_starts,
            span_fill,
            (gate_pre, grad_scaled, scan, values, value_pre, selects, delta, sums, step_pre),
            (squares, products),
            states,
            vectors + (gain_row,) + head_vectors,
            model_parts,
            index,
            model_place,
            previous,
            inner_total,
        )

    parts, others, stats, smalls, steps, row_dots = [], [], [], [], [], []
    own_parts, out_parts = [], []
    previous = None
    gate = products
    last_other, last_out = scaled_other, None
    for index in range(PARTS):
        part_grads, *previous, step, rows, stat, small = backward(index, gate, previous)
        if index == 0:
            lefts, right = (up_own, up_other), scaled
        else:
            lefts, right = (normed_own, normed_other), parts[index - 1]
        if index == 1:
            mixed = run_mixed(model_place, after(scaled, sends), w_out, model_groups)
            mixed_came = [swap_pair(piece, "mp") for piece in mixed[:model_groups]]
            arrived = after(last_other, part_grads, mixed[0])
        else:
            arrived = after(last_other, part_grads)
        last_other = swap_pair(after(part_grads, arrived), "dp")
        sends, own = run_spread(place, *lefts, right, arrived)
        if index == 0:
            last_out = send_groups(sends)
        else:
            waited = last_out if index == 1 else [last_out]
            last_out = exchange_groups(after(sends, *waited))
        own_parts.append(own)
        out_parts.append(last_out)
        gate = after(products, sends)
        parts.append(part_grads)
        others.append(last_other)
        steps.append(step)
        row_dots.append(rows)
        stats.append(stat)
        smalls.append(small)
    own_out, out_out = own_parts.pop(0), out_parts.pop(0)

    mixed_total, *mixed_pieces = run_pair(
        mixed[model_groups:], [after(mixed_came[0], sends)] + mixed_came[1:], jnp.float32
    )
    came = [swap_pair(after(piece, others[-2]), "mp") for piece in previous[:model_groups]]
    select_total, *select_pieces = run_pair(
        previous[model_groups:], [after(came[0], mixed_total)] + came[1:], jnp.float32
    )
    select_arrived = send_far(select_pieces)
    mixed_arrived = send_far([after(piece, *select_arrived) for piece in mixed_pieces])
    small_low, select_rows, select_stats = run_select(
        span_starts,
        model_spot.reshape(1),
        [select_total] + select_arrived,
        select_pre,
        conv_select,
        conv_select_bias[None, :],
        steps,
    )
    select_sums = sum_all(select_stats, "mp")
    row_total = select_rows
    for rows in row_dots:
        row_total = row_total + rows
    norm_rows = sum_all(row_total, "mp")
    weights = (w_gate, w_value, w_small)
    hiddens = [
        [blocks_in[2 * ((model_groups - group) % model_groups) + side] for group in range(model_groups)]
        for side in range(2)
    ]
    *back_theirs, gain_theirs = back_features(
        other_place,
        hiddens[1],
        scale_columns,
        parts,
        small_low,
        weights,
        model_groups,
    )
    last_arrived = after(others[-1], back_theirs[0])
    small_other = swap_pair(after(small_low, last_arrived), "dp")
    back_came = [swap_pair(after(piece, last_arrived), "mp") for piece in back_theirs]
    sends_last, own_last = run_spread(
        place, normed_own, normed_other, parts[-1], last_arrived, small_low, small_other
    )
    out_last = exchange_groups(after(sends_last, last_out))
    *back_ours, gain_ours = back_features(
        model_place,
        hiddens[0],
        scale_columns,
        parts,
        after(small_low, sends_last, *mixed_arrived),
        weights,
        model_groups,
    )
    back_total, *back_pieces = run_pair(
        back_ours, [after(back_came[0], *mixed_arrived)] + back_came[1:], jnp.bfloat16
    )
    gain_both = gain_ours + swap_pair(gain_theirs, "mp")
    gain_sums = [gain_both[0]] + send_far([gain_both[hops] for hops in range(1, model_groups)])
    back_pieces = [after(piece, *gain_sums, select_sums, norm_rows) for piece in back_pieces]
    back_arrived = send_far(back_pieces)
    own_parts.append(own_last)
    out_parts.append(out_last)
    for index in range(PARTS):
        out_parts[index] = after(out_parts[index], *back_pieces)
    out_out = [after(piece, *back_pieces) for piece in out_out]

    grad_normed = back_total
    for piece in back_arrived:
        grad_normed = grad_normed + piece.astype(jnp.float32)
    own_in = hidden_in.astype(jnp.float32)
    mixed_share = mixed_total
    for piece in mixed_arrived:
        mixed_share = mixed_share + piece
    output = (own_in + mixed_share).astype(jnp.bfloat16)
    own_gain = lax.dynamic_slice_in_dim(norm_gain, offset, feature_piece, 0)
    own_scale = scale_columns[:, :1]
    weighted_in = grad_normed * own_gain[None, :]
    grad_hidden_in = (
        cotangent.astype(jnp.float32)
        + weighted_in * own_scale
        - own_in * own_scale**2 * norm_rows[0][:, None] / model_width
    )
    packed = run_pack(stats, smalls, select_sums, gain_sums, head_dim)
    small_sums = sum_tokens(after(packed, *back_pieces))
    grad_w_out = own_out
    for piece in out_out:
        grad_w_out = grad_w_out + piece.astype(jnp.float32)
    grad_w_out = grad_w_out.T
    done = [finish(own, out) for own, out in zip(own_parts, out_parts)]
    width = inner_cols // PARTS
    grad_w_gate = jnp.concatenate([piece[:, :width] for piece in done], axis=1)
    grad_w_value = jnp.concatenate([piece[:, width : 2 * width] for piece in done], axis=1)
    grad_w_small = done[-1][:, 2 * width :]
    grad_w_step = grad_w_small[:, :local_heads]
    grad_w_select = lax.all_gather(
        grad_w_small[:, half_lanes : half_lanes + part], "mp", axis=1, tiled=True
    )
    (
        grad_taps,
        grad_bias,
        grad_select_taps,
        grad_select_bias,
        grad_step_bias,
        grad_decay_log,
        grad_skip_gain,
        grad_gate_gain,
        gain_sum,
    ) = run_unpack(
        [after(small_sums[0], grad_w_select)] + small_sums[1:], select_width, local_heads, feature_piece
    )
    return (
        output,
        grad_hidden_in,
        gain_sum[0],
        grad_w_gate,
        grad_w_value,
        grad_w_select,
        grad_w_step,
        grad_taps,
        grad_bias[0],
        grad_select_taps,
        grad_select_bias[0],
        grad_step_bias[0],
        grad_decay_log[0],
        grad_skip_gain[0],
        grad_gate_gain[0],
        grad_w_out,
    )


def solution(mesh):
    in_specs = (
        P("dp", "mp"),
        P("dp", "mp"),
        P("dp"),
        P("dp"),
        P(),
        P(None, "mp"),
        P(None, "mp"),
        P(),
        P(None, "mp"),
        P(None, "mp"),
        P("mp"),
        P(),
        P(),
        P("mp"),
        P("mp"),
        P("mp"),
        P("mp"),
        P("mp", None),
    )
    out_specs = (
        P("dp", "mp"),
        P("dp", "mp"),
        P("mp"),
        P("dp", "mp"),
        P("dp", "mp"),
        P("dp", None),
        P("dp", "mp"),
        P(None, "mp"),
        P("mp"),
        P(),
        P(),
        P("mp"),
        P("mp"),
        P("mp"),
        P("mp"),
        P("mp", "dp"),
    )
    return jax.shard_map(
        on_device, mesh=mesh, in_specs=in_specs, out_specs=out_specs, check_vma=False
    )
```
